32 devices in a mesh: parts: 2 (over y), vocab: 4 (over z), mp: 2 (over x), rep: 2 (over core).
Axes of the slice: x: 2, y: 2, z: 4, core: 2. Of those that a mesh axis runs over, the one named last changes fastest.
Arguments:
- resid_base: bfloat16 [128, 4608], P(('parts', 'vocab', 'rep'), 'mp'), parts along dimension 0, may hold values from -60 to 60
- mlp_hidden: bfloat16 [128, 36864], P(('parts', 'vocab', 'rep'), 'mp'), parts along dimension 0, may hold values from -6 to 6
- edit_in: float32 [73728], P(('parts', 'mp')), parts along dimension 0, may hold values from -0.03125 to 0.03125
- edit_out: float32 [9216], P(('parts', 'mp')), parts along dimension 0, may hold values from -6 to 6
- norm_gain: float32 [4608], P('mp'), may hold values from 0.5 to 1.5
- head: bfloat16 [4608, 8192], P(None, ('vocab', 'mp', 'rep')), may hold values from -0.25 to 0.25
- token_ids: int32 [128], P('parts'), parts along dimension 0, may hold values from 0 to 8191
Outputs:
- penalty: float32 [128], P(('parts', 'vocab', 'rep')), parts along dimension 0
- grad_in: float32 [73728], P(('parts', 'mp')), parts along dimension 0
- grad_out: float32 [9216], P(('parts', 'mp')), parts along dimension 0
The draws below stay inside these ranges and needn't reach their ends.
There are 2 independent parts, one for each index of `parts`. The reference program is written for one: setup_inputs(seed, part) draws one part's arguments, and reference() takes and returns one part's arrays. A program takes and returns all parts, laid end to end along the dimension named above; an argument that names none is the same for every part. Nothing has to cross between parts.
All inputs are finite; a program needn't handle non-finite values.
Results may differ from the reference program's by a relative error of at most 0.011.
Values may be sent and summed in bfloat16 or wider, within the bound.
No kernel may reach another device: no remote copies, remote signals or barrier semaphores. Data moves between devices by JAX's collectives and lax.ppermute only.
A program may use at most 64 MiB of HBM per device.

```python
import math
import jax
import jax.numpy as jnp
import numpy as np
from jax import lax

D = 4608
FF = 36864
TOKENS = 64
VOCAB = 8192


def draw_resid_base(key, part):
    first, second = jax.random.split(key, 2)
    noise = jax.random.normal(first, (TOKENS, D), jnp.float32)
    scales = jnp.exp(jax.random.uniform(second, (TOKENS, 1), jnp.float32, 0.0, 2.3))
    noise = jnp.clip(noise, -6.0, 6.0)
    return (noise * scales).astype(jnp.bfloat16)


def plant(values, key, low, top_value):
    index_at = [jax.random.randint(jax.random.fold_in(key, axis), (), 0, length) for axis, length in enumerate(values.shape)]
    main_axis = values.shape.index(max(values.shape))
    neighbour = index_at[:main_axis] + [(index_at[main_axis] + 1) % values.shape[main_axis]] + index_at[main_axis + 1:]
    return values.at[tuple(index_at)].set(low).at[tuple(neighbour)].set(top_value)


def block_levels(own_key, dims, cuts, least, top_value):
    def one(position, shards_of):
        heights = jax.random.uniform(jax.random.fold_in(jax.random.fold_in(own_key, 6), position), (shards_of,), jnp.float32, least / len(cuts), top_value / len(cuts))
        return jnp.repeat(jnp.exp(heights), dims[position] // shards_of).reshape((-1,) + (1,) * (len(dims) - position - 1))

    level = one(*cuts[0])
    for cut in cuts[1:]:
        level = level * one(*cut)
    return level


def cumulative_ranks(number_of, skew):
    loads = [(1 << 20) // math.isqrt(grade ** skew) + 1 for grade in range(1, number_of + 1)]
    deviation = 1 + sum(loads) // (1 << 30)
    return np.cumsum(np.array([max(1, weight // deviation) for weight in loads]))


def ranked_ids(rng, extent, amount, slope):
    table = cumulative_ranks(amount, slope)
    ticket = jax.random.randint(jax.random.fold_in(rng, 1), extent, 0, int(table[amount - 1]))
    grade = jnp.searchsorted(jnp.asarray(table, jnp.int32), ticket, side="right")
    return jax.random.permutation(jax.random.fold_in(rng, 2), amount)[grade].astype(jnp.int32)


def gaussian(stream_key, shape, scale, reach, shards=(), held_as=jnp.bfloat16):
    level = block_levels(stream_key, shape, shards, -0.22, 0.18) if shards else 1.0
    result = jax.random.normal(stream_key, shape, jnp.float32) * scale * level
    return jnp.minimum(jnp.maximum(result, -reach), reach).astype(held_as)


def setup_inputs(seed: int = 0, part: int = 0) -> dict:
    splits = jax.random.split(jax.random.key(seed), 8)
    own_keys = jax.random.split(jax.random.fold_in(splits[7], part), 8)
    return {
        "resid_base": draw_resid_base(jax.random.fold_in(jax.random.fold_in(splits[7], part), 71), part),
        "mlp_hidden": gaussian(own_keys[1], (TOKENS, FF), 1.0, 6.0, ((0, 8), (1, 2))),
        "edit_in": gaussian(own_keys[2], (FF,), FF ** -0.5, 0.03125, ((0, 2),), jnp.float32),
        "edit_out": gaussian(own_keys[3], (D,), 1.0, 6.0, ((0, 2),), jnp.float32),
        "norm_gain": jnp.clip(1.0 + 0.1 * jax.random.normal(splits[4], (D,), jnp.float32), 0.5, 1.5),
        "head": gaussian(splits[5], (D, VOCAB), (D // 9) ** -0.5, 0.25, ((1, 16),)),
        "token_ids": plant(ranked_ids(own_keys[6], (TOKENS,), VOCAB, 2), jax.random.fold_in(own_keys[6], 3), 0, VOCAB - 1).astype(jnp.int32),
    }


softcap = 30.0
epsilon = 1e-06

def reference(resid_base, mlp_hidden, edit_in, edit_out, norm_gain, head, token_ids):
    hidden_f = mlp_hidden.astype(jnp.float32)
    base_f = resid_base.astype(jnp.float32)
    mix_scale = lax.optimization_barrier(jnp.sum(hidden_f * edit_in[None, :], axis=1))
    resid = base_f + mix_scale[:, None] * edit_out[None, :]
    edit_scale = lax.rsqrt(lax.optimization_barrier(jnp.mean(resid * resid, axis=1)) + epsilon)
    base_scale = lax.rsqrt(lax.optimization_barrier(jnp.mean(base_f * base_f, axis=1)) + epsilon)
    x_edit = (resid * edit_scale[:, None] * norm_gain[None, :]).astype(jnp.bfloat16)
    x_base = (base_f * base_scale[:, None] * norm_gain[None, :]).astype(jnp.bfloat16)
    pre_edit = jnp.dot(x_edit, head, preferred_element_type=jnp.float32)
    pre_base = jnp.dot(x_base, head, preferred_element_type=jnp.float32)
    z_edit = softcap * jnp.tanh(pre_edit / softcap)
    z_base = softcap * jnp.tanh(pre_base / softcap)
    lse_edit = jnp.log(lax.optimization_barrier(jnp.sum(jnp.exp(z_edit), axis=1)))
    lse_base = jnp.log(lax.optimization_barrier(jnp.sum(jnp.exp(z_base), axis=1)))
    p_edit = jnp.exp(z_edit - lse_edit[:, None])
    p_base = jnp.exp(z_base - lse_base[:, None])
    onehot = (token_ids[:, None] == jnp.arange(VOCAB, dtype=jnp.int32)[None, :]).astype(jnp.float32)
    diff = z_base - z_edit
    penalty = lax.optimization_barrier(jnp.sum(p_base * diff, axis=1)) + lax.optimization_barrier(jnp.sum(onehot * diff, axis=1)) + 2.0 * (lse_edit - lse_base)
    dy = ((2.0 * p_edit - p_base - onehot) * (1.0 - (z_edit / softcap) ** 2)).astype(jnp.bfloat16)
    dx = lax.dot_general(dy, head, (((1,), (1,)), ((), ())), preferred_element_type=jnp.float32)
    align = lax.optimization_barrier(jnp.sum(x_edit.astype(jnp.float32) * dx, axis=1))
    normed = resid * edit_scale[:, None]
    grad_res = edit_scale[:, None] * (norm_gain[None, :] * dx) - (edit_scale * align / D)[:, None] * normed
    grad_out = lax.optimization_barrier(jnp.sum(mix_scale[:, None] * grad_res, axis=0))
    coeff = lax.optimization_barrier(jnp.sum(grad_res * edit_out[None, :], axis=1))
    grad_in = lax.optimization_barrier(jnp.sum(coeff[:, None] * hidden_f, axis=0))
    return (penalty, grad_in, grad_out)
```

```python
import functools

import jax
import jax.numpy as jnp
from jax import lax
from jax.sharding import PartitionSpec as P

softcap = 30.0
epsilon = 1e-06
bf16 = jnp.bfloat16
f32 = jnp.float32


def split_bf16(value, pieces):
    out = []
    for _ in range(pieces):
        part = lax.reduce_precision(value, 8, 7)
        out.append(part.astype(bf16))
        value = value - part
    return out


def local(nv, nm, nr, resid_base, mlp_hidden, edit_in, edit_out, norm_gain, head, token_ids):
    rows, feat = resid_base.shape
    hidden = mlp_hidden.shape[1]
    model, voc = head.shape
    group = nv * nr * rows
    peers = nv * nm * nr
    quarter = hidden // (nm * nr)
    everyone = ("vocab", "mp", "rep")

    vectors = lax.all_gather(jnp.stack([edit_out, norm_gain]), "mp", axis=1, tiled=True)
    out_all = vectors[0]
    gain_all = vectors[1]

    hidden_f = mlp_hidden.astype(f32)
    mix_part = jnp.sum(hidden_f * edit_in[None, :], axis=1)
    mix_cols = jnp.stack(split_bf16(mix_part, 3), axis=1)
    packed = jnp.concatenate([resid_base, jnp.pad(mix_cols, ((0, 0), (0, 125)))], axis=1)
    packed = jnp.broadcast_to(packed[None], (nv * nm, rows, feat + 128))
    got = lax.all_to_all(packed, ("vocab", "mp"), 0, 0)
    got = lax.all_gather(got, "rep", axis=0).reshape(nr * nv, nm, rows, feat + 128)

    pieces = mlp_hidden.reshape(rows, nm * nr, quarter).transpose(1, 0, 2)
    units = lax.all_to_all(pieces, ("mp", "rep"), 0, 0).reshape(nm, nr, rows, quarter)

    base = jnp.concatenate([got[:, m, :, :feat].reshape(group, feat) for m in range(nm)], axis=1)
    base_f = base.astype(f32)
    mix = jnp.sum(got[:, :, :, feat : feat + 3].astype(f32), axis=(1, 3)).reshape(group)
    resid = base_f + mix[:, None] * out_all[None, :]
    edit_scale = lax.rsqrt(jnp.mean(resid * resid, axis=1) + epsilon)
    base_scale = lax.rsqrt(jnp.mean(base_f * base_f, axis=1) + epsilon)
    along = jnp.sum(resid * out_all[None, :], axis=1)
    x_edit = (resid * edit_scale[:, None] * gain_all[None, :]).astype(bf16)
    x_base = (base_f * base_scale[:, None] * gain_all[None, :]).astype(bf16)
    direction = jnp.stack(split_bf16(out_all * gain_all, 3) + [jnp.zeros((model,), bf16)] * 5)
    pre = jnp.dot(
        jnp.concatenate([x_edit, x_base, direction]), head, preferred_element_type=f32
    )
    pre_edit = pre[:group]
    pre_base = pre[group : 2 * group]
    toward = jnp.sum(pre[2 * group :], axis=0)
    z_edit = softcap * jnp.tanh(pre_edit / softcap)
    z_base = softcap * jnp.tanh(pre_base / softcap)
    slope = 1.0 - (z_edit / softcap) ** 2
    exp_edit = jnp.exp(z_edit)
    exp_base = jnp.exp(z_base)
    ids = token_ids.reshape(nv, nr, rows).transpose(1, 0, 2).reshape(group)
    first_col = lax.axis_index(everyone) * voc
    onehot = (ids[:, None] == (first_col + jnp.arange(voc, dtype=jnp.int32))[None, :]).astype(f32)
    diff = z_base - z_edit
    pe = exp_edit * slope
    pb = exp_base * slope
    po = onehot * slope
    sums = jnp.stack(
        [
            jnp.sum(a, axis=1)
            for a in (
                exp_edit,
                exp_base,
                exp_base * diff,
                onehot * diff,
                pe * pre_edit,
                pb * pre_edit,
                po * pre_edit,
                pe * toward[None, :],
                pb * toward[None, :],
                po * toward[None, :],
            )
        ]
    )
    flat = 10 * group
    padded = -(-flat // 1024) * 1024
    mine = jnp.pad(sums.reshape(flat), (0, padded - flat)).reshape(padded // 128, 128)
    theirs = lax.all_to_all(
        jnp.broadcast_to(mine[None], (peers, padded // 128, 128)), everyone, 0, 0
    )
    sums = jnp.sum(theirs, axis=0).reshape(padded)[:flat].reshape(10, group)
    se, sb, kl, gap, ae, ab, ao, te, tb, to = [sums[i] for i in range(10)]
    inv_e = 2.0 / se
    inv_b = 1.0 / sb
    align = ae * inv_e - ab * inv_b - ao
    proj = te * inv_e - tb * inv_b - to
    penalty = kl * inv_b + gap + 2.0 * (jnp.log(se) - jnp.log(sb))
    shrink = edit_scale * align / model
    coeff = edit_scale * proj - shrink * (edit_scale * along)
    dy = (pe * inv_e[:, None] - pb * inv_b[:, None] - po).astype(bf16).astype(f32)
    dyw = jnp.sum((mix * edit_scale)[:, None] * dy, axis=0)
    dyw_rows = jnp.stack(split_bf16(dyw, 3) + [jnp.zeros((voc,), bf16)] * 5)
    weighted = jnp.sum(
        lax.dot_general(dyw_rows, head, (((1,), (1,)), ((), ())), preferred_element_type=f32), axis=0
    )
    w_hi, w_lo = split_bf16(weighted, 2)
    v_i = lax.axis_index("vocab")
    m_i = lax.axis_index("mp")
    r_i = lax.axis_index("rep")
    own = lax.dynamic_slice_in_dim(coeff.reshape(nr, nv, rows), v_i, 1, 1).reshape(nr, rows)
    part_in = jnp.sum(units.astype(f32) * own[None, :, :, None], axis=(1, 2)).astype(bf16)
    slab = jnp.concatenate([w_hi.reshape(nm, feat), w_lo.reshape(nm, feat), part_in], axis=1)
    width = 2 * feat + quarter
    if width % 128 == 0:
        slab = slab.reshape(nm, width // 128, 128)
    slab = jnp.broadcast_to(slab[None, :, None], (nv, nm, nr) + slab.shape[1:])
    back = lax.all_to_all(slab.reshape((peers,) + slab.shape[3:]), everyone, 0, 0)
    back = back.reshape(nv, nm * nr, width).astype(f32)
    grad_in = jnp.sum(back[:, :, 2 * feat :], axis=0).reshape(hidden)
    weighted_own = jnp.sum(back[:, :, :feat] + back[:, :, feat : 2 * feat], axis=(0, 1))
    pull = mix * shrink * edit_scale
    base_own = lax.dynamic_slice_in_dim(base, m_i * feat, feat, 1).astype(f32)
    second = jnp.sum(pull[:, None] * base_own, axis=0) + jnp.sum(pull * mix) * edit_out
    grad_out = norm_gain * weighted_own - second
    penalty = lax.dynamic_slice(penalty.reshape(nr, nv, rows), (r_i, v_i, 0), (1, 1, rows))
    return (penalty.reshape(rows), grad_in, grad_out)


def solution(mesh):
    in_specs = (
        P(("parts", "vocab", "rep"), "mp"),
        P(("parts", "vocab", "rep"), "mp"),
        P(("parts", "mp")),
        P(("parts", "mp")),
        P("mp"),
        P(None, ("vocab", "mp", "rep")),
        P("parts"),
    )
    out_specs = (P(("parts", "vocab", "rep")), P(("parts", "mp")), P(("parts", "mp")))
    step = functools.partial(local, mesh.shape["vocab"], mesh.shape["mp"], mesh.shape["rep"])
    return jax.shard_map(step, mesh=mesh, in_specs=in_specs, out_specs=out_specs, check_vma=False)
```

```python
import functools

import jax
import jax.numpy as jnp
from jax import lax
from jax.experimental import pallas as pl
from jax.experimental.pallas import tpu as pltpu
from jax.sharding import PartitionSpec as P

softcap = 30.0
epsilon = 1e-06
bf16 = jnp.bfloat16
f32 = jnp.float32


def split_bf16(value, pieces):
    out = []
    for _ in range(pieces):
        part = lax.reduce_precision(value, 8, 7)
        out.append(part.astype(bf16))
        value = value - part
    return out


def from_peers(value, axis, size):
    moves = [[(i, (i + k) % size) for i in range(size)] for k in range(size)]
    return [value] + [lax.ppermute(value, axis, moves[k]) for k in range(1, size)]


def to_peers(pick, axis, size, index):
    moves = [[(i, (i + k) % size) for i in range(size)] for k in range(size)]
    return [pick(index)] + [
        lax.ppermute(pick((index + k) % size), axis, moves[k]) for k in range(1, size)
    ]


def in_order(values, index):
    size = len(values)
    ordered = []
    for j in range(size):
        value = values[0]
        for k in range(1, size):
            value = jnp.where((index - j) % size == k, values[k], value)
        ordered.append(value)
    return ordered


def plain(nv, nm, nr, resid_base, mlp_hidden, edit_in, edit_out, norm_gain, head, token_ids):
    rows, feat = resid_base.shape
    hidden = mlp_hidden.shape[1]
    model, voc = head.shape
    group = nv * nr * rows
    peers = nv * nm * nr
    quarter = hidden // (nm * nr)
    everyone = ("vocab", "mp", "rep")

    v_i = lax.axis_index("vocab")
    m_i = lax.axis_index("mp")
    r_i = lax.axis_index("rep")

    vectors = from_peers(jnp.stack([edit_out, norm_gain]), "mp", nm)
    vectors = jnp.concatenate(in_order(vectors, m_i), axis=1)
    out_all = vectors[0]
    gain_all = vectors[1]

    units = mlp_hidden.reshape(rows, nm, nr, quarter)
    units = jnp.concatenate(
        [
            part
            for part in to_peers(
                lambda r: lax.dynamic_index_in_dim(units, r, 2, keepdims=False), "rep", nr, r_i
            )
        ]
    )
    units = to_peers(
        lambda m: lax.dynamic_index_in_dim(units, m, 1, keepdims=False), "mp", nm, m_i
    )

    hidden_f = mlp_hidden.astype(f32)
    mix_part = jnp.sum(hidden_f * edit_in[None, :], axis=1)
    mix_cols = jnp.stack(split_bf16(mix_part, 3), axis=1)
    packed = jnp.concatenate([resid_base, jnp.pad(mix_cols, ((0, 0), (0, 125)))], axis=1)
    packed = jnp.broadcast_to(packed[None], (nv * nm, rows, feat + 128))
    got = lax.all_to_all(packed, ("vocab", "mp"), 0, 0)
    got = jnp.concatenate(in_order(from_peers(got, "rep", nr), r_i)).reshape(nr * nv, nm, rows, feat + 128)

    base = jnp.concatenate([got[:, m, :, :feat].reshape(group, feat) for m in range(nm)], axis=1)
    base_f = base.astype(f32)
    mix = jnp.sum(got[:, :, :, feat : feat + 3].astype(f32), axis=(1, 3)).reshape(group)
    resid = base_f + mix[:, None] * out_all[None, :]
    edit_scale = lax.rsqrt(jnp.mean(resid * resid, axis=1) + epsilon)
    base_scale = lax.rsqrt(jnp.mean(base_f * base_f, axis=1) + epsilon)
    along = jnp.sum(resid * out_all[None, :], axis=1)
    x_edit = (resid * edit_scale[:, None] * gain_all[None, :]).astype(bf16)
    x_base = (base_f * base_scale[:, None] * gain_all[None, :]).astype(bf16)
    direction = jnp.stack(split_bf16(out_all * gain_all, 3) + [jnp.zeros((model,), bf16)] * 5)
    pre = jnp.dot(
        jnp.concatenate([x_edit, x_base, direction]), head, preferred_element_type=f32
    )
    pre_edit = pre[:group]
    pre_base = pre[group : 2 * group]
    toward = jnp.sum(pre[2 * group :], axis=0)
    z_edit = softcap * jnp.tanh(pre_edit / softcap)
    z_base = softcap * jnp.tanh(pre_base / softcap)
    slope = 1.0 - (z_edit / softcap) ** 2
    exp_edit = jnp.exp(z_edit)
    exp_base = jnp.exp(z_base)
    ids = token_ids.reshape(nv, nr, rows).transpose(1, 0, 2).reshape(group)
    first_col = lax.axis_index(everyone) * voc
    onehot = (ids[:, None] == (first_col + jnp.arange(voc, dtype=jnp.int32))[None, :]).astype(f32)
    diff = z_base - z_edit
    pe = exp_edit * slope
    pb = exp_base * slope
    po = onehot * slope
    sums = jnp.stack(
        [
            jnp.sum(a, axis=1)
            for a in (
                exp_edit,
                exp_base,
                exp_base * diff,
                onehot * diff,
                pe * pre_edit,
                pb * pre_edit,
                po * pre_edit,
                pe * toward[None, :],
                pb * toward[None, :],
                po * toward[None, :],
            )
        ]
    )
    weight = mix * edit_scale
    wo = jnp.sum(weight[:, None] * po, axis=0)
    high_e, low_e = split_bf16(pe, 2)
    high_b, low_b = split_bf16(pb, 2)
    tail = jnp.stack(split_bf16(wo, 3) + [jnp.zeros((voc,), bf16)] * 5)
    outer = lax.dot_general(
        jnp.concatenate([high_e, high_b, low_e, low_b, tail]),
        head,
        (((1,), (1,)), ((), ())),
        preferred_element_type=f32,
    )
    rows_e = outer[:group] + outer[2 * group : 3 * group]
    rows_b = outer[group : 2 * group] + outer[3 * group : 4 * group]
    row_o = jnp.sum(outer[4 * group :], axis=0)
    flat = 10 * group
    padded = -(-flat // 1024) * 1024
    mine = jnp.pad(sums.reshape(flat), (0, padded - flat)).reshape(padded // 128, 128)
    theirs = lax.all_to_all(
        jnp.broadcast_to(mine[None], (peers, padded // 128, 128)), everyone, 0, 0
    )
    sums = jnp.sum(theirs, axis=0).reshape(padded)[:flat].reshape(10, group)
    se, sb, kl, gap, ae, ab, ao, te, tb, to = [sums[i] for i in range(10)]
    inv_e = 2.0 / se
    inv_b = 1.0 / sb
    align = ae * inv_e - ab * inv_b - ao
    proj = te * inv_e - tb * inv_b - to
    penalty = kl * inv_b + gap + 2.0 * (jnp.log(se) - jnp.log(sb))
    shrink = edit_scale * align / model
    coeff = edit_scale * proj - shrink * (edit_scale * along)
    weighted = jnp.sum((weight * inv_e)[:, None] * rows_e, axis=0) - jnp.sum((weight * inv_b)[:, None] * rows_b, axis=0) - row_o
    w_hi, w_lo = split_bf16(weighted, 2)
    mine = lax.dynamic_index_in_dim(coeff.reshape(nr, nv, rows), v_i, 1, keepdims=False)
    own = jnp.concatenate([lax.dynamic_index_in_dim(mine, (r_i - k) % nr, 0, keepdims=False) for k in range(nr)])
    part_in = [jnp.sum(u.astype(f32) * own[:, None], axis=0) for u in units]
    part_in = jnp.stack(in_order(part_in, m_i)).astype(bf16)
    slab = jnp.concatenate([w_hi.reshape(nm, feat), w_lo.reshape(nm, feat), part_in], axis=1)
    width = 2 * feat + quarter
    if width % 128 == 0:
        slab = slab.reshape(nm, width // 128, 128)
    slab = jnp.broadcast_to(slab[None, :, None], (nv, nm, nr) + slab.shape[1:])
    back = lax.all_to_all(slab.reshape((peers,) + slab.shape[3:]), everyone, 0, 0)
    back = back.reshape(nv, nm * nr, width).astype(f32)
    grad_in = jnp.sum(back[:, :, 2 * feat :], axis=0).reshape(hidden)
    weighted_own = jnp.sum(back[:, :, :feat] + back[:, :, feat : 2 * feat], axis=(0, 1))
    pull = mix * shrink * edit_scale
    base_own = lax.dynamic_slice_in_dim(base, m_i * feat, feat, 1).astype(f32)
    second = jnp.sum(pull[:, None] * base_own, axis=0) + jnp.sum(pull * mix) * edit_out
    grad_out = norm_gain * weighted_own - second
    penalty = lax.dynamic_slice(penalty.reshape(nr, nv, rows), (r_i, v_i, 0), (1, 1, rows))
    return (penalty.reshape(rows), grad_in, grad_out)


def send_kernel(copies, base_ref, hidden_ref, in_ref, packed_ref):
    rows, hidden = hidden_ref.shape
    feat = base_ref.shape[1]
    total = jnp.zeros((rows, 128), f32)
    for c in range(0, hidden, 128):
        total += hidden_ref[:, c : c + 128].astype(f32) * in_ref[:, c : c + 128]
    mix = jnp.sum(total, axis=1, keepdims=True)
    lane = lax.broadcasted_iota(jnp.int32, (rows, 128), 1)
    cols = jnp.zeros((rows, 128), f32)
    for i in range(3):
        piece = mix.astype(bf16).astype(f32)
        cols = jnp.where(lane == i, piece, cols)
        mix = mix - piece
    cols = cols.astype(bf16)
    for i in range(copies):
        packed_ref[i, :, :feat] = base_ref[...]
        packed_ref[i, :, feat:] = cols


def score_kernel(nv, nm, own_ref, other_ref, vec_ref, ids_ref, head_ref, slab_ref, cols_ref, ops_ref, x_ref):
    rows = own_ref.shape[1]
    feat = own_ref.shape[2] - 128
    model, voc = head_ref.shape
    pair = 2 * rows
    group = 2 * nv * rows
    half = group // 2

    lane_t = lax.broadcasted_iota(jnp.int32, (pair, 128), 1)
    for k, got_ref in enumerate((own_ref, other_ref)):
        for v in range(0, nv, 2):
            at = (k * nv + v) * rows

            def tile(m, c):
                first = got_ref[v * nm + m, :, c : c + 128].astype(f32)
                second = got_ref[(v + 1) * nm + m, :, c : c + 128].astype(f32)
                return jnp.concatenate([first, second], axis=0)

            mixed = tile(0, feat)
            for m in range(1, nm):
                mixed += tile(m, feat)
            mix = jnp.sum(mixed, axis=1, keepdims=True)
            mix_b = jnp.broadcast_to(mix, (pair, 128))
            sq_b = jnp.zeros((pair, 128), f32)
            sq_e = jnp.zeros((pair, 128), f32)
            dot_o = jnp.zeros((pair, 128), f32)
            for m in range(nm):
                for c in range(0, feat, 128):
                    d = m * feat + c
                    out = vec_ref[0:1, d : d + 128]
                    b = tile(m, c)
                    e = b + mix_b * out
                    sq_b += b * b
                    sq_e += e * e
                    dot_o += e * out
            scale_e = lax.rsqrt(jnp.sum(sq_e, axis=1, keepdims=True) / model + epsilon)
            scale_b = lax.rsqrt(jnp.sum(sq_b, axis=1, keepdims=True) / model + epsilon)
            along = jnp.sum(dot_o, axis=1, keepdims=True)
            cols_ref[at : at + pair, :] = jnp.where(
                lane_t == 0, mix, jnp.where(lane_t == 1, scale_e, jnp.where(lane_t == 2, along, 0.0))
            )
            scale_e = jnp.broadcast_to(scale_e, (pair, 128))
            scale_b = jnp.broadcast_to(scale_b, (pair, 128))
            for m in range(nm):
                for c in range(0, feat, 128):
                    d = m * feat + c
                    out = vec_ref[0:1, d : d + 128]
                    gain = vec_ref[1:2, d : d + 128]
                    b = tile(m, c)
                    e = b + mix_b * out
                    x_ref[at : at + pair, d : d + 128] = (e * scale_e * gain).astype(bf16)
                    x_ref[group + at : group + at + pair, d : d + 128] = (b * scale_b * gain).astype(bf16)
    sub = lax.broadcasted_iota(jnp.int32, (16, 128), 0)
    for d in range(0, model, 128):
        rest = vec_ref[0:1, d : d + 128] * vec_ref[1:2, d : d + 128]
        block = jnp.zeros((16, 128), f32)
        for i in range(3):
            piece = rest.astype(bf16).astype(f32)
            block = jnp.where(sub == i, piece, block)
            rest = rest - piece
        x_ref[2 * group :, d : d + 128] = block.astype(bf16)

    pre = jnp.dot(x_ref[...], head_ref[...], preferred_element_type=f32)
    pre_edit = pre[:group]
    pre_base = pre[group : 2 * group]
    toward = jnp.sum(pre[2 * group :], axis=0, keepdims=True)
    th = jnp.tanh(pre_edit / softcap)
    z_edit = softcap * th
    z_base = softcap * jnp.tanh(pre_base / softcap)
    slope = 1.0 - th * th
    exp_edit = jnp.exp(z_edit)
    exp_base = jnp.exp(z_base)
    first_col = lax.axis_index(("vocab", "mp", "rep")) * voc
    column = lax.broadcasted_iota(jnp.int32, (group, voc), 1) + first_col
    hit = column == ids_ref[...]
    diff = z_base - z_edit
    pe = exp_edit * slope
    pb = exp_base * slope
    po = jnp.where(hit, slope, 0.0)

    def total(a):
        return jnp.sum(a, axis=1, keepdims=True)

    sums = [
        total(exp_edit),
        total(exp_base),
        total(exp_base * diff),
        total(jnp.where(hit, diff, 0.0)),
        total(pe * pre_edit),
        total(pb * pre_edit),
        total(po * pre_edit),
        total(pe * toward),
        total(pb * toward),
        total(po * toward),
    ]
    lane = lax.broadcasted_iota(jnp.int32, (group, 128), 1)
    first = jnp.zeros((group, 128), f32)
    second = jnp.zeros((group, 128), f32)
    for i in range(8):
        first = jnp.where(lane == i, sums[i], first)
    for i in range(8, 10):
        second = jnp.where(lane == i - 8, sums[i], second)
    straight = jnp.concatenate([first, second], axis=0)
    swapped = jnp.concatenate([first[half:], first[:half], second[half:], second[:half]], axis=0)
    table = jnp.where(lax.axis_index("rep") == 0, straight, swapped)
    table = table.T[:8]
    for p in range(slab_ref.shape[0]):
        slab_ref[p] = table

    high_e = pe.astype(bf16)
    high_b = pb.astype(bf16)
    ops_ref[:group] = high_e
    ops_ref[group : 2 * group] = high_b
    ops_ref[2 * group : 3 * group] = (pe - high_e.astype(f32)).astype(bf16)
    ops_ref[3 * group : 4 * group] = (pb - high_b.astype(f32)).astype(bf16)
    weight = cols_ref[:, 0:1] * cols_ref[:, 1:2]
    rest = jnp.sum(weight * po, axis=0, keepdims=True)
    sub = lax.broadcasted_iota(jnp.int32, (16, voc), 0)
    block = jnp.zeros((16, voc), f32)
    for i in range(3):
        piece = rest.astype(bf16).astype(f32)
        block = jnp.where(sub == i, piece, block)
        rest = rest - piece
    ops_ref[4 * group :] = block.astype(bf16)


def close_kernel(nv, nm, theirs_ref, cols_ref, outer_ref, own_ref, other_ref, out_ref, *refs):
    units = refs[:nm]
    slab_ref, second_ref, penalty_ref, coeff_ref, pen_ref, vec_ref = refs[nm:]
    rows = own_ref.shape[1]
    feat = own_ref.shape[2] - 128
    model = outer_ref.shape[1]
    group = 2 * nv * rows
    half = group // 2
    tiles = feat // 128
    v_i = lax.axis_index("vocab")
    m_i = lax.axis_index("mp")
    r_i = lax.axis_index("rep")

    table = theirs_ref[0]
    for p in range(1, theirs_ref.shape[0]):
        table += theirs_ref[p]
    table = jnp.concatenate([table, jnp.zeros((120, 128), f32)], axis=0).T
    first = table[:group]
    second = table[group:]
    swap_first = jnp.concatenate([first[half:], first[:half]], axis=0)
    swap_second = jnp.concatenate([second[half:], second[:half]], axis=0)
    first = jnp.where(r_i == 0, first, swap_first)
    second = jnp.where(r_i == 0, second, swap_second)
    se, sb, kl, gap, ae, ab, ao, te = [first[:, i : i + 1] for i in range(8)]
    tb, to = second[:, 0:1], second[:, 1:2]
    mix = cols_ref[:, 0:1]
    scale = cols_ref[:, 1:2]
    along = cols_ref[:, 2:3]
    inv_e = 2.0 / se
    inv_b = 1.0 / sb
    align = ae * inv_e - ab * inv_b - ao
    proj = te * inv_e - tb * inv_b - to
    penalty = kl * inv_b + gap + 2.0 * (jnp.log(se) - jnp.log(sb))
    shrink = scale * align / model
    coeff = scale * proj - shrink * (scale * along)
    weight = mix * scale
    pull = weight * shrink
    coeff_ref[...] = jnp.broadcast_to(coeff, (group, 128))
    pen_ref[...] = jnp.broadcast_to(penalty, (group, 128))
    penalty_ref[...] = pen_ref[pl.ds(pl.multiple_of(v_i * rows, rows), rows), :]

    by_e = jnp.broadcast_to(weight * inv_e, (group, 128))
    by_b = jnp.broadcast_to(weight * inv_b, (group, 128))
    for m in range(nm):
        for t in range(tiles):
            d = m * feat + t * 128
            plus = (outer_ref[:group, d : d + 128] + outer_ref[2 * group : 3 * group, d : d + 128]) * by_e
            less = (outer_ref[group : 2 * group, d : d + 128] + outer_ref[3 * group : 4 * group, d : d + 128]) * by_b
            row = jnp.sum(plus - less, axis=0, keepdims=True)
            row -= jnp.sum(outer_ref[4 * group :, d : d + 128], axis=0, keepdims=True)
            high = row.astype(bf16).astype(f32)
            vec_ref[m, t : t + 1, :] = high
            vec_ref[m, tiles + t : tiles + t + 1, :] = row - high
    own = jnp.concatenate(
        [
            coeff_ref[pl.ds(pl.multiple_of((k * nv + v_i) * rows, rows), rows), :]
            for k in range(2)
        ],
        axis=0,
    )
    for k in range(nm):
        m = lax.rem(m_i - k + nm, nm)
        for t in range(units[k].shape[1] // 128):
            row = jnp.sum(units[k][:, t * 128 : (t + 1) * 128].astype(f32) * own, axis=0, keepdims=True)
            vec_ref[m, pl.ds(2 * tiles + t, 1), :] = row
    for m in range(nm):
        block = vec_ref[m].astype(bf16)
        for v in range(nv):
            for r in range(2):
                slab_ref[(v * nm + m) * 2 + r] = block

    by_p = jnp.broadcast_to(pull, (group, 128))
    pulled = jnp.sum(pull * mix, axis=0, keepdims=True)
    for t in range(tiles):
        c = t * 128
        part = jnp.zeros((rows, 128), f32)
        for k, got_ref in enumerate((own_ref, other_ref)):
            for v in range(nv):
                at = (k * nv + v) * rows
                part += got_ref[v * nm + m_i, :, c : c + 128].astype(f32) * by_p[at : at + rows]
        second_ref[t : t + 1, :] = (
            jnp.sum(part, axis=0, keepdims=True) + pulled * out_ref[:, c : c + 128]
        )


def sum_kernel(back_ref, gain_ref, second_ref, in_ref, out_ref):
    peers = back_ref.shape[0]
    tiles = gain_ref.shape[0]
    units = back_ref.shape[1] - 2 * tiles
    pieces = in_ref.shape[0] // units
    wide = jnp.zeros((tiles, 128), f32)
    for q in range(pieces):
        total = back_ref[q].astype(f32)
        for p in range(q + pieces, peers, pieces):
            total += back_ref[p].astype(f32)
        wide += total[:tiles] + total[tiles : 2 * tiles]
        in_ref[q * units : (q + 1) * units, :] = total[2 * tiles :]
    out_ref[...] = gain_ref[...] * wide - second_ref[...]


def call(kernel, out_shape, scratch=()):
    return pl.pallas_call(
        kernel,
        out_shape=out_shape,
        scratch_shapes=scratch,
        compiler_params=pltpu.CompilerParams(vmem_limit_bytes=40 << 20),
    )


def fused(nv, nm, nr, resid_base, mlp_hidden, edit_in, edit_out, norm_gain, head, token_ids):
    rows, feat = resid_base.shape
    hidden = mlp_hidden.shape[1]
    model, voc = head.shape
    group = nv * nr * rows
    peers = nv * nm * nr
    quarter = hidden // (nm * nr)
    everyone = ("vocab", "mp", "rep")
    m_i = lax.axis_index("mp")
    r_i = lax.axis_index("rep")
    shape = jax.ShapeDtypeStruct

    packed = call(
        functools.partial(send_kernel, nv * nm), shape((nv * nm, rows, feat + 128), bf16)
    )(resid_base, mlp_hidden, edit_in.reshape(1, hidden))
    got = lax.all_to_all(packed, ("vocab", "mp"), 0, 0)
    other = lax.ppermute(got, "rep", [(0, 1), (1, 0)])

    vectors = from_peers(jnp.stack([edit_out, norm_gain]), "mp", nm)
    vectors = jnp.concatenate(in_order(vectors, m_i), axis=1)
    ids = token_ids.reshape(nv, nr, rows)
    ids = jnp.concatenate(
        [lax.dynamic_index_in_dim(ids, (r_i + k) % nr, 1, keepdims=False) for k in range(nr)]
    ).reshape(group, 1)

    units = mlp_hidden.reshape(rows, nm, nr, quarter)
    units = jnp.concatenate(
        to_peers(lambda r: lax.dynamic_index_in_dim(units, r, 2, keepdims=False), "rep", nr, r_i)
    )
    units = to_peers(
        lambda m: lax.dynamic_index_in_dim(units, m, 1, keepdims=False), "mp", nm, m_i
    )

    slab, cols, ops = call(
        functools.partial(score_kernel, nv, nm),
        (
            shape((peers, 8, 128), f32),
            shape((group, 128), f32),
            shape((4 * group + 16, voc), bf16),
        ),
        [pltpu.VMEM((2 * group + 16, model), bf16)],
    )(got, other, vectors, ids, head)
    theirs = lax.all_to_all(slab, everyone, 0, 0)
    outer = lax.dot_general(ops, head, (((1,), (1,)), ((), ())), preferred_element_type=f32)

    width = (2 * feat + quarter) // 128
    slab, second, penalty = call(
        functools.partial(close_kernel, nv, nm),
        (
            shape((peers, width, 128), bf16),
            shape((feat // 128, 128), f32),
            shape((rows, 128), f32),
        ),
        [
            pltpu.VMEM((group, 128), f32),
            pltpu.VMEM((group, 128), f32),
            pltpu.VMEM((nm, width, 128), f32),
        ],
    )(theirs, cols, outer, got, other, edit_out.reshape(1, feat), *units)
    back = lax.all_to_all(slab, everyone, 0, 0)
    grad_in, grad_out = call(
        sum_kernel, (shape((hidden // 128, 128), f32), shape((feat // 128, 128), f32))
    )(back, norm_gain.reshape(feat // 128, 128), second)
    return (penalty[:, 0], grad_in.reshape(hidden), grad_out.reshape(feat))


def local(nv, nm, nr, resid_base, mlp_hidden, *rest):
    rows, feat = resid_base.shape
    quarter = mlp_hidden.shape[1] // (nm * nr)
    whole_tiles = rows == 8 and feat % 128 == 0 and quarter % 128 == 0
    small = nr == 2 and nv % 2 == 0 and nv * nr * rows == 64
    step = fused if whole_tiles and small else plain
    return step(nv, nm, nr, resid_base, mlp_hidden, *rest)


def solution(mesh):
    in_specs = (
        P(("parts", "vocab", "rep"), "mp"),
        P(("parts", "vocab", "rep"), "mp"),
        P(("parts", "mp")),
        P(("parts", "mp")),
        P("mp"),
        P(None, ("vocab", "mp", "rep")),
        P("parts"),
    )
    out_specs = (P(("parts", "vocab", "rep")), P(("parts", "mp")), P(("parts", "mp")))
    step = functools.partial(local, mesh.shape["vocab"], mesh.shape["mp"], mesh.shape["rep"])
    return jax.shard_map(step, mesh=mesh, in_specs=in_specs, out_specs=out_specs, check_vma=False)
```

```python
import functools

import jax
import jax.numpy as jnp
from jax import lax
from jax.experimental import pallas as pl
from jax.experimental.pallas import tpu as pltpu
from jax.sharding import PartitionSpec as P

softcap = 30.0
epsilon = 1e-06
bf16 = jnp.bfloat16
f32 = jnp.float32


def split_bf16(value, pieces):
    out = []
    for _ in range(pieces):
        part = lax.reduce_precision(value, 8, 7)
        out.append(part.astype(bf16))
        value = value - part
    return out


def from_peers(value, axis, size):
    moves = [[(i, (i + k) % size) for i in range(size)] for k in range(size)]
    return [value] + [lax.ppermute(value, axis, moves[k]) for k in range(1, size)]


def to_peers(pick, axis, size, index):
    moves = [[(i, (i + k) % size) for i in range(size)] for k in range(size)]
    return [pick(index)] + [
        lax.ppermute(pick((index + k) % size), axis, moves[k]) for k in range(1, size)
    ]


def in_order(values, index):
    size = len(values)
    ordered = []
    for j in range(size):
        value = values[0]
        for k in range(1, size):
            value = jnp.where((index - j) % size == k, values[k], value)
        ordered.append(value)
    return ordered


def plain(nv, nm, nr, resid_base, mlp_hidden, edit_in, edit_out, norm_gain, head, token_ids):
    rows, feat = resid_base.shape
    hidden = mlp_hidden.shape[1]
    model, voc = head.shape
    group = nv * nr * rows
    peers = nv * nm * nr
    quarter = hidden // (nm * nr)
    everyone = ("vocab", "mp", "rep")

    v_i = lax.axis_index("vocab")
    m_i = lax.axis_index("mp")
    r_i = lax.axis_index("rep")

    vectors = from_peers(jnp.stack([edit_out, norm_gain]), "mp", nm)
    vectors = jnp.concatenate(in_order(vectors, m_i), axis=1)
    out_all = vectors[0]
    gain_all = vectors[1]

    units = mlp_hidden.reshape(rows, nm, nr, quarter)
    units = jnp.concatenate(
        [
            part
            for part in to_peers(
                lambda r: lax.dynamic_index_in_dim(units, r, 2, keepdims=False), "rep", nr, r_i
            )
        ]
    )
    units = to_peers(
        lambda m: lax.dynamic_index_in_dim(units, m, 1, keepdims=False), "mp", nm, m_i
    )

    hidden_f = mlp_hidden.astype(f32)
    mix_part = jnp.sum(hidden_f * edit_in[None, :], axis=1)
    mix_cols = jnp.stack(split_bf16(mix_part, 3), axis=1)
    packed = jnp.concatenate([resid_base, jnp.pad(mix_cols, ((0, 0), (0, 125)))], axis=1)
    packed = jnp.broadcast_to(packed[None], (nv * nm, rows, feat + 128))
    got = lax.all_to_all(packed, ("vocab", "mp"), 0, 0)
    got = jnp.concatenate(in_order(from_peers(got, "rep", nr), r_i)).reshape(nr * nv, nm, rows, feat + 128)

    base = jnp.concatenate([got[:, m, :, :feat].reshape(group, feat) for m in range(nm)], axis=1)
    base_f = base.astype(f32)
    mix = jnp.sum(got[:, :, :, feat : feat + 3].astype(f32), axis=(1, 3)).reshape(group)
    resid = base_f + mix[:, None] * out_all[None, :]
    edit_scale = lax.rsqrt(jnp.mean(resid * resid, axis=1) + epsilon)
    base_scale = lax.rsqrt(jnp.mean(base_f * base_f, axis=1) + epsilon)
    along = jnp.sum(resid * out_all[None, :], axis=1)
    x_edit = (resid * edit_scale[:, None] * gain_all[None, :]).astype(bf16)
    x_base = (base_f * base_scale[:, None] * gain_all[None, :]).astype(bf16)
    direction = jnp.stack(split_bf16(out_all * gain_all, 3) + [jnp.zeros((model,), bf16)] * 5)
    pre = jnp.dot(
        jnp.concatenate([x_edit, x_base, direction]), head, preferred_element_type=f32
    )
    pre_edit = pre[:group]
    pre_base = pre[group : 2 * group]
    toward = jnp.sum(pre[2 * group :], axis=0)
    z_edit = softcap * jnp.tanh(pre_edit / softcap)
    z_base = softcap * jnp.tanh(pre_base / softcap)
    slope = 1.0 - (z_edit / softcap) ** 2
    exp_edit = jnp.exp(z_edit)
    exp_base = jnp.exp(z_base)
    ids = token_ids.reshape(nv, nr, rows).transpose(1, 0, 2).reshape(group)
    first_col = lax.axis_index(everyone) * voc
    onehot = (ids[:, None] == (first_col + jnp.arange(voc, dtype=jnp.int32))[None, :]).astype(f32)
    diff = z_base - z_edit
    pe = exp_edit * slope
    pb = exp_base * slope
    po = onehot * slope
    sums = jnp.stack(
        [
            jnp.sum(a, axis=1)
            for a in (
                exp_edit,
                exp_base,
                exp_base * diff,
                onehot * diff,
                pe * pre_edit,
                pb * pre_edit,
                po * pre_edit,
                pe * toward[None, :],
                pb * toward[None, :],
                po * toward[None, :],
            )
        ]
    )
    weight = mix * edit_scale
    wo = jnp.sum(weight[:, None] * po, axis=0)
    high_e, low_e = split_bf16(pe, 2)
    high_b, low_b = split_bf16(pb, 2)
    tail = jnp.stack(split_bf16(wo, 3) + [jnp.zeros((voc,), bf16)] * 5)
    outer = lax.dot_general(
        jnp.concatenate([high_e, high_b, low_e, low_b, tail]),
        head,
        (((1,), (1,)), ((), ())),
        preferred_element_type=f32,
    )
    rows_e = outer[:group] + outer[2 * group : 3 * group]
    rows_b = outer[group : 2 * group] + outer[3 * group : 4 * group]
    row_o = jnp.sum(outer[4 * group :], axis=0)
    flat = 10 * group
    padded = -(-flat // 1024) * 1024
    mine = jnp.pad(sums.reshape(flat), (0, padded - flat)).reshape(padded // 128, 128)
    theirs = lax.all_to_all(
        jnp.broadcast_to(mine[None], (peers, padded // 128, 128)), everyone, 0, 0
    )
    sums = jnp.sum(theirs, axis=0).reshape(padded)[:flat].reshape(10, group)
    se, sb, kl, gap, ae, ab, ao, te, tb, to = [sums[i] for i in range(10)]
    inv_e = 2.0 / se
    inv_b = 1.0 / sb
    align = ae * inv_e - ab * inv_b - ao
    proj = te * inv_e - tb * inv_b - to
    penalty = kl * inv_b + gap + 2.0 * (jnp.log(se) - jnp.log(sb))
    shrink = edit_scale * align / model
    coeff = edit_scale * proj - shrink * (edit_scale * along)
    weighted = jnp.sum((weight * inv_e)[:, None] * rows_e, axis=0) - jnp.sum((weight * inv_b)[:, None] * rows_b, axis=0) - row_o
    w_hi, w_lo = split_bf16(weighted, 2)
    mine = lax.dynamic_index_in_dim(coeff.reshape(nr, nv, rows), v_i, 1, keepdims=False)
    own = jnp.concatenate([lax.dynamic_index_in_dim(mine, (r_i - k) % nr, 0, keepdims=False) for k in range(nr)])
    part_in = [jnp.sum(u.astype(f32) * own[:, None], axis=0) for u in units]
    part_in = jnp.stack(in_order(part_in, m_i)).astype(bf16)
    slab = jnp.concatenate([w_hi.reshape(nm, feat), w_lo.reshape(nm, feat), part_in], axis=1)
    width = 2 * feat + quarter
    if width % 128 == 0:
        slab = slab.reshape(nm, width // 128, 128)
    slab = jnp.broadcast_to(slab[None, :, None], (nv, nm, nr) + slab.shape[1:])
    back = lax.all_to_all(slab.reshape((peers,) + slab.shape[3:]), everyone, 0, 0)
    back = back.reshape(nv, nm * nr, width).astype(f32)
    grad_in = jnp.sum(back[:, :, 2 * feat :], axis=0).reshape(hidden)
    weighted_own = jnp.sum(back[:, :, :feat] + back[:, :, feat : 2 * feat], axis=(0, 1))
    pull = mix * shrink * edit_scale
    base_own = lax.dynamic_slice_in_dim(base, m_i * feat, feat, 1).astype(f32)
    second = jnp.sum(pull[:, None] * base_own, axis=0) + jnp.sum(pull * mix) * edit_out
    grad_out = norm_gain * weighted_own - second
    penalty = lax.dynamic_slice(penalty.reshape(nr, nv, rows), (r_i, v_i, 0), (1, 1, rows))
    return (penalty.reshape(rows), grad_in, grad_out)


def send_kernel(copies, pieces, base_hbm, hidden_hbm, in_hbm, out_hbm, gain_hbm, packed_hbm, vec_ref, keep_ref, give_ref, base_ref, hidden_ref, in_ref, packed_ref, sems):
    rows, hidden = hidden_ref.shape
    feat = base_ref.shape[1]
    quarter = hidden // (2 * pieces)
    get_hidden = pltpu.make_async_copy(hidden_hbm, hidden_ref, sems.at[0])
    get_in = pltpu.make_async_copy(in_hbm, in_ref, sems.at[1])
    get_base = pltpu.make_async_copy(base_hbm, base_ref, sems.at[2])
    get_out = pltpu.make_async_copy(out_hbm, vec_ref.at[0], sems.at[3])
    get_gain = pltpu.make_async_copy(gain_hbm, vec_ref.at[1], sems.at[4])
    get_hidden.start()
    get_in.start()
    get_base.start()
    get_out.start()
    get_gain.start()
    get_base.wait()
    for i in range(copies):
        packed_ref[i, :, :feat] = base_ref[...]
    get_hidden.wait()
    get_in.wait()
    total = jnp.zeros((rows, 128), f32)
    for c in range(0, hidden, 128):
        total += hidden_ref[:, c : c + 128].astype(f32) * in_ref[:, c : c + 128]
    mix = jnp.sum(total, axis=1, keepdims=True)
    lane = lax.broadcasted_iota(jnp.int32, (rows, 128), 1)
    cols = jnp.zeros((rows, 128), f32)
    for i in range(3):
        piece = mix.astype(bf16).astype(f32)
        cols = jnp.where(lane == i, piece, cols)
        mix = mix - piece
    cols = cols.astype(bf16)
    for i in range(copies):
        packed_ref[i, :, feat:] = cols
    put = pltpu.make_async_copy(packed_ref, packed_hbm, sems.at[5])
    put.start()
    r_i = lax.axis_index("rep")
    for i in range(pieces):
        for ref, r in ((keep_ref, r_i), (give_ref, 1 - r_i)):
            start = pl.multiple_of((2 * i + r) * quarter, 128)
            ref[i] = hidden_ref[:, pl.ds(start, quarter)]
    get_out.wait()
    get_gain.wait()
    put.wait()


def stage_kernel(after_ref, head_hbm, head_ref, sems):
    copies = sems.shape[0]
    part = head_ref.shape[0] // copies
    moves = []
    for i in range(copies):
        span = pl.ds(i * part, part)
        moves.append(pltpu.make_async_copy(head_hbm.at[span], head_ref.at[span], sems.at[i]))
        moves[-1].start()
    for move in moves:
        move.wait()


def score_kernel(nv, nm, own_ref, other_ref, vec_ref, ids_ref, early_ref, head_hbm, slab_hbm, cols_ref, ops_hbm, x_ref, slab_ref, ops_ref, late_ref, sems):
    rows = own_ref.shape[1]
    feat = own_ref.shape[2] - 128
    model, voc = head_hbm.shape
    pair = 2 * rows
    group = 2 * nv * rows
    half = group // 2

    early = early_ref.shape[0]
    part = (model - early) // 2
    moves = []
    for i in range(2):
        move = pltpu.make_async_copy(
            head_hbm.at[pl.ds(early + i * part, part)],
            late_ref.at[pl.ds(i * part, part)],
            sems.at[2 + i],
        )
        move.start()
        moves.append(move)

    lane_t = lax.broadcasted_iota(jnp.int32, (pair, 128), 1)
    for k, got_ref in enumerate((own_ref, other_ref)):
        for v in range(0, nv, 2):
            at = (k * nv + v) * rows

            def tile(m, c):
                first = got_ref[v * nm + m, :, c : c + 128].astype(f32)
                second = got_ref[(v + 1) * nm + m, :, c : c + 128].astype(f32)
                return jnp.concatenate([first, second], axis=0)

            mixed = tile(0, feat)
            for m in range(1, nm):
                mixed += tile(m, feat)
            mix = jnp.sum(mixed, axis=1, keepdims=True)
            mix_b = jnp.broadcast_to(mix, (pair, 128))
            sq_b = jnp.zeros((pair, 128), f32)
            sq_e = jnp.zeros((pair, 128), f32)
            dot_o = jnp.zeros((pair, 128), f32)
            for m in range(nm):
                for c in range(0, feat, 128):
                    out = vec_ref[m, 0, c // 128 : c // 128 + 1, :]
                    b = tile(m, c)
                    e = b + mix_b * out
                    sq_b += b * b
                    sq_e += e * e
                    dot_o += e * out
            scale_e = lax.rsqrt(jnp.sum(sq_e, axis=1, keepdims=True) / model + epsilon)
            scale_b = lax.rsqrt(jnp.sum(sq_b, axis=1, keepdims=True) / model + epsilon)
            along = jnp.sum(dot_o, axis=1, keepdims=True)
            cols_ref[at : at + pair, :] = jnp.where(
                lane_t == 0, mix, jnp.where(lane_t == 1, scale_e, jnp.where(lane_t == 2, along, 0.0))
            )
            scale_e = jnp.broadcast_to(scale_e, (pair, 128))
            scale_b = jnp.broadcast_to(scale_b, (pair, 128))
            for m in range(nm):
                for c in range(0, feat, 128):
                    d = m * feat + c
                    t = c // 128
                    out = vec_ref[m, 0, t : t + 1, :]
                    gain = vec_ref[m, 1, t : t + 1, :]
                    b = tile(m, c)
                    e = b + mix_b * out
                    x_ref[at : at + pair, d : d + 128] = (e * scale_e * gain).astype(bf16)
                    x_ref[group + at : group + at + pair, d : d + 128] = (b * scale_b * gain).astype(bf16)
    sub = lax.broadcasted_iota(jnp.int32, (16, 128), 0)
    for d in range(0, model, 128):
        m, t = d // feat, d % feat // 128
        rest = vec_ref[m, 0, t : t + 1, :] * vec_ref[m, 1, t : t + 1, :]
        block = jnp.zeros((16, 128), f32)
        for i in range(3):
            piece = rest.astype(bf16).astype(f32)
            block = jnp.where(sub == i, piece, block)
            rest = rest - piece
        x_ref[2 * group :, d : d + 128] = block.astype(bf16)

    pre = jnp.dot(x_ref[:, :early], early_ref[...], preferred_element_type=f32)
    for move in moves:
        move.wait()
    pre += jnp.dot(x_ref[:, early:], late_ref[...], preferred_element_type=f32)
    pre_edit = pre[:group]
    pre_base = pre[group : 2 * group]
    toward = jnp.sum(pre[2 * group :], axis=0, keepdims=True)
    th = jnp.tanh(pre_edit / softcap)
    z_edit = softcap * th
    z_base = softcap * jnp.tanh(pre_base / softcap)
    slope = 1.0 - th * th
    exp_edit = jnp.exp(z_edit)
    exp_base = jnp.exp(z_base)
    first_col = lax.axis_index(("vocab", "mp", "rep")) * voc
    column = lax.broadcasted_iota(jnp.int32, (group, voc), 1) + first_col
    hit = column == ids_ref[...]
    diff = z_base - z_edit
    pe = exp_edit * slope
    pb = exp_base * slope
    po = jnp.where(hit, slope, 0.0)

    def total(a):
        return jnp.sum(a, axis=1, keepdims=True)

    sums = [
        total(exp_edit),
        total(exp_base),
        total(exp_base * diff),
        total(jnp.where(hit, diff, 0.0)),
        total(pe * pre_edit),
        total(pb * pre_edit),
        total(po * pre_edit),
        total(pe * toward),
        total(pb * toward),
        total(po * toward),
    ]
    lane = lax.broadcasted_iota(jnp.int32, (group, 128), 1)
    first = jnp.zeros((group, 128), f32)
    second = jnp.zeros((group, 128), f32)
    for i in range(8):
        first = jnp.where(lane == i, sums[i], first)
    for i in range(8, 10):
        second = jnp.where(lane == i - 8, sums[i], second)
    straight = jnp.concatenate([first, second], axis=0)
    swapped = jnp.concatenate([first[half:], first[:half], second[half:], second[:half]], axis=0)
    table = jnp.where(lax.axis_index("rep") == 0, straight, swapped)
    table = table.T[:8]
    for p in range(slab_ref.shape[0]):
        slab_ref[p] = table
    put_slab = pltpu.make_async_copy(slab_ref, slab_hbm, sems.at[0])
    put_slab.start()

    high_e = pe.astype(bf16)
    high_b = pb.astype(bf16)
    ops_ref[:group] = high_e
    ops_ref[group : 2 * group] = high_b
    ops_ref[2 * group : 3 * group] = (pe - high_e.astype(f32)).astype(bf16)
    ops_ref[3 * group : 4 * group] = (pb - high_b.astype(f32)).astype(bf16)
    weight = cols_ref[:, 0:1] * cols_ref[:, 1:2]
    rest = jnp.sum(weight * po, axis=0, keepdims=True)
    sub = lax.broadcasted_iota(jnp.int32, (16, voc), 0)
    block = jnp.zeros((16, voc), f32)
    for i in range(3):
        piece = rest.astype(bf16).astype(f32)
        block = jnp.where(sub == i, piece, block)
        rest = rest - piece
    ops_ref[4 * group :] = block.astype(bf16)
    put_ops = pltpu.make_async_copy(ops_ref, ops_hbm, sems.at[1])
    put_ops.start()
    put_slab.wait()
    put_ops.wait()


def outer_kernel(ops_hbm, head_hbm, outer_ref, ops_ref, head_ref, sems):
    both = outer_ref.shape[0] - 16
    part = 512
    get = pltpu.make_async_copy(ops_hbm, ops_ref, sems.at[0])
    get.start()
    moves = []
    for i in range(head_hbm.shape[0] // part):
        span = pl.ds(i * part, part)
        moves.append(pltpu.make_async_copy(head_hbm.at[span], head_ref.at[span], sems.at[1 + i]))
        moves[i].start()
    get.wait()
    for i, move in enumerate(moves):
        move.wait()
        c = i * part
        block = lax.dot_general(
            ops_ref[...],
            head_ref[c : c + part, :],
            (((1,), (1,)), ((), ())),
            preferred_element_type=f32,
        )
        outer_ref[:both, c : c + part] = block[:both] + block[both : 2 * both]
        outer_ref[both:, c : c + part] = block[2 * both :]


def close_kernel(nv, nm, theirs_ref, cols_ref, outer_ref, own_ref, all_ref, *refs):
    units = refs[:nm]
    slab_hbm, penalty_hbm, coeff_ref, pen_ref, pull_ref, vec_ref, slab_ref, second_ref, sems = refs[nm:]
    rows = own_ref.shape[1]
    feat = own_ref.shape[2] - 128
    model = outer_ref.shape[1]
    group = 2 * nv * rows
    half = group // 2
    tiles = feat // 128
    v_i = lax.axis_index("vocab")
    m_i = lax.axis_index("mp")
    r_i = lax.axis_index("rep")

    table = theirs_ref[0]
    for p in range(1, theirs_ref.shape[0]):
        table += theirs_ref[p]
    table = jnp.concatenate([table, jnp.zeros((120, 128), f32)], axis=0).T
    first = table[:group]
    second = table[group:]
    swap_first = jnp.concatenate([first[half:], first[:half]], axis=0)
    swap_second = jnp.concatenate([second[half:], second[:half]], axis=0)
    first = jnp.where(r_i == 0, first, swap_first)
    second = jnp.where(r_i == 0, second, swap_second)
    se, sb, kl, gap, ae, ab, ao, te = [first[:, i : i + 1] for i in range(8)]
    tb, to = second[:, 0:1], second[:, 1:2]
    mix = cols_ref[:, 0:1]
    scale = cols_ref[:, 1:2]
    along = cols_ref[:, 2:3]
    inv_e = 2.0 / se
    inv_b = 1.0 / sb
    align = ae * inv_e - ab * inv_b - ao
    proj = te * inv_e - tb * inv_b - to
    penalty = kl * inv_b + gap + 2.0 * (jnp.log(se) - jnp.log(sb))
    shrink = scale * align / model
    coeff = scale * proj - shrink * (scale * along)
    weight = mix * scale
    pull = weight * shrink
    coeff_ref[...] = jnp.broadcast_to(coeff, (group, 128))
    pen_ref[...] = jnp.broadcast_to(penalty, (group, 128))
    put_pen = pltpu.make_async_copy(
        pen_ref.at[pl.ds(pl.multiple_of(v_i * rows, rows), rows)], penalty_hbm, sems.at[0]
    )
    put_pen.start()

    pull_ref[...] = jnp.broadcast_to(pull, (group, 128))
    pulls = pull_ref[pl.ds(pl.multiple_of(v_i * rows, rows), rows), :]
    pull_ref[...] = jnp.broadcast_to(pull * mix, (group, 128))
    pulled = jnp.sum(pull_ref[pl.ds(pl.multiple_of(v_i * rows, rows), rows), :], axis=0, keepdims=True)
    for t in range(tiles):
        part = own_ref[v_i * nm + m_i, :, t * 128 : (t + 1) * 128].astype(f32) * pulls
        second_ref[t : t + 1, :] = (
            jnp.sum(part, axis=0, keepdims=True) + pulled * all_ref[m_i, 0, t : t + 1, :]
        )

    by_e = jnp.broadcast_to(weight * inv_e, (group, 128))
    by_b = jnp.broadcast_to(weight * inv_b, (group, 128))
    for m in range(nm):
        for t in range(tiles):
            d = m * feat + t * 128
            plus = outer_ref[:group, d : d + 128] * by_e
            less = outer_ref[group : 2 * group, d : d + 128] * by_b
            row = jnp.sum(plus - less, axis=0, keepdims=True)
            row -= jnp.sum(outer_ref[2 * group :, d : d + 128], axis=0, keepdims=True)
            row = row * all_ref[m, 1, t : t + 1, :] - jnp.where(
                m_i == m, second_ref[t : t + 1, :], 0.0
            )
            high = row.astype(bf16).astype(f32)
            vec_ref[m, t : t + 1, :] = high
            vec_ref[m, tiles + t : tiles + t + 1, :] = row - high
    own = jnp.concatenate(
        [
            coeff_ref[pl.ds(pl.multiple_of((k * nv + v_i) * rows, rows), rows), :]
            for k in range(2)
        ],
        axis=0,
    )
    for k in range(nm):
        m = lax.rem(m_i - k + nm, nm)
        for t in range(units[k].shape[1] // 128):
            row = jnp.sum(units[k][:, t * 128 : (t + 1) * 128].astype(f32) * own, axis=0, keepdims=True)
            vec_ref[m, pl.ds(2 * tiles + t, 1), :] = row
    for m in range(nm):
        block = vec_ref[m].astype(bf16)
        for v in range(nv):
            for r in range(2):
                slab_ref[(v * nm + m) * 2 + r] = block
    put_slab = pltpu.make_async_copy(slab_ref, slab_hbm, sems.at[1])
    put_slab.start()

    put_pen.wait()
    put_slab.wait()


def sum_kernel(back_ref, in_ref, out_ref):
    peers = back_ref.shape[0]
    tiles = out_ref.shape[0]
    units = back_ref.shape[1] - 2 * tiles
    pieces = in_ref.shape[0] // units
    wide = jnp.zeros((tiles, 128), f32)
    for q in range(pieces):
        total = back_ref[q].astype(f32)
        for p in range(q + pieces, peers, pieces):
            total += back_ref[p].astype(f32)
        wide += total[:tiles] + total[tiles : 2 * tiles]
        in_ref[q * units : (q + 1) * units, :] = total[2 * tiles :]
    out_ref[...] = wide


def in_hbm(value):
    return pltpu.with_memory_space_constraint(value, pltpu.HBM)


def call(kernel, out_shape, scratch=(), megabytes=6, **more):
    return pl.pallas_call(
        kernel,
        out_shape=out_shape,
        scratch_shapes=scratch,
        compiler_params=pltpu.CompilerParams(vmem_limit_bytes=megabytes << 20),
        **more,
    )


def fused(nv, nm, nr, resid_base, mlp_hidden, edit_in, edit_out, norm_gain, head, token_ids):
    rows, feat = resid_base.shape
    hidden = mlp_hidden.shape[1]
    model, voc = head.shape
    group = nv * nr * rows
    peers = nv * nm * nr
    quarter = hidden // (nm * nr)
    everyone = ("vocab", "mp", "rep")
    m_i = lax.axis_index("mp")
    r_i = lax.axis_index("rep")
    shape = jax.ShapeDtypeStruct

    tiles = feat // 128
    hbm = pl.BlockSpec(memory_space=pltpu.HBM)
    vmem = pl.BlockSpec(memory_space=pltpu.VMEM)
    out_tiles = edit_out.reshape(tiles, 128)
    gain_tiles = norm_gain.reshape(tiles, 128)

    early = model // 2

    packed, vectors, keep, give = call(
        functools.partial(send_kernel, nv * nm, nm),
        (
            pltpu.HBM((nv * nm, rows, feat + 128), bf16),
            shape((2, tiles, 128), f32),
            shape((nm, rows, quarter), bf16),
            shape((nm, rows, quarter), bf16),
        ),
        [
            pltpu.VMEM((rows, feat), bf16),
            pltpu.VMEM((rows, hidden), bf16),
            pltpu.VMEM((1, hidden), f32),
            pltpu.VMEM((nv * nm, rows, feat + 128), bf16),
            pltpu.SemaphoreType.DMA((6,)),
        ],
        in_specs=[hbm] * 5,
        out_specs=(hbm, vmem, vmem, vmem),
    )(
        *(
            in_hbm(a)
            for a in (resid_base, mlp_hidden, edit_in.reshape(1, hidden), out_tiles, gain_tiles)
        )
    )
    got = lax.all_to_all(packed, ("vocab", "mp"), 0, 0)
    other = lax.ppermute(got, "rep", [(0, 1), (1, 0)])
    vectors = from_peers(vectors, "mp", nm)
    staged = call(
        stage_kernel,
        pltpu.VMEM((early, voc), bf16),
        [pltpu.SemaphoreType.DMA((4,))],
        in_specs=[vmem, hbm],
        out_specs=vmem,
    )(got, in_hbm(head))
    vectors = jnp.stack(in_order(vectors, m_i))
    ids = token_ids.reshape(nv, nr, rows)
    ids = jnp.concatenate(
        [lax.dynamic_index_in_dim(ids, (r_i + k) % nr, 1, keepdims=False) for k in range(nr)]
    ).reshape(group, 1)

    units = jnp.concatenate([keep, lax.ppermute(give, "rep", [(0, 1), (1, 0)])], axis=1)
    units = to_peers(
        lambda m: lax.dynamic_index_in_dim(units, m, 0, keepdims=False), "mp", nm, m_i
    )
    slab, cols, ops = call(
        functools.partial(score_kernel, nv, nm),
        (
            pltpu.HBM((peers, 8, 128), f32),
            shape((group, 128), f32),
            pltpu.HBM((4 * group + 16, voc), bf16),
        ),
        [
            pltpu.VMEM((2 * group + 16, model), bf16),
            pltpu.VMEM((peers, 8, 128), f32),
            pltpu.VMEM((4 * group + 16, voc), bf16),
            pltpu.VMEM((model - early, voc), bf16),
            pltpu.SemaphoreType.DMA((4,)),
        ],
        8,
        in_specs=[vmem] * 5 + [hbm],
        out_specs=(hbm, vmem, hbm),
    )(got, other, vectors, ids, staged, in_hbm(head))
    theirs = lax.all_to_all(slab, everyone, 0, 0)
    outer = call(
        outer_kernel,
        shape((2 * group + 16, model), f32),
        [
            pltpu.VMEM((4 * group + 16, voc), bf16),
            pltpu.VMEM((model, voc), bf16),
            pltpu.SemaphoreType.DMA((1 + model // 512,)),
        ],
        12,
        in_specs=[hbm, hbm],
    )(in_hbm(ops), in_hbm(head))

    width = (2 * feat + quarter) // 128
    slab, penalty = call(
        functools.partial(close_kernel, nv, nm),
        (pltpu.HBM((peers, width, 128), bf16), pltpu.HBM((rows, 128), f32)),
        [
            pltpu.VMEM((group, 128), f32),
            pltpu.VMEM((group, 128), f32),
            pltpu.VMEM((group, 128), f32),
            pltpu.VMEM((nm, width, 128), f32),
            pltpu.VMEM((peers, width, 128), bf16),
            pltpu.VMEM((tiles, 128), f32),
            pltpu.SemaphoreType.DMA((2,)),
        ],
        in_specs=[vmem] * (5 + nm),
        out_specs=(hbm, hbm),
    )(theirs, cols, outer, got, vectors, *units)
    back = lax.all_to_all(slab, everyone, 0, 0)
    grad_in, grad_out = call(
        sum_kernel, (shape((hidden // 128, 128), f32), shape((tiles, 128), f32))
    )(back)
    return (penalty[:, 0], grad_in.reshape(hidden), grad_out.reshape(feat))


def local(nv, nm, nr, resid_base, mlp_hidden, *rest):
    rows, feat = resid_base.shape
    quarter = mlp_hidden.shape[1] // (nm * nr)
    whole_tiles = rows == 8 and feat % 128 == 0 and quarter % 128 == 0
    small = nr == 2 and nv % 2 == 0 and nv * nr * rows == 64
    step = fused if whole_tiles and small else plain
    return step(nv, nm, nr, resid_base, mlp_hidden, *rest)


def solution(mesh):
    in_specs = (
        P(("parts", "vocab", "rep"), "mp"),
        P(("parts", "vocab", "rep"), "mp"),
        P(("parts", "mp")),
        P(("parts", "mp")),
        P("mp"),
        P(None, ("vocab", "mp", "rep")),
        P("parts"),
    )
    out_specs = (P(("parts", "vocab", "rep")), P(("parts", "mp")), P(("parts", "mp")))
    step = functools.partial(local, mesh.shape["vocab"], mesh.shape["mp"], mesh.shape["rep"])
    return jax.shard_map(step, mesh=mesh, in_specs=in_specs, out_specs=out_specs, check_vma=False)
```

```python
import functools

import jax
import jax.numpy as jnp
from jax import lax
from jax.experimental import pallas as pl
from jax.experimental.pallas import tpu as pltpu
from jax.sharding import PartitionSpec as P

softcap = 30.0
epsilon = 1e-06
bf16 = jnp.bfloat16
f32 = jnp.float32


def split_bf16(value, pieces):
    out = []
    for _ in range(pieces):
        part = lax.reduce_precision(value, 8, 7)
        out.append(part.astype(bf16))
        value = value - part
    return out


def from_peers(value, axis, size):
    moves = [[(i, (i + k) % size) for i in range(size)] for k in range(size)]
    return [value] + [lax.ppermute(value, axis, moves[k]) for k in range(1, size)]


def to_peers(pick, axis, size, index):
    moves = [[(i, (i + k) % size) for i in range(size)] for k in range(size)]
    return [pick(index)] + [
        lax.ppermute(pick((index + k) % size), axis, moves[k]) for k in range(1, size)
    ]


def in_order(values, index):
    size = len(values)
    ordered = []
    for j in range(size):
        value = values[0]
        for k in range(1, size):
            value = jnp.where((index - j) % size == k, values[k], value)
        ordered.append(value)
    return ordered


def plain(nv, nm, nr, resid_base, mlp_hidden, edit_in, edit_out, norm_gain, head, token_ids):
    rows, feat = resid_base.shape
    hidden = mlp_hidden.shape[1]
    model, voc = head.shape
    group = nv * nr * rows
    peers = nv * nm * nr
    quarter = hidden // (nm * nr)
    everyone = ("vocab", "mp", "rep")

    v_i = lax.axis_index("vocab")
    m_i = lax.axis_index("mp")
    r_i = lax.axis_index("rep")

    vectors = from_peers(jnp.stack([edit_out, norm_gain]), "mp", nm)
    vectors = jnp.concatenate(in_order(vectors, m_i), axis=1)
    out_all = vectors[0]
    gain_all = vectors[1]

    units = mlp_hidden.reshape(rows, nm, nr, quarter)
    units = jnp.concatenate(
        [
            part
            for part in to_peers(
                lambda r: lax.dynamic_index_in_dim(units, r, 2, keepdims=False), "rep", nr, r_i
            )
        ]
    )
    units = to_peers(
        lambda m: lax.dynamic_index_in_dim(units, m, 1, keepdims=False), "mp", nm, m_i
    )

    hidden_f = mlp_hidden.astype(f32)
    mix_part = jnp.sum(hidden_f * edit_in[None, :], axis=1)
    mix_cols = jnp.stack(split_bf16(mix_part, 3), axis=1)
    packed = jnp.concatenate([resid_base, jnp.pad(mix_cols, ((0, 0), (0, 125)))], axis=1)
    packed = jnp.broadcast_to(packed[None], (nv * nm, rows, feat + 128))
    got = lax.all_to_all(packed, ("vocab", "mp"), 0, 0)
    got = jnp.concatenate(in_order(from_peers(got, "rep", nr), r_i)).reshape(nr * nv, nm, rows, feat + 128)

    base = jnp.concatenate([got[:, m, :, :feat].reshape(group, feat) for m in range(nm)], axis=1)
    base_f = base.astype(f32)
    mix = jnp.sum(got[:, :, :, feat : feat + 3].astype(f32), axis=(1, 3)).reshape(group)
    resid = base_f + mix[:, None] * out_all[None, :]
    edit_scale = lax.rsqrt(jnp.mean(resid * resid, axis=1) + epsilon)
    base_scale = lax.rsqrt(jnp.mean(base_f * base_f, axis=1) + epsilon)
    along = jnp.sum(resid * out_all[None, :], axis=1)
    x_edit = (resid * edit_scale[:, None] * gain_all[None, :]).astype(bf16)
    x_base = (base_f * base_scale[:, None] * gain_all[None, :]).astype(bf16)
    direction = jnp.stack(split_bf16(out_all * gain_all, 3) + [jnp.zeros((model,), bf16)] * 5)
    pre = jnp.dot(
        jnp.concatenate([x_edit, x_base, direction]), head, preferred_element_type=f32
    )
    pre_edit = pre[:group]
    pre_base = pre[group : 2 * group]
    toward = jnp.sum(pre[2 * group :], axis=0)
    z_edit = softcap * jnp.tanh(pre_edit / softcap)
    z_base = softcap * jnp.tanh(pre_base / softcap)
    slope = 1.0 - (z_edit / softcap) ** 2
    exp_edit = jnp.exp(z_edit)
    exp_base = jnp.exp(z_base)
    ids = token_ids.reshape(nv, nr, rows).transpose(1, 0, 2).reshape(group)
    first_col = lax.axis_index(everyone) * voc
    onehot = (ids[:, None] == (first_col + jnp.arange(voc, dtype=jnp.int32))[None, :]).astype(f32)
    diff = z_base - z_edit
    pe = exp_edit * slope
    pb = exp_base * slope
    po = onehot * slope
    sums = jnp.stack(
        [
            jnp.sum(a, axis=1)
            for a in (
                exp_edit,
                exp_base,
                exp_base * diff,
                onehot * diff,
                pe * pre_edit,
                pb * pre_edit,
                po * pre_edit,
                pe * toward[None, :],
                pb * toward[None, :],
                po * toward[None, :],
            )
        ]
    )
    weight = mix * edit_scale
    wo = jnp.sum(weight[:, None] * po, axis=0)
    high_e, low_e = split_bf16(pe, 2)
    high_b, low_b = split_bf16(pb, 2)
    tail = jnp.stack(split_bf16(wo, 3) + [jnp.zeros((voc,), bf16)] * 5)
    outer = lax.dot_general(
        jnp.concatenate([high_e, high_b, low_e, low_b, tail]),
        head,
        (((1,), (1,)), ((), ())),
        preferred_element_type=f32,
    )
    rows_e = outer[:group] + outer[2 * group : 3 * group]
    rows_b = outer[group : 2 * group] + outer[3 * group : 4 * group]
    row_o = jnp.sum(outer[4 * group :], axis=0)
    flat = 10 * group
    padded = -(-flat // 1024) * 1024
    mine = jnp.pad(sums.reshape(flat), (0, padded - flat)).reshape(padded // 128, 128)
    theirs = lax.all_to_all(
        jnp.broadcast_to(mine[None], (peers, padded // 128, 128)), everyone, 0, 0
    )
    sums = jnp.sum(theirs, axis=0).reshape(padded)[:flat].reshape(10, group)
    se, sb, kl, gap, ae, ab, ao, te, tb, to = [sums[i] for i in range(10)]
    inv_e = 2.0 / se
    inv_b = 1.0 / sb
    align = ae * inv_e - ab * inv_b - ao
    proj = te * inv_e - tb * inv_b - to
    penalty = kl * inv_b + gap + 2.0 * (jnp.log(se) - jnp.log(sb))
    shrink = edit_scale * align / model
    coeff = edit_scale * proj - shrink * (edit_scale * along)
    weighted = jnp.sum((weight * inv_e)[:, None] * rows_e, axis=0) - jnp.sum((weight * inv_b)[:, None] * rows_b, axis=0) - row_o
    w_hi, w_lo = split_bf16(weighted, 2)
    mine = lax.dynamic_index_in_dim(coeff.reshape(nr, nv, rows), v_i, 1, keepdims=False)
    own = jnp.concatenate([lax.dynamic_index_in_dim(mine, (r_i - k) % nr, 0, keepdims=False) for k in range(nr)])
    part_in = [jnp.sum(u.astype(f32) * own[:, None], axis=0) for u in units]
    part_in = jnp.stack(in_order(part_in, m_i)).astype(bf16)
    slab = jnp.concatenate([w_hi.reshape(nm, feat), w_lo.reshape(nm, feat), part_in], axis=1)
    width = 2 * feat + quarter
    if width % 128 == 0:
        slab = slab.reshape(nm, width // 128, 128)
    slab = jnp.broadcast_to(slab[None, :, None], (nv, nm, nr) + slab.shape[1:])
    back = lax.all_to_all(slab.reshape((peers,) + slab.shape[3:]), everyone, 0, 0)
    back = back.reshape(nv, nm * nr, width).astype(f32)
    grad_in = jnp.sum(back[:, :, 2 * feat :], axis=0).reshape(hidden)
    weighted_own = jnp.sum(back[:, :, :feat] + back[:, :, feat : 2 * feat], axis=(0, 1))
    pull = mix * shrink * edit_scale
    base_own = lax.dynamic_slice_in_dim(base, m_i * feat, feat, 1).astype(f32)
    second = jnp.sum(pull[:, None] * base_own, axis=0) + jnp.sum(pull * mix) * edit_out
    grad_out = norm_gain * weighted_own - second
    penalty = lax.dynamic_slice(penalty.reshape(nr, nv, rows), (r_i, v_i, 0), (1, 1, rows))
    return (penalty.reshape(rows), grad_in, grad_out)


def send_kernel(copies, pieces, base_hbm, hidden_hbm, in_hbm, out_hbm, gain_hbm, packed_hbm, vec_ref, *refs):
    unit_refs = refs[: 2 * pieces]
    base_ref, hidden_ref, in_ref, packed_ref, sems = refs[2 * pieces :]
    rows, hidden = hidden_ref.shape
    feat = base_ref.shape[1]
    quarter = hidden // (2 * pieces)
    get_hidden = pltpu.make_async_copy(hidden_hbm, hidden_ref, sems.at[0])
    get_in = pltpu.make_async_copy(in_hbm, in_ref, sems.at[1])
    get_base = pltpu.make_async_copy(base_hbm, base_ref, sems.at[2])
    get_out = pltpu.make_async_copy(out_hbm, vec_ref.at[0], sems.at[3])
    get_gain = pltpu.make_async_copy(gain_hbm, vec_ref.at[1], sems.at[4])
    get_hidden.start()
    get_in.start()
    get_base.start()
    get_out.start()
    get_gain.start()
    get_base.wait()
    for i in range(copies):
        packed_ref[i, :, :feat] = base_ref[...]
    get_hidden.wait()
    get_in.wait()
    total = jnp.zeros((rows, 128), f32)
    for c in range(0, hidden, 128):
        total += hidden_ref[:, c : c + 128].astype(f32) * in_ref[:, c : c + 128]
    mix = jnp.sum(total, axis=1, keepdims=True)
    lane = lax.broadcasted_iota(jnp.int32, (rows, 128), 1)
    cols = jnp.zeros((rows, 128), f32)
    for i in range(3):
        piece = mix.astype(bf16).astype(f32)
        cols = jnp.where(lane == i, piece, cols)
        mix = mix - piece
    cols = cols.astype(bf16)
    for i in range(copies):
        packed_ref[i, :, feat:] = cols
    put = pltpu.make_async_copy(packed_ref, packed_hbm, sems.at[5])
    put.start()
    m_i = lax.axis_index("mp")
    r_i = lax.axis_index("rep")
    for i in range(pieces):
        for j in range(2):
            to = 2 * lax.rem(m_i + i, pieces) + lax.rem(r_i + j, 2)
            start = pl.multiple_of(to * quarter, 128)
            unit_refs[2 * i + j][...] = hidden_ref[:, pl.ds(start, quarter)]
    get_out.wait()
    get_gain.wait()
    put.wait()


def normed_rows(nv, nm, got_ref, vec_ref, cols_ref, x_ref):
    rows = got_ref.shape[1]
    feat = got_ref.shape[2] - 128
    model = nm * feat
    half = nv * rows
    pair = 2 * rows
    lane = lax.broadcasted_iota(jnp.int32, (pair, 128), 1)
    for v in range(0, nv, 2):
        at = v * rows

        def tile(m, c):
            first = got_ref[v * nm + m, :, c : c + 128].astype(f32)
            second = got_ref[(v + 1) * nm + m, :, c : c + 128].astype(f32)
            return jnp.concatenate([first, second], axis=0)

        mixed = tile(0, feat)
        for m in range(1, nm):
            mixed += tile(m, feat)
        mix = jnp.sum(mixed, axis=1, keepdims=True)
        mix_b = jnp.broadcast_to(mix, (pair, 128))
        sq_b = jnp.zeros((pair, 128), f32)
        sq_e = jnp.zeros((pair, 128), f32)
        dot_o = jnp.zeros((pair, 128), f32)
        for m in range(nm):
            for c in range(0, feat, 128):
                out = vec_ref[m, 0, c // 128 : c // 128 + 1, :]
                b = tile(m, c)
                e = b + mix_b * out
                sq_b += b * b
                sq_e += e * e
                dot_o += e * out
        scale_e = lax.rsqrt(jnp.sum(sq_e, axis=1, keepdims=True) / model + epsilon)
        scale_b = lax.rsqrt(jnp.sum(sq_b, axis=1, keepdims=True) / model + epsilon)
        along = jnp.sum(dot_o, axis=1, keepdims=True)
        cols_ref[at : at + pair, :] = jnp.where(
            lane == 0, mix, jnp.where(lane == 1, scale_e, jnp.where(lane == 2, along, 0.0))
        )
        scale_e = jnp.broadcast_to(scale_e, (pair, 128))
        scale_b = jnp.broadcast_to(scale_b, (pair, 128))
        for m in range(nm):
            for c in range(0, feat, 128):
                d = m * feat + c
                t = c // 128
                out = vec_ref[m, 0, t : t + 1, :]
                gain = vec_ref[m, 1, t : t + 1, :]
                b = tile(m, c)
                e = b + mix_b * out
                x_ref[at : at + pair, d : d + 128] = (e * scale_e * gain).astype(bf16)
                x_ref[half + at : half + at + pair, d : d + 128] = (b * scale_b * gain).astype(bf16)


def early_kernel(nv, nm, own_ref, vec_ref, head_hbm, head_ref, pre_ref, cols_ref, x_ref, sems):
    model = head_hbm.shape[0]
    part = model // sems.shape[0]
    moves = []
    for i in range(sems.shape[0]):
        span = pl.ds(i * part, part)
        moves.append(pltpu.make_async_copy(head_hbm.at[span], head_ref.at[span], sems.at[i]))
        moves[i].start()
    feat = own_ref.shape[2] - 128
    half = cols_ref.shape[0]
    normed_rows(nv, nm, own_ref, vec_ref, cols_ref, x_ref)
    sub = lax.broadcasted_iota(jnp.int32, (16, 128), 0)
    for d in range(0, model, 128):
        m, t = d // feat, d % feat // 128
        rest = vec_ref[m, 0, t : t + 1, :] * vec_ref[m, 1, t : t + 1, :]
        block = jnp.zeros((16, 128), f32)
        for i in range(3):
            piece = rest.astype(bf16).astype(f32)
            block = jnp.where(sub == i, piece, block)
            rest = rest - piece
        x_ref[2 * half :, d : d + 128] = block.astype(bf16)
    pre = None
    for i, move in enumerate(moves):
        move.wait()
        span = slice(i * part, (i + 1) * part)
        block = jnp.dot(x_ref[:, span], head_ref[span, :], preferred_element_type=f32)
        pre = block if pre is None else pre + block
    pre_ref[...] = pre


def score_kernel(nv, nm, other_ref, vec_ref, ids_ref, head_ref, early_ref, early_cols_ref, slab_hbm, cols_ref, ops_hbm, x_ref, slab_ref, ops_ref, sems):
    voc = head_ref.shape[1]
    half = early_cols_ref.shape[0]
    group = 2 * half
    cols_ref[:half] = early_cols_ref[...]
    normed_rows(nv, nm, other_ref, vec_ref, cols_ref.at[half:], x_ref)
    late = jnp.dot(x_ref[...], head_ref[...], preferred_element_type=f32)
    pre_edit = jnp.concatenate([early_ref[:half], late[:half]], axis=0)
    pre_base = jnp.concatenate([early_ref[half:group], late[half:]], axis=0)
    toward = jnp.sum(early_ref[group:], axis=0, keepdims=True)
    th = jnp.tanh(pre_edit / softcap)
    z_edit = softcap * th
    z_base = softcap * jnp.tanh(pre_base / softcap)
    slope = 1.0 - th * th
    exp_edit = jnp.exp(z_edit)
    exp_base = jnp.exp(z_base)
    first_col = lax.axis_index(("vocab", "mp", "rep")) * voc
    column = lax.broadcasted_iota(jnp.int32, (group, voc), 1) + first_col
    hit = column == ids_ref[...]
    diff = z_base - z_edit
    pe = exp_edit * slope
    pb = exp_base * slope
    po = jnp.where(hit, slope, 0.0)

    def total(a):
        return jnp.sum(a, axis=1, keepdims=True)

    sums = [
        total(exp_edit),
        total(exp_base),
        total(exp_base * diff),
        total(jnp.where(hit, diff, 0.0)),
        total(pe * pre_edit),
        total(pb * pre_edit),
        total(po * pre_edit),
        total(pe * toward),
        total(pb * toward),
        total(po * toward),
    ]
    lane = lax.broadcasted_iota(jnp.int32, (group, 128), 1)
    first = jnp.zeros((group, 128), f32)
    second = jnp.zeros((group, 128), f32)
    for i in range(8):
        first = jnp.where(lane == i, sums[i], first)
    for i in range(8, 10):
        second = jnp.where(lane == i - 8, sums[i], second)
    straight = jnp.concatenate([first, second], axis=0)
    swapped = jnp.concatenate([first[half:], first[:half], second[half:], second[:half]], axis=0)
    table = jnp.where(lax.axis_index("rep") == 0, straight, swapped)
    table = table.T[:8]
    for p in range(slab_ref.shape[0]):
        slab_ref[p] = table
    put_slab = pltpu.make_async_copy(slab_ref, slab_hbm, sems.at[0])
    put_slab.start()

    high_e = pe.astype(bf16)
    high_b = pb.astype(bf16)
    ops_ref[:group] = high_e
    ops_ref[group : 2 * group] = high_b
    ops_ref[2 * group : 3 * group] = (pe - high_e.astype(f32)).astype(bf16)
    ops_ref[3 * group : 4 * group] = (pb - high_b.astype(f32)).astype(bf16)
    weight = cols_ref[:, 0:1] * cols_ref[:, 1:2]
    rest = jnp.sum(weight * po, axis=0, keepdims=True)
    sub = lax.broadcasted_iota(jnp.int32, (16, voc), 0)
    block = jnp.zeros((16, voc), f32)
    for i in range(3):
        piece = rest.astype(bf16).astype(f32)
        block = jnp.where(sub == i, piece, block)
        rest = rest - piece
    ops_ref[4 * group :] = block.astype(bf16)
    put_ops = pltpu.make_async_copy(ops_ref, ops_hbm, sems.at[1])
    put_ops.start()
    put_slab.wait()
    put_ops.wait()


def outer_kernel(ops_hbm, head_hbm, outer_ref, ops_ref, head_ref, sems):
    both = outer_ref.shape[0] - 16
    part = 512
    get = pltpu.make_async_copy(ops_hbm, ops_ref, sems.at[0])
    get.start()
    moves = []
    for i in range(head_hbm.shape[0] // part):
        span = pl.ds(i * part, part)
        moves.append(pltpu.make_async_copy(head_hbm.at[span], head_ref.at[span], sems.at[1 + i]))
        moves[i].start()
    get.wait()
    for i, move in enumerate(moves):
        move.wait()
        c = i * part
        block = lax.dot_general(
            ops_ref[...],
            head_ref[c : c + part, :],
            (((1,), (1,)), ((), ())),
            preferred_element_type=f32,
        )
        outer_ref[:both, c : c + part] = block[:both] + block[both : 2 * both]
        outer_ref[both:, c : c + part] = block[2 * both :]


def close_kernel(nv, nm, theirs_ref, cols_ref, outer_ref, own_ref, all_ref, *refs):
    units = refs[: 2 * nm]
    slab_hbm, penalty_hbm, coeff_ref, pen_ref, pull_ref, vec_ref, slab_ref, second_ref, sems = refs[2 * nm :]
    rows = own_ref.shape[1]
    feat = own_ref.shape[2] - 128
    model = outer_ref.shape[1]
    group = 2 * nv * rows
    half = group // 2
    tiles = feat // 128
    v_i = lax.axis_index("vocab")
    m_i = lax.axis_index("mp")
    r_i = lax.axis_index("rep")

    table = theirs_ref[0]
    for p in range(1, theirs_ref.shape[0]):
        table += theirs_ref[p]
    table = jnp.concatenate([table, jnp.zeros((120, 128), f32)], axis=0).T
    first = table[:group]
    second = table[group:]
    swap_first = jnp.concatenate([first[half:], first[:half]], axis=0)
    swap_second = jnp.concatenate([second[half:], second[:half]], axis=0)
    first = jnp.where(r_i == 0, first, swap_first)
    second = jnp.where(r_i == 0, second, swap_second)
    se, sb, kl, gap, ae, ab, ao, te = [first[:, i : i + 1] for i in range(8)]
    tb, to = second[:, 0:1], second[:, 1:2]
    mix = cols_ref[:, 0:1]
    scale = cols_ref[:, 1:2]
    along = cols_ref[:, 2:3]
    inv_e = 2.0 / se
    inv_b = 1.0 / sb
    align = ae * inv_e - ab * inv_b - ao
    proj = te * inv_e - tb * inv_b - to
    penalty = kl * inv_b + gap + 2.0 * (jnp.log(se) - jnp.log(sb))
    shrink = scale * align / model
    coeff = scale * proj - shrink * (scale * along)
    weight = mix * scale
    pull = weight * shrink
    coeff_ref[...] = jnp.broadcast_to(coeff, (group, 128))
    pen_ref[...] = jnp.broadcast_to(penalty, (group, 128))
    put_pen = pltpu.make_async_copy(
        pen_ref.at[pl.ds(pl.multiple_of(v_i * rows, rows), rows)], penalty_hbm, sems.at[0]
    )
    put_pen.start()

    pull_ref[...] = jnp.broadcast_to(pull, (group, 128))
    pulls = pull_ref[pl.ds(pl.multiple_of(v_i * rows, rows), rows), :]
    pull_ref[...] = jnp.broadcast_to(pull * mix, (group, 128))
    pulled = jnp.sum(pull_ref[pl.ds(pl.multiple_of(v_i * rows, rows), rows), :], axis=0, keepdims=True)
    for t in range(tiles):
        part = own_ref[v_i * nm + m_i, :, t * 128 : (t + 1) * 128].astype(f32) * pulls
        second_ref[t : t + 1, :] = (
            jnp.sum(part, axis=0, keepdims=True) + pulled * all_ref[m_i, 0, t : t + 1, :]
        )

    by_e = jnp.broadcast_to(weight * inv_e, (group, 128))
    by_b = jnp.broadcast_to(weight * inv_b, (group, 128))
    for m in range(nm):
        for t in range(tiles):
            d = m * feat + t * 128
            plus = outer_ref[:group, d : d + 128] * by_e
            less = outer_ref[group : 2 * group, d : d + 128] * by_b
            row = jnp.sum(plus - less, axis=0, keepdims=True)
            row -= jnp.sum(outer_ref[2 * group :, d : d + 128], axis=0, keepdims=True)
            row = row * all_ref[m, 1, t : t + 1, :] - jnp.where(
                m_i == m, second_ref[t : t + 1, :], 0.0
            )
            vec_ref[m, t : t + 1, :] = row
    own = [
        coeff_ref[pl.ds(pl.multiple_of((k * nv + v_i) * rows, rows), rows), :] for k in range(2)
    ]
    for k in range(nm):
        m = lax.rem(m_i - k + nm, nm)
        for t in range(units[0].shape[1] // 128):
            c = t * 128
            row = units[2 * k][:, c : c + 128].astype(f32) * own[0]
            row += units[2 * k + 1][:, c : c + 128].astype(f32) * own[1]
            vec_ref[m, pl.ds(tiles + t, 1), :] = jnp.sum(row, axis=0, keepdims=True)
    for m in range(nm):
        block = vec_ref[m].astype(bf16)
        for v in range(nv):
            for r in range(2):
                slab_ref[(v * nm + m) * 2 + r] = block
    put_slab = pltpu.make_async_copy(slab_ref, slab_hbm, sems.at[1])
    put_slab.start()

    put_pen.wait()
    put_slab.wait()


def sum_kernel(back_ref, in_ref, out_ref):
    peers = back_ref.shape[0]
    tiles = out_ref.shape[0]
    units = back_ref.shape[1] - tiles
    pieces = in_ref.shape[0] // units
    wide = jnp.zeros((tiles, 128), f32)
    for q in range(pieces):
        total = back_ref[q].astype(f32)
        for p in range(q + pieces, peers, pieces):
            total += back_ref[p].astype(f32)
        wide += total[:tiles]
        in_ref[q * units : (q + 1) * units, :] = total[tiles:]
    out_ref[...] = wide


def in_hbm(value):
    return pltpu.with_memory_space_constraint(value, pltpu.HBM)


def call(kernel, out_shape, scratch=(), megabytes=6, **more):
    return pl.pallas_call(
        kernel,
        out_shape=out_shape,
        scratch_shapes=scratch,
        compiler_params=pltpu.CompilerParams(vmem_limit_bytes=megabytes << 20),
        **more,
    )


def fused(nv, nm, nr, resid_base, mlp_hidden, edit_in, edit_out, norm_gain, head, token_ids):
    rows, feat = resid_base.shape
    hidden = mlp_hidden.shape[1]
    model, voc = head.shape
    group = nv * nr * rows
    peers = nv * nm * nr
    quarter = hidden // (nm * nr)
    everyone = ("vocab", "mp", "rep")
    m_i = lax.axis_index("mp")
    r_i = lax.axis_index("rep")
    shape = jax.ShapeDtypeStruct

    tiles = feat // 128
    hbm = pl.BlockSpec(memory_space=pltpu.HBM)
    vmem = pl.BlockSpec(memory_space=pltpu.VMEM)
    out_tiles = edit_out.reshape(tiles, 128)
    gain_tiles = norm_gain.reshape(tiles, 128)

    packed, vectors, *units = call(
        functools.partial(send_kernel, nv * nm, nm),
        (
            pltpu.HBM((nv * nm, rows, feat + 128), bf16),
            shape((2, tiles, 128), f32),
        )
        + (shape((rows, quarter), bf16),) * (2 * nm),
        [
            pltpu.VMEM((rows, feat), bf16),
            pltpu.VMEM((rows, hidden), bf16),
            pltpu.VMEM((1, hidden), f32),
            pltpu.VMEM((nv * nm, rows, feat + 128), bf16),
            pltpu.SemaphoreType.DMA((6,)),
        ],
        in_specs=[hbm] * 5,
        out_specs=(hbm,) + (vmem,) * (1 + 2 * nm),
    )(
        *(
            in_hbm(a)
            for a in (resid_base, mlp_hidden, edit_in.reshape(1, hidden), out_tiles, gain_tiles)
        )
    )
    got = lax.all_to_all(packed, ("vocab", "mp"), 0, 0)
    other = lax.ppermute(got, "rep", [(0, 1), (1, 0)])
    vectors = from_peers(vectors, "mp", nm)
    vectors = jnp.stack(in_order(vectors, m_i))
    half = group // 2
    staged, early, early_cols = call(
        functools.partial(early_kernel, nv, nm),
        (
            pltpu.VMEM((model, voc), bf16),
            shape((group + 16, voc), f32),
            shape((half, 128), f32),
        ),
        [pltpu.VMEM((group + 16, model), bf16), pltpu.SemaphoreType.DMA((6,))],
        8,
        in_specs=[vmem, vmem, hbm],
        out_specs=(vmem, vmem, vmem),
    )(got, vectors, in_hbm(head))
    ids = token_ids.reshape(nv, nr, rows)
    ids = jnp.concatenate(
        [lax.dynamic_index_in_dim(ids, (r_i + k) % nr, 1, keepdims=False) for k in range(nr)]
    ).reshape(group, 1)

    for i in range(nm):
        for j in range(2):
            if i or j:
                moves = [
                    (2 * m + r, 2 * ((m + i) % nm) + (r + j) % 2)
                    for m in range(nm)
                    for r in range(2)
                ]
                units[2 * i + j] = lax.ppermute(units[2 * i + j], ("mp", "rep"), moves)

    slab, cols, ops = call(
        functools.partial(score_kernel, nv, nm),
        (
            pltpu.HBM((peers, 8, 128), f32),
            shape((group, 128), f32),
            pltpu.HBM((4 * group + 16, voc), bf16),
        ),
        [
            pltpu.VMEM((group, model), bf16),
            pltpu.VMEM((peers, 8, 128), f32),
            pltpu.VMEM((4 * group + 16, voc), bf16),
            pltpu.SemaphoreType.DMA((2,)),
        ],
        in_specs=[vmem] * 6,
        out_specs=(hbm, vmem, hbm),
    )(other, vectors, ids, staged, early, early_cols)
    theirs = lax.all_to_all(slab, everyone, 0, 0)
    outer = call(
        outer_kernel,
        shape((2 * group + 16, model), f32),
        [
            pltpu.VMEM((4 * group + 16, voc), bf16),
            pltpu.VMEM((model, voc), bf16),
            pltpu.SemaphoreType.DMA((1 + model // 512,)),
        ],
        12,
        in_specs=[hbm, hbm],
    )(in_hbm(ops), in_hbm(head))

    width = (feat + quarter) // 128
    slab, penalty = call(
        functools.partial(close_kernel, nv, nm),
        (pltpu.HBM((peers, width, 128), bf16), pltpu.HBM((rows, 128), f32)),
        [
            pltpu.VMEM((group, 128), f32),
            pltpu.VMEM((group, 128), f32),
            pltpu.VMEM((group, 128), f32),
            pltpu.VMEM((nm, width, 128), f32),
            pltpu.VMEM((peers, width, 128), bf16),
            pltpu.VMEM((tiles, 128), f32),
            pltpu.SemaphoreType.DMA((2,)),
        ],
        in_specs=[vmem] * (5 + 2 * nm),
        out_specs=(hbm, hbm),
    )(theirs, cols, outer, got, vectors, *units)
    back = lax.all_to_all(slab, everyone, 0, 0)
    grad_in, grad_out = call(
        sum_kernel, (shape((hidden // 128, 128), f32), shape((tiles, 128), f32))
    )(back)
    return (penalty[:, 0], grad_in.reshape(hidden), grad_out.reshape(feat))


def local(nv, nm, nr, resid_base, mlp_hidden, *rest):
    rows, feat = resid_base.shape
    quarter = mlp_hidden.shape[1] // (nm * nr)
    whole_tiles = rows == 8 and feat % 128 == 0 and quarter % 128 == 0
    small = nr == 2 and nv % 2 == 0 and nv * nr * rows == 64
    step = fused if whole_tiles and small else plain
    return step(nv, nm, nr, resid_base, mlp_hidden, *rest)


def solution(mesh):
    in_specs = (
        P(("parts", "vocab", "rep"), "mp"),
        P(("parts", "vocab", "rep"), "mp"),
        P(("parts", "mp")),
        P(("parts", "mp")),
        P("mp"),
        P(None, ("vocab", "mp", "rep")),
        P("parts"),
    )
    out_specs = (P(("parts", "vocab", "rep")), P(("parts", "mp")), P(("parts", "mp")))
    step = functools.partial(local, mesh.shape["vocab"], mesh.shape["mp"], mesh.shape["rep"])
    return jax.shard_map(step, mesh=mesh, in_specs=in_specs, out_specs=out_specs, check_vma=False)
```

```python
import functools

import jax
import jax.numpy as jnp
from jax import lax
from jax.experimental import pallas as pl
from jax.experimental.pallas import tpu as pltpu
from jax.sharding import PartitionSpec as P

softcap = 30.0
epsilon = 1e-06
bf16 = jnp.bfloat16
f32 = jnp.float32


def split_bf16(value, pieces):
    out = []
    for _ in range(pieces):
        part = lax.reduce_precision(value, 8, 7)
        out.append(part.astype(bf16))
        value = value - part
    return out


def from_peers(value, axis, size):
    moves = [[(i, (i + k) % size) for i in range(size)] for k in range(size)]
    return [value] + [lax.ppermute(value, axis, moves[k]) for k in range(1, size)]


def to_peers(pick, axis, size, index):
    moves = [[(i, (i + k) % size) for i in range(size)] for k in range(size)]
    return [pick(index)] + [
        lax.ppermute(pick((index + k) % size), axis, moves[k]) for k in range(1, size)
    ]


def in_order(values, index):
    size = len(values)
    ordered = []
    for j in range(size):
        value = values[0]
        for k in range(1, size):
            value = jnp.where((index - j) % size == k, values[k], value)
        ordered.append(value)
    return ordered


def plain(nv, nm, nr, resid_base, mlp_hidden, edit_in, edit_out, norm_gain, head, token_ids):
    rows, feat = resid_base.shape
    hidden = mlp_hidden.shape[1]
    model, voc = head.shape
    group = nv * nr * rows
    peers = nv * nm * nr
    quarter = hidden // (nm * nr)
    everyone = ("vocab", "mp", "rep")

    v_i = lax.axis_index("vocab")
    m_i = lax.axis_index("mp")
    r_i = lax.axis_index("rep")

    vectors = from_peers(jnp.stack([edit_out, norm_gain]), "mp", nm)
    vectors = jnp.concatenate(in_order(vectors, m_i), axis=1)
    out_all = vectors[0]
    gain_all = vectors[1]

    units = mlp_hidden.reshape(rows, nm, nr, quarter)
    units = jnp.concatenate(
        [
            part
            for part in to_peers(
                lambda r: lax.dynamic_index_in_dim(units, r, 2, keepdims=False), "rep", nr, r_i
            )
        ]
    )
    units = to_peers(
        lambda m: lax.dynamic_index_in_dim(units, m, 1, keepdims=False), "mp", nm, m_i
    )

    hidden_f = mlp_hidden.astype(f32)
    mix_part = jnp.sum(hidden_f * edit_in[None, :], axis=1)
    mix_cols = jnp.stack(split_bf16(mix_part, 3), axis=1)
    packed = jnp.concatenate([resid_base, jnp.pad(mix_cols, ((0, 0), (0, 125)))], axis=1)
    packed = jnp.broadcast_to(packed[None], (nv * nm, rows, feat + 128))
    got = lax.all_to_all(packed, ("vocab", "mp"), 0, 0)
    got = jnp.concatenate(in_order(from_peers(got, "rep", nr), r_i)).reshape(nr * nv, nm, rows, feat + 128)

    base = jnp.concatenate([got[:, m, :, :feat].reshape(group, feat) for m in range(nm)], axis=1)
    base_f = base.astype(f32)
    mix = jnp.sum(got[:, :, :, feat : feat + 3].astype(f32), axis=(1, 3)).reshape(group)
    resid = base_f + mix[:, None] * out_all[None, :]
    edit_scale = lax.rsqrt(jnp.mean(resid * resid, axis=1) + epsilon)
    base_scale = lax.rsqrt(jnp.mean(base_f * base_f, axis=1) + epsilon)
    along = jnp.sum(resid * out_all[None, :], axis=1)
    x_edit = (resid * edit_scale[:, None] * gain_all[None, :]).astype(bf16)
    x_base = (base_f * base_scale[:, None] * gain_all[None, :]).astype(bf16)
    direction = jnp.stack(split_bf16(out_all * gain_all, 3) + [jnp.zeros((model,), bf16)] * 5)
    pre = jnp.dot(
        jnp.concatenate([x_edit, x_base, direction]), head, preferred_element_type=f32
    )
    pre_edit = pre[:group]
    pre_base = pre[group : 2 * group]
    toward = jnp.sum(pre[2 * group :], axis=0)
    z_edit = softcap * jnp.tanh(pre_edit / softcap)
    z_base = softcap * jnp.tanh(pre_base / softcap)
    slope = 1.0 - (z_edit / softcap) ** 2
    exp_edit = jnp.exp(z_edit)
    exp_base = jnp.exp(z_base)
    ids = token_ids.reshape(nv, nr, rows).transpose(1, 0, 2).reshape(group)
    first_col = lax.axis_index(everyone) * voc
    onehot = (ids[:, None] == (first_col + jnp.arange(voc, dtype=jnp.int32))[None, :]).astype(f32)
    diff = z_base - z_edit
    pe = exp_edit * slope
    pb = exp_base * slope
    po = onehot * slope
    sums = jnp.stack(
        [
            jnp.sum(a, axis=1)
            for a in (
                exp_edit,
                exp_base,
                exp_base * diff,
                onehot * diff,
                pe * pre_edit,
                pb * pre_edit,
                po * pre_edit,
                pe * toward[None, :],
                pb * toward[None, :],
                po * toward[None, :],
            )
        ]
    )
    weight = mix * edit_scale
    wo = jnp.sum(weight[:, None] * po, axis=0)
    high_e, low_e = split_bf16(pe, 2)
    high_b, low_b = split_bf16(pb, 2)
    tail = jnp.stack(split_bf16(wo, 3) + [jnp.zeros((voc,), bf16)] * 5)
    outer = lax.dot_general(
        jnp.concatenate([high_e, high_b, low_e, low_b, tail]),
        head,
        (((1,), (1,)), ((), ())),
        preferred_element_type=f32,
    )
    rows_e = outer[:group] + outer[2 * group : 3 * group]
    rows_b = outer[group : 2 * group] + outer[3 * group : 4 * group]
    row_o = jnp.sum(outer[4 * group :], axis=0)
    flat = 10 * group
    padded = -(-flat // 1024) * 1024
    mine = jnp.pad(sums.reshape(flat), (0, padded - flat)).reshape(padded // 128, 128)
    theirs = lax.all_to_all(
        jnp.broadcast_to(mine[None], (peers, padded // 128, 128)), everyone, 0, 0
    )
    sums = jnp.sum(theirs, axis=0).reshape(padded)[:flat].reshape(10, group)
    se, sb, kl, gap, ae, ab, ao, te, tb, to = [sums[i] for i in range(10)]
    inv_e = 2.0 / se
    inv_b = 1.0 / sb
    align = ae * inv_e - ab * inv_b - ao
    proj = te * inv_e - tb * inv_b - to
    penalty = kl * inv_b + gap + 2.0 * (jnp.log(se) - jnp.log(sb))
    shrink = edit_scale * align / model
    coeff = edit_scale * proj - shrink * (edit_scale * along)
    weighted = jnp.sum((weight * inv_e)[:, None] * rows_e, axis=0) - jnp.sum((weight * inv_b)[:, None] * rows_b, axis=0) - row_o
    w_hi, w_lo = split_bf16(weighted, 2)
    mine = lax.dynamic_index_in_dim(coeff.reshape(nr, nv, rows), v_i, 1, keepdims=False)
    own = jnp.concatenate([lax.dynamic_index_in_dim(mine, (r_i - k) % nr, 0, keepdims=False) for k in range(nr)])
    part_in = [jnp.sum(u.astype(f32) * own[:, None], axis=0) for u in units]
    part_in = jnp.stack(in_order(part_in, m_i)).astype(bf16)
    slab = jnp.concatenate([w_hi.reshape(nm, feat), w_lo.reshape(nm, feat), part_in], axis=1)
    width = 2 * feat + quarter
    if width % 128 == 0:
        slab = slab.reshape(nm, width // 128, 128)
    slab = jnp.broadcast_to(slab[None, :, None], (nv, nm, nr) + slab.shape[1:])
    back = lax.all_to_all(slab.reshape((peers,) + slab.shape[3:]), everyone, 0, 0)
    back = back.reshape(nv, nm * nr, width).astype(f32)
    grad_in = jnp.sum(back[:, :, 2 * feat :], axis=0).reshape(hidden)
    weighted_own = jnp.sum(back[:, :, :feat] + back[:, :, feat : 2 * feat], axis=(0, 1))
    pull = mix * shrink * edit_scale
    base_own = lax.dynamic_slice_in_dim(base, m_i * feat, feat, 1).astype(f32)
    second = jnp.sum(pull[:, None] * base_own, axis=0) + jnp.sum(pull * mix) * edit_out
    grad_out = norm_gain * weighted_own - second
    penalty = lax.dynamic_slice(penalty.reshape(nr, nv, rows), (r_i, v_i, 0), (1, 1, rows))
    return (penalty.reshape(rows), grad_in, grad_out)


def send_kernel(copies, pieces, base_hbm, hidden_hbm, in_hbm, out_hbm, gain_hbm, packed_hbm, vec_ref, *refs):
    unit_refs = refs[: 2 * pieces]
    base_ref, hidden_ref, in_ref, packed_ref, mix_ref, sems = refs[2 * pieces :]
    rows, hidden = hidden_ref.shape
    feat = base_ref.shape[1]
    quarter = hidden // (2 * pieces)
    get_hidden = pltpu.make_async_copy(hidden_hbm, hidden_ref, sems.at[0])
    get_in = pltpu.make_async_copy(in_hbm, in_ref, sems.at[1])
    get_base = pltpu.make_async_copy(base_hbm, base_ref, sems.at[2])
    later = [
        pltpu.make_async_copy(out_hbm, vec_ref.at[0], sems.at[3]),
        pltpu.make_async_copy(gain_hbm, vec_ref.at[1], sems.at[4]),
    ]
    m_i = lax.axis_index("mp")
    r_i = lax.axis_index("rep")
    for i in range(pieces):
        for j in range(2):
            to = 2 * lax.rem(m_i + i, pieces) + lax.rem(r_i + j, 2)
            start = pl.multiple_of(to * quarter, 128)
            k = 2 * i + j
            later.append(
                pltpu.make_async_copy(
                    hidden_hbm.at[:, pl.ds(start, quarter)], unit_refs[k], sems.at[7 + k]
                )
            )
    get_base.start()
    get_hidden.start()
    get_in.start()
    for move in later:
        move.start()
    get_base.wait()
    for i in range(copies):
        packed_ref[i] = base_ref[...]
    put_base = pltpu.make_async_copy(packed_ref, packed_hbm.at[:, :, pl.ds(0, feat)], sems.at[5])
    put_base.start()
    get_hidden.wait()
    get_in.wait()
    total = jnp.zeros((rows, 128), f32)
    for c in range(0, hidden, 128):
        total += hidden_ref[:, c : c + 128].astype(f32) * in_ref[:, c : c + 128]
    mix = jnp.sum(total, axis=1, keepdims=True)
    lane = lax.broadcasted_iota(jnp.int32, (rows, 128), 1)
    cols = jnp.zeros((rows, 128), f32)
    for i in range(3):
        piece = mix.astype(bf16).astype(f32)
        cols = jnp.where(lane == i, piece, cols)
        mix = mix - piece
    cols = cols.astype(bf16)
    for i in range(copies):
        mix_ref[i] = cols
    put_mix = pltpu.make_async_copy(mix_ref, packed_hbm.at[:, :, pl.ds(feat, 128)], sems.at[6])
    put_mix.start()
    for move in later:
        move.wait()
    put_base.wait()
    put_mix.wait()


def normed_rows(nv, nm, got_ref, vec_ref, cols_ref, x_ref):
    rows = got_ref.shape[1]
    feat = got_ref.shape[2] - 128
    model = nm * feat
    half = nv * rows
    pair = 2 * rows
    lane = lax.broadcasted_iota(jnp.int32, (pair, 128), 1)
    for v in range(0, nv, 2):
        at = v * rows

        def tile(m, c):
            first = got_ref[v * nm + m, :, c : c + 128].astype(f32)
            second = got_ref[(v + 1) * nm + m, :, c : c + 128].astype(f32)
            return jnp.concatenate([first, second], axis=0)

        mixed = tile(0, feat)
        for m in range(1, nm):
            mixed += tile(m, feat)
        mix = jnp.sum(mixed, axis=1, keepdims=True)
        mix_b = jnp.broadcast_to(mix, (pair, 128))
        sq_b = jnp.zeros((pair, 128), f32)
        sq_e = jnp.zeros((pair, 128), f32)
        dot_o = jnp.zeros((pair, 128), f32)
        for m in range(nm):
            for c in range(0, feat, 128):
                out = vec_ref[m, 0, c // 128 : c // 128 + 1, :]
                b = tile(m, c)
                e = b + mix_b * out
                sq_b += b * b
                sq_e += e * e
                dot_o += e * out
        scale_e = lax.rsqrt(jnp.sum(sq_e, axis=1, keepdims=True) / model + epsilon)
        scale_b = lax.rsqrt(jnp.sum(sq_b, axis=1, keepdims=True) / model + epsilon)
        along = jnp.sum(dot_o, axis=1, keepdims=True)
        cols_ref[at : at + pair, :] = jnp.where(
            lane == 0, mix, jnp.where(lane == 1, scale_e, jnp.where(lane == 2, along, 0.0))
        )
        scale_e = jnp.broadcast_to(scale_e, (pair, 128))
        scale_b = jnp.broadcast_to(scale_b, (pair, 128))
        for m in range(nm):
            for c in range(0, feat, 128):
                d = m * feat + c
                t = c // 128
                out = vec_ref[m, 0, t : t + 1, :]
                gain = vec_ref[m, 1, t : t + 1, :]
                b = tile(m, c)
                e = b + mix_b * out
                x_ref[at : at + pair, d : d + 128] = (e * scale_e * gain).astype(bf16)
                x_ref[half + at : half + at + pair, d : d + 128] = (b * scale_b * gain).astype(bf16)


def early_kernel(nv, nm, own_ref, vec_ref, head_hbm, head_ref, pre_ref, cols_ref, x_ref, sems):
    model = head_hbm.shape[0]
    part = model // sems.shape[0]
    moves = []
    for i in range(sems.shape[0]):
        span = pl.ds(i * part, part)
        moves.append(pltpu.make_async_copy(head_hbm.at[span], head_ref.at[span], sems.at[i]))
    for move in moves:
        move.start()
    feat = own_ref.shape[2] - 128
    half = cols_ref.shape[0]
    normed_rows(nv, nm, own_ref, vec_ref, cols_ref, x_ref)
    sub = lax.broadcasted_iota(jnp.int32, (16, 128), 0)
    for d in range(0, model, 128):
        m, t = d // feat, d % feat // 128
        rest = vec_ref[m, 0, t : t + 1, :] * vec_ref[m, 1, t : t + 1, :]
        block = jnp.zeros((16, 128), f32)
        for i in range(3):
            piece = rest.astype(bf16).astype(f32)
            block = jnp.where(sub == i, piece, block)
            rest = rest - piece
        x_ref[2 * half :, d : d + 128] = block.astype(bf16)
    pre = None
    for i, move in enumerate(moves):
        move.wait()
        span = slice(i * part, (i + 1) * part)
        block = jnp.dot(x_ref[:, span], head_ref[span, :], preferred_element_type=f32)
        pre = block if pre is None else pre + block
    pre_ref[...] = pre


def score_kernel(nv, nm, other_ref, vec_ref, ids_ref, head_ref, early_ref, early_cols_ref, slab_hbm, cols_ref, ops_hbm, x_ref, slab_ref, ops_ref, sems):
    voc = head_ref.shape[1]
    half = early_cols_ref.shape[0]
    group = 2 * half
    cols_ref[:half] = early_cols_ref[...]
    normed_rows(nv, nm, other_ref, vec_ref, cols_ref.at[half:], x_ref)
    late = jnp.dot(x_ref[...], head_ref[...], preferred_element_type=f32)
    pre_edit = jnp.concatenate([early_ref[:half], late[:half]], axis=0)
    pre_base = jnp.concatenate([early_ref[half:group], late[half:]], axis=0)
    toward = jnp.sum(early_ref[group:], axis=0, keepdims=True)
    th = jnp.tanh(pre_edit / softcap)
    z_edit = softcap * th
    z_base = softcap * jnp.tanh(pre_base / softcap)
    slope = 1.0 - th * th
    exp_edit = jnp.exp(z_edit)
    exp_base = jnp.exp(z_base)
    first_col = lax.axis_index(("vocab", "mp", "rep")) * voc
    column = lax.broadcasted_iota(jnp.int32, (group, voc), 1) + first_col
    hit = column == ids_ref[...]
    diff = z_base - z_edit
    pe = exp_edit * slope
    pb = exp_base * slope
    po = jnp.where(hit, slope, 0.0)

    high_e = pe.astype(bf16)
    high_b = pb.astype(bf16)
    ops_ref[:group] = high_e
    ops_ref[group : 2 * group] = high_b
    ops_ref[2 * group : 3 * group] = (pe - high_e.astype(f32)).astype(bf16)
    ops_ref[3 * group : 4 * group] = (pb - high_b.astype(f32)).astype(bf16)
    weight = cols_ref[:, 0:1] * cols_ref[:, 1:2]
    rest = jnp.sum(weight * po, axis=0, keepdims=True)
    sub = lax.broadcasted_iota(jnp.int32, (16, voc), 0)
    block = jnp.zeros((16, voc), f32)
    for i in range(3):
        piece = rest.astype(bf16).astype(f32)
        block = jnp.where(sub == i, piece, block)
        rest = rest - piece
    ops_ref[4 * group :] = block.astype(bf16)
    put_ops = pltpu.make_async_copy(ops_ref, ops_hbm, sems.at[1])
    put_ops.start()

    def total(a):
        return jnp.sum(a, axis=1, keepdims=True)

    sums = [
        total(exp_edit),
        total(exp_base),
        total(exp_base * diff),
        total(jnp.where(hit, diff, 0.0)),
        total(pe * pre_edit),
        total(pb * pre_edit),
        total(po * pre_edit),
        total(pe * toward),
        total(pb * toward),
        total(po * toward),
    ]
    lane = lax.broadcasted_iota(jnp.int32, (group, 128), 1)
    first = jnp.zeros((group, 128), f32)
    second = jnp.zeros((group, 128), f32)
    for i in range(8):
        first = jnp.where(lane == i, sums[i], first)
    for i in range(8, 10):
        second = jnp.where(lane == i - 8, sums[i], second)
    straight = jnp.concatenate([first, second], axis=0)
    swapped = jnp.concatenate([first[half:], first[:half], second[half:], second[:half]], axis=0)
    table = jnp.where(lax.axis_index("rep") == 0, straight, swapped)
    table = table.T[:8]
    for p in range(slab_ref.shape[0]):
        slab_ref[p] = table
    put_slab = pltpu.make_async_copy(slab_ref, slab_hbm, sems.at[0])
    put_slab.start()

    put_slab.wait()
    put_ops.wait()


def outer_kernel(ops_hbm, head_hbm, outer_ref, ops_ref, head_ref, sems):
    both = outer_ref.shape[0] - 16
    part = head_hbm.shape[0] // (sems.shape[0] - 1)
    get = pltpu.make_async_copy(ops_hbm, ops_ref, sems.at[0])
    get.start()
    moves = []
    for i in range(head_hbm.shape[0] // part):
        span = pl.ds(i * part, part)
        moves.append(pltpu.make_async_copy(head_hbm.at[span], head_ref.at[span], sems.at[1 + i]))
    for move in moves:
        move.start()
    get.wait()
    for i, move in enumerate(moves):
        move.wait()
        c = i * part
        block = lax.dot_general(
            ops_ref[...],
            head_ref[c : c + part, :],
            (((1,), (1,)), ((), ())),
            preferred_element_type=f32,
        )
        outer_ref[:both, c : c + part] = block[:both] + block[both : 2 * both]
        outer_ref[both:, c : c + part] = block[2 * both :]


def close_kernel(nv, nm, theirs_ref, cols_ref, outer_ref, own_ref, all_ref, *refs):
    units = refs[: 2 * nm]
    slab_hbm, penalty_hbm, coeff_ref, pen_ref, pull_ref, vec_ref, slab_ref, second_ref, sems = refs[2 * nm :]
    rows = own_ref.shape[1]
    feat = own_ref.shape[2] - 128
    model = outer_ref.shape[1]
    group = 2 * nv * rows
    half = group // 2
    tiles = feat // 128
    v_i = lax.axis_index("vocab")
    m_i = lax.axis_index("mp")
    r_i = lax.axis_index("rep")

    table = theirs_ref[0]
    for p in range(1, theirs_ref.shape[0]):
        table += theirs_ref[p]
    table = jnp.concatenate([table, jnp.zeros((120, 128), f32)], axis=0).T
    first = table[:group]
    second = table[group:]
    swap_first = jnp.concatenate([first[half:], first[:half]], axis=0)
    swap_second = jnp.concatenate([second[half:], second[:half]], axis=0)
    first = jnp.where(r_i == 0, first, swap_first)
    second = jnp.where(r_i == 0, second, swap_second)
    se, sb, kl, gap, ae, ab, ao, te = [first[:, i : i + 1] for i in range(8)]
    tb, to = second[:, 0:1], second[:, 1:2]
    mix = cols_ref[:, 0:1]
    scale = cols_ref[:, 1:2]
    along = cols_ref[:, 2:3]
    inv_e = 2.0 / se
    inv_b = 1.0 / sb
    align = ae * inv_e - ab * inv_b - ao
    proj = te * inv_e - tb * inv_b - to
    penalty = kl * inv_b + gap + 2.0 * (jnp.log(se) - jnp.log(sb))
    shrink = scale * align / model
    coeff = scale * proj - shrink * (scale * along)
    weight = mix * scale
    pull = weight * shrink
    coeff_ref[...] = jnp.broadcast_to(coeff, (group, 128))
    pen_ref[...] = jnp.broadcast_to(penalty, (group, 128))
    put_pen = pltpu.make_async_copy(
        pen_ref.at[pl.ds(pl.multiple_of(v_i * rows, rows), rows)], penalty_hbm, sems.at[0]
    )
    put_pen.start()

    pull_ref[...] = jnp.broadcast_to(pull, (group, 128))
    pulls = pull_ref[pl.ds(pl.multiple_of(v_i * rows, rows), rows), :]
    pull_ref[...] = jnp.broadcast_to(pull * mix, (group, 128))
    pulled = jnp.sum(pull_ref[pl.ds(pl.multiple_of(v_i * rows, rows), rows), :], axis=0, keepdims=True)
    for t in range(tiles):
        part = own_ref[v_i * nm + m_i, :, t * 128 : (t + 1) * 128].astype(f32) * pulls
        second_ref[t : t + 1, :] = (
            jnp.sum(part, axis=0, keepdims=True) + pulled * all_ref[m_i, 0, t : t + 1, :]
        )

    own = [
        coeff_ref[pl.ds(pl.multiple_of((k * nv + v_i) * rows, rows), rows), :] for k in range(2)
    ]
    for k in range(nm):
        m = lax.rem(m_i - k + nm, nm)
        for t in range(units[0].shape[1] // 128):
            c = t * 128
            row = units[2 * k][:, c : c + 128].astype(f32) * own[0]
            row += units[2 * k + 1][:, c : c + 128].astype(f32) * own[1]
            vec_ref[m, pl.ds(tiles + t, 1), :] = jnp.sum(row, axis=0, keepdims=True)
    by_e = jnp.broadcast_to(weight * inv_e, (group, 128))
    by_b = jnp.broadcast_to(weight * inv_b, (group, 128))
    puts = []
    for m in range(nm):
        for t in range(tiles):
            d = m * feat + t * 128
            plus = outer_ref[:group, d : d + 128] * by_e
            less = outer_ref[group : 2 * group, d : d + 128] * by_b
            row = jnp.sum(plus - less, axis=0, keepdims=True)
            row -= jnp.sum(outer_ref[2 * group :, d : d + 128], axis=0, keepdims=True)
            row = row * all_ref[m, 1, t : t + 1, :] - jnp.where(
                m_i == m, second_ref[t : t + 1, :], 0.0
            )
            vec_ref[m, t : t + 1, :] = row
        block = vec_ref[m].astype(bf16)
        for v in range(nv):
            for r in range(2):
                slab_ref[m, 2 * v + r] = block
        for v in range(nv):
            put = pltpu.make_async_copy(
                slab_ref.at[m, pl.ds(2 * v, 2)],
                slab_hbm.at[pl.ds((v * nm + m) * 2, 2)],
                sems.at[1 + v * nm + m],
            )
            put.start()
            puts.append(put)
    put_pen.wait()
    for put in puts:
        put.wait()


def sum_kernel(back_ref, in_ref, out_ref):
    peers = back_ref.shape[0]
    tiles = out_ref.shape[0]
    units = back_ref.shape[1] - tiles
    pieces = in_ref.shape[0] // units
    wide = jnp.zeros((tiles, 128), f32)
    for q in range(pieces):
        total = back_ref[q].astype(f32)
        for p in range(q + pieces, peers, pieces):
            total += back_ref[p].astype(f32)
        wide += total[:tiles]
        in_ref[q * units : (q + 1) * units, :] = total[tiles:]
    out_ref[...] = wide


def in_hbm(value):
    return pltpu.with_memory_space_constraint(value, pltpu.HBM)


def call(kernel, out_shape, scratch=(), megabytes=6, **more):
    return pl.pallas_call(
        kernel,
        out_shape=out_shape,
        scratch_shapes=scratch,
        compiler_params=pltpu.CompilerParams(vmem_limit_bytes=megabytes << 20),
        **more,
    )


def fused(nv, nm, nr, resid_base, mlp_hidden, edit_in, edit_out, norm_gain, head, token_ids):
    rows, feat = resid_base.shape
    hidden = mlp_hidden.shape[1]
    model, voc = head.shape
    group = nv * nr * rows
    peers = nv * nm * nr
    quarter = hidden // (nm * nr)
    everyone = ("vocab", "mp", "rep")
    m_i = lax.axis_index("mp")
    r_i = lax.axis_index("rep")
    shape = jax.ShapeDtypeStruct

    tiles = feat // 128
    hbm = pl.BlockSpec(memory_space=pltpu.HBM)
    vmem = pl.BlockSpec(memory_space=pltpu.VMEM)
    out_tiles = edit_out.reshape(tiles, 128)
    gain_tiles = norm_gain.reshape(tiles, 128)

    packed, vectors, *units = call(
        functools.partial(send_kernel, nv * nm, nm),
        (
            pltpu.HBM((nv * nm, rows, feat + 128), bf16),
            shape((2, tiles, 128), f32),
        )
        + (shape((rows, quarter), bf16),) * (2 * nm),
        [
            pltpu.VMEM((rows, feat), bf16),
            pltpu.VMEM((rows, hidden), bf16),
            pltpu.VMEM((1, hidden), f32),
            pltpu.VMEM((nv * nm, rows, feat), bf16),
            pltpu.VMEM((nv * nm, rows, 128), bf16),
            pltpu.SemaphoreType.DMA((7 + 2 * nm,)),
        ],
        in_specs=[hbm] * 5,
        out_specs=(hbm,) + (vmem,) * (1 + 2 * nm),
    )(
        *(
            in_hbm(a)
            for a in (resid_base, mlp_hidden, edit_in.reshape(1, hidden), out_tiles, gain_tiles)
        )
    )
    got = lax.all_to_all(packed, ("vocab", "mp"), 0, 0)
    other = lax.ppermute(got, "rep", [(0, 1), (1, 0)])
    for i in range(nm):
        for j in range(2):
            if i or j:
                moves = [
                    (2 * m + r, 2 * ((m + i) % nm) + (r + j) % 2)
                    for m in range(nm)
                    for r in range(2)
                ]
                units[2 * i + j] = lax.ppermute(units[2 * i + j], ("mp", "rep"), moves)
    vectors = from_peers(vectors, "mp", nm)
    vectors, units = lax.optimization_barrier((vectors, units))
    vectors = jnp.stack(in_order(vectors, m_i))
    half = group // 2
    staged, early, early_cols = call(
        functools.partial(early_kernel, nv, nm),
        (
            pltpu.VMEM((model, voc), bf16),
            shape((group + 16, voc), f32),
            shape((half, 128), f32),
        ),
        [pltpu.VMEM((group + 16, model), bf16), pltpu.SemaphoreType.DMA((6,))],
        8,
        in_specs=[vmem, vmem, hbm],
        out_specs=(vmem, vmem, vmem),
    )(got, vectors, in_hbm(head))
    ids = token_ids.reshape(nv, nr, rows)
    ids = jnp.concatenate(
        [lax.dynamic_index_in_dim(ids, (r_i + k) % nr, 1, keepdims=False) for k in range(nr)]
    ).reshape(group, 1)

    slab, cols, ops = call(
        functools.partial(score_kernel, nv, nm),
        (
            pltpu.HBM((peers, 8, 128), f32),
            shape((group, 128), f32),
            pltpu.HBM((4 * group + 16, voc), bf16),
        ),
        [
            pltpu.VMEM((group, model), bf16),
            pltpu.VMEM((peers, 8, 128), f32),
            pltpu.VMEM((4 * group + 16, voc), bf16),
            pltpu.SemaphoreType.DMA((2,)),
        ],
        in_specs=[vmem] * 6,
        out_specs=(hbm, vmem, hbm),
    )(other, vectors, ids, staged, early, early_cols)
    theirs = lax.all_to_all(slab, everyone, 0, 0)
    outer = call(
        outer_kernel,
        shape((2 * group + 16, model), f32),
        [
            pltpu.VMEM((4 * group + 16, voc), bf16),
            pltpu.VMEM((model, voc), bf16),
            pltpu.SemaphoreType.DMA((4,)),
        ],
        12,
        in_specs=[hbm, hbm],
    )(in_hbm(ops), in_hbm(head))

    width = (feat + quarter) // 128
    slab, penalty = call(
        functools.partial(close_kernel, nv, nm),
        (pltpu.HBM((peers, width, 128), bf16), pltpu.HBM((rows, 128), f32)),
        [
            pltpu.VMEM((group, 128), f32),
            pltpu.VMEM((group, 128), f32),
            pltpu.VMEM((group, 128), f32),
            pltpu.VMEM((nm, width, 128), f32),
            pltpu.VMEM((nm, 2 * nv, width, 128), bf16),
            pltpu.VMEM((tiles, 128), f32),
            pltpu.SemaphoreType.DMA((1 + nm * nv,)),
        ],
        in_specs=[vmem] * (5 + 2 * nm),
        out_specs=(hbm, hbm),
    )(theirs, cols, outer, got, vectors, *units)
    back = lax.all_to_all(slab, everyone, 0, 0)
    grad_in, grad_out = call(
        sum_kernel, (shape((hidden // 128, 128), f32), shape((tiles, 128), f32))
    )(back)
    return (penalty[:, 0], grad_in.reshape(hidden), grad_out.reshape(feat))


def local(nv, nm, nr, resid_base, mlp_hidden, *rest):
    rows, feat = resid_base.shape
    quarter = mlp_hidden.shape[1] // (nm * nr)
    whole_tiles = rows == 8 and feat % 128 == 0 and quarter % 128 == 0
    small = nr == 2 and nv % 2 == 0 and nv * nr * rows == 64
    step = fused if whole_tiles and small else plain
    return step(nv, nm, nr, resid_base, mlp_hidden, *rest)


def solution(mesh):
    in_specs = (
        P(("parts", "vocab", "rep"), "mp"),
        P(("parts", "vocab", "rep"), "mp"),
        P(("parts", "mp")),
        P(("parts", "mp")),
        P("mp"),
        P(None, ("vocab", "mp", "rep")),
        P("parts"),
    )
    out_specs = (P(("parts", "vocab", "rep")), P(("parts", "mp")), P(("parts", "mp")))
    step = functools.partial(local, mesh.shape["vocab"], mesh.shape["mp"], mesh.shape["rep"])
    return jax.shard_map(step, mesh=mesh, in_specs=in_specs, out_specs=out_specs, check_vma=False)
```

```python
import functools

import jax
import jax.numpy as jnp
from jax import lax
from jax.experimental import pallas as pl
from jax.experimental.pallas import tpu as pltpu
from jax.sharding import PartitionSpec as P

softcap = 30.0
epsilon = 1e-06
bf16 = jnp.bfloat16
f32 = jnp.float32


def split_bf16(value, pieces):
    out = []
    for _ in range(pieces):
        part = lax.reduce_precision(value, 8, 7)
        out.append(part.astype(bf16))
        value = value - part
    return out


def from_peers(value, axis, size):
    moves = [[(i, (i + k) % size) for i in range(size)] for k in range(size)]
    return [value] + [lax.ppermute(value, axis, moves[k]) for k in range(1, size)]


def to_peers(pick, axis, size, index):
    moves = [[(i, (i + k) % size) for i in range(size)] for k in range(size)]
    return [pick(index)] + [
        lax.ppermute(pick((index + k) % size), axis, moves[k]) for k in range(1, size)
    ]


def in_order(values, index):
    size = len(values)
    ordered = []
    for j in range(size):
        value = values[0]
        for k in range(1, size):
            value = jnp.where((index - j) % size == k, values[k], value)
        ordered.append(value)
    return ordered


def plain(nv, nm, nr, resid_base, mlp_hidden, edit_in, edit_out, norm_gain, head, token_ids):
    rows, feat = resid_base.shape
    hidden = mlp_hidden.shape[1]
    model, voc = head.shape
    group = nv * nr * rows
    peers = nv * nm * nr
    quarter = hidden // (nm * nr)
    everyone = ("vocab", "mp", "rep")

    v_i = lax.axis_index("vocab")
    m_i = lax.axis_index("mp")
    r_i = lax.axis_index("rep")

    vectors = from_peers(jnp.stack([edit_out, norm_gain]), "mp", nm)
    vectors = jnp.concatenate(in_order(vectors, m_i), axis=1)
    out_all = vectors[0]
    gain_all = vectors[1]

    units = mlp_hidden.reshape(rows, nm, nr, quarter)
    units = jnp.concatenate(
        [
            part
            for part in to_peers(
                lambda r: lax.dynamic_index_in_dim(units, r, 2, keepdims=False), "rep", nr, r_i
            )
        ]
    )
    units = to_peers(
        lambda m: lax.dynamic_index_in_dim(units, m, 1, keepdims=False), "mp", nm, m_i
    )

    hidden_f = mlp_hidden.astype(f32)
    mix_part = jnp.sum(hidden_f * edit_in[None, :], axis=1)
    mix_cols = jnp.stack(split_bf16(mix_part, 3), axis=1)
    packed = jnp.concatenate([resid_base, jnp.pad(mix_cols, ((0, 0), (0, 125)))], axis=1)
    packed = jnp.broadcast_to(packed[None], (nv * nm, rows, feat + 128))
    got = lax.all_to_all(packed, ("vocab", "mp"), 0, 0)
    got = jnp.concatenate(in_order(from_peers(got, "rep", nr), r_i)).reshape(nr * nv, nm, rows, feat + 128)

    base = jnp.concatenate([got[:, m, :, :feat].reshape(group, feat) for m in range(nm)], axis=1)
    base_f = base.astype(f32)
    mix = jnp.sum(got[:, :, :, feat : feat + 3].astype(f32), axis=(1, 3)).reshape(group)
    resid = base_f + mix[:, None] * out_all[None, :]
    edit_scale = lax.rsqrt(jnp.mean(resid * resid, axis=1) + epsilon)
    base_scale = lax.rsqrt(jnp.mean(base_f * base_f, axis=1) + epsilon)
    along = jnp.sum(resid * out_all[None, :], axis=1)
    x_edit = (resid * edit_scale[:, None] * gain_all[None, :]).astype(bf16)
    x_base = (base_f * base_scale[:, None] * gain_all[None, :]).astype(bf16)
    direction = jnp.stack(split_bf16(out_all * gain_all, 3) + [jnp.zeros((model,), bf16)] * 5)
    pre = jnp.dot(
        jnp.concatenate([x_edit, x_base, direction]), head, preferred_element_type=f32
    )
    pre_edit = pre[:group]
    pre_base = pre[group : 2 * group]
    toward = jnp.sum(pre[2 * group :], axis=0)
    z_edit = softcap * jnp.tanh(pre_edit / softcap)
    z_base = softcap * jnp.tanh(pre_base / softcap)
    slope = 1.0 - (z_edit / softcap) ** 2
    exp_edit = jnp.exp(z_edit)
    exp_base = jnp.exp(z_base)
    ids = token_ids.reshape(nv, nr, rows).transpose(1, 0, 2).reshape(group)
    first_col = lax.axis_index(everyone) * voc
    onehot = (ids[:, None] == (first_col + jnp.arange(voc, dtype=jnp.int32))[None, :]).astype(f32)
    diff = z_base - z_edit
    pe = exp_edit * slope
    pb = exp_base * slope
    po = onehot * slope
    sums = jnp.stack(
        [
            jnp.sum(a, axis=1)
            for a in (
                exp_edit,
                exp_base,
                exp_base * diff,
                onehot * diff,
                pe * pre_edit,
                pb * pre_edit,
                po * pre_edit,
                pe * toward[None, :],
                pb * toward[None, :],
                po * toward[None, :],
            )
        ]
    )
    weight = mix * edit_scale
    wo = jnp.sum(weight[:, None] * po, axis=0)
    high_e, low_e = split_bf16(pe, 2)
    high_b, low_b = split_bf16(pb, 2)
    tail = jnp.stack(split_bf16(wo, 3) + [jnp.zeros((voc,), bf16)] * 5)
    outer = lax.dot_general(
        jnp.concatenate([high_e, high_b, low_e, low_b, tail]),
        head,
        (((1,), (1,)), ((), ())),
        preferred_element_type=f32,
    )
    rows_e = outer[:group] + outer[2 * group : 3 * group]
    rows_b = outer[group : 2 * group] + outer[3 * group : 4 * group]
    row_o = jnp.sum(outer[4 * group :], axis=0)
    flat = 10 * group
    padded = -(-flat // 1024) * 1024
    mine = jnp.pad(sums.reshape(flat), (0, padded - flat)).reshape(padded // 128, 128)
    theirs = lax.all_to_all(
        jnp.broadcast_to(mine[None], (peers, padded // 128, 128)), everyone, 0, 0
    )
    sums = jnp.sum(theirs, axis=0).reshape(padded)[:flat].reshape(10, group)
    se, sb, kl, gap, ae, ab, ao, te, tb, to = [sums[i] for i in range(10)]
    inv_e = 2.0 / se
    inv_b = 1.0 / sb
    align = ae * inv_e - ab * inv_b - ao
    proj = te * inv_e - tb * inv_b - to
    penalty = kl * inv_b + gap + 2.0 * (jnp.log(se) - jnp.log(sb))
    shrink = edit_scale * align / model
    coeff = edit_scale * proj - shrink * (edit_scale * along)
    weighted = jnp.sum((weight * inv_e)[:, None] * rows_e, axis=0) - jnp.sum((weight * inv_b)[:, None] * rows_b, axis=0) - row_o
    w_hi, w_lo = split_bf16(weighted, 2)
    mine = lax.dynamic_index_in_dim(coeff.reshape(nr, nv, rows), v_i, 1, keepdims=False)
    own = jnp.concatenate([lax.dynamic_index_in_dim(mine, (r_i - k) % nr, 0, keepdims=False) for k in range(nr)])
    part_in = [jnp.sum(u.astype(f32) * own[:, None], axis=0) for u in units]
    part_in = jnp.stack(in_order(part_in, m_i)).astype(bf16)
    slab = jnp.concatenate([w_hi.reshape(nm, feat), w_lo.reshape(nm, feat), part_in], axis=1)
    width = 2 * feat + quarter
    if width % 128 == 0:
        slab = slab.reshape(nm, width // 128, 128)
    slab = jnp.broadcast_to(slab[None, :, None], (nv, nm, nr) + slab.shape[1:])
    back = lax.all_to_all(slab.reshape((peers,) + slab.shape[3:]), everyone, 0, 0)
    back = back.reshape(nv, nm * nr, width).astype(f32)
    grad_in = jnp.sum(back[:, :, 2 * feat :], axis=0).reshape(hidden)
    weighted_own = jnp.sum(back[:, :, :feat] + back[:, :, feat : 2 * feat], axis=(0, 1))
    pull = mix * shrink * edit_scale
    base_own = lax.dynamic_slice_in_dim(base, m_i * feat, feat, 1).astype(f32)
    second = jnp.sum(pull[:, None] * base_own, axis=0) + jnp.sum(pull * mix) * edit_out
    grad_out = norm_gain * weighted_own - second
    penalty = lax.dynamic_slice(penalty.reshape(nr, nv, rows), (r_i, v_i, 0), (1, 1, rows))
    return (penalty.reshape(rows), grad_in, grad_out)


def send_kernel(copies, pieces, base_hbm, hidden_hbm, in_hbm, out_hbm, gain_hbm, packed_hbm, vec_ref, *refs):
    unit_refs = refs[:2]
    base_ref, hidden_ref, in_ref, packed_ref, mix_ref, sems = refs[2:]
    rows, hidden = hidden_ref.shape
    feat = base_ref.shape[1]
    quarter = hidden // (2 * pieces)
    get_hidden = pltpu.make_async_copy(hidden_hbm, hidden_ref, sems.at[0])
    get_in = pltpu.make_async_copy(in_hbm, in_ref, sems.at[1])
    get_base = pltpu.make_async_copy(base_hbm, base_ref, sems.at[2])
    later = [
        pltpu.make_async_copy(out_hbm, vec_ref.at[0], sems.at[3]),
        pltpu.make_async_copy(gain_hbm, vec_ref.at[1], sems.at[4]),
    ]
    r_i = lax.axis_index("rep")
    for i in range(pieces):
        for j in range(2):
            start = pl.multiple_of((2 * i + lax.rem(r_i + j, 2)) * quarter, 128)
            later.append(
                pltpu.make_async_copy(
                    hidden_hbm.at[:, pl.ds(start, quarter)],
                    unit_refs[j].at[i],
                    sems.at[7 + 2 * i + j],
                )
            )
    get_base.start()
    get_hidden.start()
    get_in.start()
    for move in later:
        move.start()
    get_base.wait()
    for i in range(copies):
        packed_ref[i] = base_ref[...]
    put_base = pltpu.make_async_copy(packed_ref, packed_hbm.at[:, :, pl.ds(0, feat)], sems.at[5])
    put_base.start()
    get_hidden.wait()
    get_in.wait()
    total = jnp.zeros((rows, 128), f32)
    for c in range(0, hidden, 128):
        total += hidden_ref[:, c : c + 128].astype(f32) * in_ref[:, c : c + 128]
    mix = jnp.sum(total, axis=1, keepdims=True)
    lane = lax.broadcasted_iota(jnp.int32, (rows, 128), 1)
    cols = jnp.zeros((rows, 128), f32)
    for i in range(3):
        piece = mix.astype(bf16).astype(f32)
        cols = jnp.where(lane == i, piece, cols)
        mix = mix - piece
    cols = cols.astype(bf16)
    for i in range(copies):
        mix_ref[i] = cols
    put_mix = pltpu.make_async_copy(mix_ref, packed_hbm.at[:, :, pl.ds(feat, 128)], sems.at[6])
    put_mix.start()
    for move in later:
        move.wait()
    put_base.wait()
    put_mix.wait()


def normed_rows(nv, nm, got_ref, vec_ref, cols_ref, x_ref):
    rows = got_ref.shape[1]
    feat = got_ref.shape[2] - 128
    model = nm * feat
    half = nv * rows
    pair = 2 * rows
    lane = lax.broadcasted_iota(jnp.int32, (pair, 128), 1)
    for v in range(0, nv, 2):
        at = v * rows

        def tile(m, c):
            first = got_ref[v * nm + m, :, c : c + 128].astype(f32)
            second = got_ref[(v + 1) * nm + m, :, c : c + 128].astype(f32)
            return jnp.concatenate([first, second], axis=0)

        mixed = tile(0, feat)
        for m in range(1, nm):
            mixed += tile(m, feat)
        mix = jnp.sum(mixed, axis=1, keepdims=True)
        mix_b = jnp.broadcast_to(mix, (pair, 128))
        sq_b = jnp.zeros((pair, 128), f32)
        sq_e = jnp.zeros((pair, 128), f32)
        dot_o = jnp.zeros((pair, 128), f32)
        for m in range(nm):
            for c in range(0, feat, 128):
                out = vec_ref[m, 0, c // 128 : c // 128 + 1, :]
                b = tile(m, c)
                e = b + mix_b * out
                sq_b += b * b
                sq_e += e * e
                dot_o += e * out
        scale_e = lax.rsqrt(jnp.sum(sq_e, axis=1, keepdims=True) / model + epsilon)
        scale_b = lax.rsqrt(jnp.sum(sq_b, axis=1, keepdims=True) / model + epsilon)
        along = jnp.sum(dot_o, axis=1, keepdims=True)
        cols_ref[at : at + pair, :] = jnp.where(
            lane == 0, mix, jnp.where(lane == 1, scale_e, jnp.where(lane == 2, along, 0.0))
        )
        scale_e = jnp.broadcast_to(scale_e, (pair, 128))
        scale_b = jnp.broadcast_to(scale_b, (pair, 128))
        for m in range(nm):
            for c in range(0, feat, 128):
                d = m * feat + c
                t = c // 128
                out = vec_ref[m, 0, t : t + 1, :]
                gain = vec_ref[m, 1, t : t + 1, :]
                b = tile(m, c)
                e = b + mix_b * out
                x_ref[at : at + pair, d : d + 128] = (e * scale_e * gain).astype(bf16)
                x_ref[half + at : half + at + pair, d : d + 128] = (b * scale_b * gain).astype(bf16)


def early_kernel(nv, nm, own_ref, vec_ref, head_hbm, head_ref, pre_ref, cols_ref, x_ref, sems):
    model = head_hbm.shape[0]
    part = model // sems.shape[0]
    moves = []
    for i in range(sems.shape[0]):
        span = pl.ds(i * part, part)
        moves.append(pltpu.make_async_copy(head_hbm.at[span], head_ref.at[span], sems.at[i]))
    for move in moves:
        move.start()
    feat = own_ref.shape[2] - 128
    half = cols_ref.shape[0]
    normed_rows(nv, nm, own_ref, vec_ref, cols_ref, x_ref)
    sub = lax.broadcasted_iota(jnp.int32, (16, 128), 0)
    for d in range(0, model, 128):
        m, t = d // feat, d % feat // 128
        rest = vec_ref[m, 0, t : t + 1, :] * vec_ref[m, 1, t : t + 1, :]
        block = jnp.zeros((16, 128), f32)
        for i in range(3):
            piece = rest.astype(bf16).astype(f32)
            block = jnp.where(sub == i, piece, block)
            rest = rest - piece
        x_ref[2 * half :, d : d + 128] = block.astype(bf16)
    pre = None
    for i, move in enumerate(moves):
        move.wait()
        span = slice(i * part, (i + 1) * part)
        block = jnp.dot(x_ref[:, span], head_ref[span, :], preferred_element_type=f32)
        pre = block if pre is None else pre + block
    pre_ref[...] = pre


def score_kernel(nv, nm, other_ref, vec_ref, ids_ref, head_ref, early_ref, early_cols_ref, slab_hbm, cols_ref, ops_hbm, x_ref, slab_ref, ops_ref, sems):
    voc = head_ref.shape[1]
    half = early_cols_ref.shape[0]
    group = 2 * half
    cols_ref[:half] = early_cols_ref[...]
    normed_rows(nv, nm, other_ref, vec_ref, cols_ref.at[half:], x_ref)
    late = jnp.dot(x_ref[...], head_ref[...], preferred_element_type=f32)
    pre_edit = jnp.concatenate([early_ref[:half], late[:half]], axis=0)
    pre_base = jnp.concatenate([early_ref[half:group], late[half:]], axis=0)
    toward = jnp.sum(early_ref[group:], axis=0, keepdims=True)
    th = jnp.tanh(pre_edit / softcap)
    z_edit = softcap * th
    z_base = softcap * jnp.tanh(pre_base / softcap)
    slope = 1.0 - th * th
    exp_edit = jnp.exp(z_edit)
    exp_base = jnp.exp(z_base)
    first_col = lax.axis_index(("vocab", "mp", "rep")) * voc
    column = lax.broadcasted_iota(jnp.int32, (group, voc), 1) + first_col
    hit = column == ids_ref[...]
    diff = z_base - z_edit
    pe = exp_edit * slope
    pb = exp_base * slope
    po = jnp.where(hit, slope, 0.0)

    high_e = pe.astype(bf16)
    high_b = pb.astype(bf16)
    ops_ref[:group] = high_e
    ops_ref[group : 2 * group] = high_b
    ops_ref[2 * group : 3 * group] = (pe - high_e.astype(f32)).astype(bf16)
    ops_ref[3 * group : 4 * group] = (pb - high_b.astype(f32)).astype(bf16)
    weight = cols_ref[:, 0:1] * cols_ref[:, 1:2]
    rest = jnp.sum(weight * po, axis=0, keepdims=True)
    sub = lax.broadcasted_iota(jnp.int32, (16, voc), 0)
    block = jnp.zeros((16, voc), f32)
    for i in range(3):
        piece = rest.astype(bf16).astype(f32)
        block = jnp.where(sub == i, piece, block)
        rest = rest - piece
    ops_ref[4 * group :] = block.astype(bf16)
    put_ops = pltpu.make_async_copy(ops_ref, ops_hbm, sems.at[1])
    put_ops.start()

    def total(a):
        return jnp.sum(a, axis=1, keepdims=True)

    sums = [
        total(exp_edit),
        total(exp_base),
        total(exp_base * diff),
        total(jnp.where(hit, diff, 0.0)),
        total(pe * pre_edit),
        total(pb * pre_edit),
        total(po * pre_edit),
        total(pe * toward),
        total(pb * toward),
        total(po * toward),
    ]
    lane = lax.broadcasted_iota(jnp.int32, (group, 128), 1)
    first = jnp.zeros((group, 128), f32)
    second = jnp.zeros((group, 128), f32)
    for i in range(8):
        first = jnp.where(lane == i, sums[i], first)
    for i in range(8, 10):
        second = jnp.where(lane == i - 8, sums[i], second)
    straight = jnp.concatenate([first, second], axis=0)
    swapped = jnp.concatenate([first[half:], first[:half], second[half:], second[:half]], axis=0)
    table = jnp.where(lax.axis_index("rep") == 0, straight, swapped)
    table = table.T[:8]
    for p in range(slab_ref.shape[0]):
        slab_ref[p] = table
    put_slab = pltpu.make_async_copy(slab_ref, slab_hbm, sems.at[0])
    put_slab.start()

    put_slab.wait()
    put_ops.wait()


def outer_kernel(ops_hbm, head_hbm, outer_ref, ops_ref, head_ref, sems):
    both = outer_ref.shape[0] - 16
    part = outer_ref.shape[1] // (sems.shape[0] - 1)
    get = pltpu.make_async_copy(ops_hbm, ops_ref, sems.at[0])
    get.start()
    moves = []
    for i in range(outer_ref.shape[1] // part):
        span = pl.ds(i * part, part)
        source = head_hbm.at[span]
        moves.append(pltpu.make_async_copy(source, head_ref.at[span], sems.at[1 + i]))
    for move in moves:
        move.start()
    get.wait()
    for i, move in enumerate(moves):
        move.wait()
        c = i * part
        block = lax.dot_general(
            ops_ref[...],
            head_ref[c : c + part, :],
            (((1,), (1,)), ((), ())),
            preferred_element_type=f32,
        )
        outer_ref[:both, c : c + part] = block[:both] + block[both : 2 * both]
        outer_ref[both:, c : c + part] = block[2 * both :]


def close_kernel(nv, nm, theirs_ref, cols_ref, outer_ref, own_ref, all_ref, *refs):
    units = refs[:nm]
    slab_hbm, penalty_hbm, coeff_ref, pen_ref, pull_ref, vec_ref, slab_ref, second_ref, sems = refs[nm:]
    rows = own_ref.shape[1]
    feat = own_ref.shape[2] - 128
    model = outer_ref.shape[1]
    group = 2 * nv * rows
    half = group // 2
    tiles = feat // 128
    v_i = lax.axis_index("vocab")
    m_i = lax.axis_index("mp")
    r_i = lax.axis_index("rep")

    table = theirs_ref[0]
    for p in range(1, theirs_ref.shape[0]):
        table += theirs_ref[p]
    table = jnp.concatenate([table, jnp.zeros((120, 128), f32)], axis=0).T
    first = table[:group]
    second = table[group:]
    swap_first = jnp.concatenate([first[half:], first[:half]], axis=0)
    swap_second = jnp.concatenate([second[half:], second[:half]], axis=0)
    first = jnp.where(r_i == 0, first, swap_first)
    second = jnp.where(r_i == 0, second, swap_second)
    se, sb, kl, gap, ae, ab, ao, te = [first[:, i : i + 1] for i in range(8)]
    tb, to = second[:, 0:1], second[:, 1:2]
    mix = cols_ref[:, 0:1]
    scale = cols_ref[:, 1:2]
    along = cols_ref[:, 2:3]
    inv_e = 2.0 / se
    inv_b = 1.0 / sb
    align = ae * inv_e - ab * inv_b - ao
    proj = te * inv_e - tb * inv_b - to
    penalty = kl * inv_b + gap + 2.0 * (jnp.log(se) - jnp.log(sb))
    shrink = scale * align / model
    coeff = scale * proj - shrink * (scale * along)
    weight = mix * scale
    pull = weight * shrink
    coeff_ref[...] = jnp.broadcast_to(coeff, (group, 128))
    pen_ref[...] = jnp.broadcast_to(penalty, (group, 128))
    put_pen = pltpu.make_async_copy(
        pen_ref.at[pl.ds(pl.multiple_of(v_i * rows, rows), rows)], penalty_hbm, sems.at[0]
    )
    put_pen.start()

    pull_ref[...] = jnp.broadcast_to(pull, (group, 128))
    pulls = pull_ref[pl.ds(pl.multiple_of(v_i * rows, rows), rows), :]
    pull_ref[...] = jnp.broadcast_to(pull * mix, (group, 128))
    pulled = jnp.sum(pull_ref[pl.ds(pl.multiple_of(v_i * rows, rows), rows), :], axis=0, keepdims=True)
    for t in range(tiles):
        part = own_ref[v_i * nm + m_i, :, t * 128 : (t + 1) * 128].astype(f32) * pulls
        second_ref[t : t + 1, :] = (
            jnp.sum(part, axis=0, keepdims=True) + pulled * all_ref[m_i, 0, t : t + 1, :]
        )

    own = [
        coeff_ref[pl.ds(pl.multiple_of((k * nv + v_i) * rows, rows), rows), :] for k in range(2)
    ]
    for k in range(nm):
        m = lax.rem(m_i - k + nm, nm)
        for t in range(units[0].shape[1] // 128):
            c = t * 128
            row = units[k][:rows, c : c + 128].astype(f32) * own[0]
            row += units[k][rows:, c : c + 128].astype(f32) * own[1]
            vec_ref[m, pl.ds(tiles + t, 1), :] = jnp.sum(row, axis=0, keepdims=True)
    by_e = jnp.broadcast_to(weight * inv_e, (group, 128))
    by_b = jnp.broadcast_to(weight * inv_b, (group, 128))
    puts = []
    for m in range(nm):
        for t in range(tiles):
            d = m * feat + t * 128
            plus = outer_ref[:group, d : d + 128] * by_e
            less = outer_ref[group : 2 * group, d : d + 128] * by_b
            row = jnp.sum(plus - less, axis=0, keepdims=True)
            row -= jnp.sum(outer_ref[2 * group :, d : d + 128], axis=0, keepdims=True)
            row = row * all_ref[m, 1, t : t + 1, :] - jnp.where(
                m_i == m, second_ref[t : t + 1, :], 0.0
            )
            vec_ref[m, t : t + 1, :] = row
        block = vec_ref[m].astype(bf16)
        for v in range(nv):
            for r in range(2):
                slab_ref[m, 2 * v + r] = block
        for v in range(nv):
            put = pltpu.make_async_copy(
                slab_ref.at[m, pl.ds(2 * v, 2)],
                slab_hbm.at[pl.ds((v * nm + m) * 2, 2)],
                sems.at[1 + v * nm + m],
            )
            put.start()
            puts.append(put)
    put_pen.wait()
    for put in puts:
        put.wait()


def sum_kernel(back_ref, in_ref, out_ref):
    peers = back_ref.shape[0]
    tiles = out_ref.shape[0]
    units = back_ref.shape[1] - tiles
    pieces = in_ref.shape[0] // units
    wide = jnp.zeros((tiles, 128), f32)
    for q in range(pieces):
        total = back_ref[q].astype(f32)
        for p in range(q + pieces, peers, pieces):
            total += back_ref[p].astype(f32)
        wide += total[:tiles]
        in_ref[q * units : (q + 1) * units, :] = total[tiles:]
    out_ref[...] = wide


def in_hbm(value):
    return pltpu.with_memory_space_constraint(value, pltpu.HBM)


def call(kernel, out_shape, scratch=(), megabytes=6, **more):
    return pl.pallas_call(
        kernel,
        out_shape=out_shape,
        scratch_shapes=scratch,
        compiler_params=pltpu.CompilerParams(vmem_limit_bytes=megabytes << 20),
        **more,
    )


def fused(nv, nm, nr, resid_base, mlp_hidden, edit_in, edit_out, norm_gain, head, token_ids):
    rows, feat = resid_base.shape
    hidden = mlp_hidden.shape[1]
    model, voc = head.shape
    group = nv * nr * rows
    peers = nv * nm * nr
    quarter = hidden // (nm * nr)
    everyone = ("vocab", "mp", "rep")
    m_i = lax.axis_index("mp")
    r_i = lax.axis_index("rep")
    shape = jax.ShapeDtypeStruct

    tiles = feat // 128
    hbm = pl.BlockSpec(memory_space=pltpu.HBM)
    vmem = pl.BlockSpec(memory_space=pltpu.VMEM)
    out_tiles = edit_out.reshape(tiles, 128)
    gain_tiles = norm_gain.reshape(tiles, 128)

    packed, vectors, keep, give = call(
        functools.partial(send_kernel, nv * nm, nm),
        (
            pltpu.HBM((nv * nm, rows, feat + 128), bf16),
            shape((2, tiles, 128), f32),
        )
        + (shape((nm, rows, quarter), bf16),) * 2,
        [
            pltpu.VMEM((rows, feat), bf16),
            pltpu.VMEM((rows, hidden), bf16),
            pltpu.VMEM((1, hidden), f32),
            pltpu.VMEM((nv * nm, rows, feat), bf16),
            pltpu.VMEM((nv * nm, rows, 128), bf16),
            pltpu.SemaphoreType.DMA((7 + 2 * nm,)),
        ],
        in_specs=[hbm] * 5,
        out_specs=(hbm,) + (vmem,) * 3,
    )(
        *(
            in_hbm(a)
            for a in (resid_base, mlp_hidden, edit_in.reshape(1, hidden), out_tiles, gain_tiles)
        )
    )
    got = lax.all_to_all(packed, ("vocab", "mp"), 0, 0)
    other = lax.ppermute(got, "rep", [(0, 1), (1, 0)])
    units = jnp.concatenate([keep, lax.ppermute(give, "rep", [(0, 1), (1, 0)])], axis=1)
    units = [lax.dynamic_index_in_dim(units, (m_i + k) % nm, 0, keepdims=False) for k in range(nm)]
    vectors = from_peers(vectors, "mp", nm)
    vectors, units = lax.optimization_barrier((vectors, units))
    vectors = jnp.stack(in_order(vectors, m_i))
    half = group // 2
    staged, early, early_cols = call(
        functools.partial(early_kernel, nv, nm),
        (
            pltpu.VMEM((model, voc), bf16),
            shape((group + 16, voc), f32),
            shape((half, 128), f32),
        ),
        [pltpu.VMEM((group + 16, model), bf16), pltpu.SemaphoreType.DMA((6,))],
        8,
        in_specs=[vmem, vmem, hbm],
        out_specs=(vmem, vmem, vmem),
    )(got, vectors, in_hbm(head))
    ids = token_ids.reshape(nv, nr, rows)
    ids = jnp.concatenate(
        [lax.dynamic_index_in_dim(ids, (r_i + k) % nr, 1, keepdims=False) for k in range(nr)]
    ).reshape(group, 1)

    slab, cols, ops = call(
        functools.partial(score_kernel, nv, nm),
        (
            pltpu.HBM((peers, 8, 128), f32),
            shape((group, 128), f32),
            pltpu.HBM((4 * group + 16, voc), bf16),
        ),
        [
            pltpu.VMEM((group, model), bf16),
            pltpu.VMEM((peers, 8, 128), f32),
            pltpu.VMEM((4 * group + 16, voc), bf16),
            pltpu.SemaphoreType.DMA((2,)),
        ],
        in_specs=[vmem] * 6,
        out_specs=(hbm, vmem, hbm),
    )(other, vectors, ids, staged, early, early_cols)
    theirs = lax.all_to_all(slab, everyone, 0, 0)
    parts = 3
    outer = call(
        outer_kernel,
        shape((2 * group + 16, model), f32),
        [
            pltpu.VMEM((4 * group + 16, voc), bf16),
            pltpu.VMEM((model, voc), bf16),
            pltpu.SemaphoreType.DMA((1 + parts,)),
        ],
        12,
        in_specs=[hbm, hbm],
    )(in_hbm(ops), in_hbm(head))

    moves = [[(m, (m + k) % nm) for m in range(nm)] for k in range(nm)]
    units = [units[0]] + [lax.ppermute(units[k], "mp", moves[k]) for k in range(1, nm)]

    width = (feat + quarter) // 128
    slab, penalty = call(
        functools.partial(close_kernel, nv, nm),
        (pltpu.HBM((peers, width, 128), bf16), pltpu.HBM((rows, 128), f32)),
        [
            pltpu.VMEM((group, 128), f32),
            pltpu.VMEM((group, 128), f32),
            pltpu.VMEM((group, 128), f32),
            pltpu.VMEM((nm, width, 128), f32),
            pltpu.VMEM((nm, 2 * nv, width, 128), bf16),
            pltpu.VMEM((tiles, 128), f32),
            pltpu.SemaphoreType.DMA((1 + nm * nv,)),
        ],
        in_specs=[vmem] * (5 + nm),
        out_specs=(hbm, hbm),
    )(theirs, cols, outer, got, vectors, *units)
    back = lax.all_to_all(slab, everyone, 0, 0)
    grad_in, grad_out = call(
        sum_kernel, (shape((hidden // 128, 128), f32), shape((tiles, 128), f32))
    )(back)
    return (penalty[:, 0], grad_in.reshape(hidden), grad_out.reshape(feat))


def local(nv, nm, nr, resid_base, mlp_hidden, *rest):
    rows, feat = resid_base.shape
    quarter = mlp_hidden.shape[1] // (nm * nr)
    whole_tiles = rows == 8 and feat % 128 == 0 and quarter % 128 == 0
    small = nr == 2 and nv % 2 == 0 and nv * nr * rows == 64
    step = fused if whole_tiles and small else plain
    return step(nv, nm, nr, resid_base, mlp_hidden, *rest)


def solution(mesh):
    in_specs = (
        P(("parts", "vocab", "rep"), "mp"),
        P(("parts", "vocab", "rep"), "mp"),
        P(("parts", "mp")),
        P(("parts", "mp")),
        P("mp"),
        P(None, ("vocab", "mp", "rep")),
        P("parts"),
    )
    out_specs = (P(("parts", "vocab", "rep")), P(("parts", "mp")), P(("parts", "mp")))
    step = functools.partial(local, mesh.shape["vocab"], mesh.shape["mp"], mesh.shape["rep"])
    return jax.shard_map(step, mesh=mesh, in_specs=in_specs, out_specs=out_specs, check_vma=False)
```

```python
import functools

import jax
import jax.numpy as jnp
from jax import lax
from jax.experimental import pallas as pl
from jax.experimental.pallas import tpu as pltpu
from jax.sharding import PartitionSpec as P

softcap = 30.0
epsilon = 1e-06
bf16 = jnp.bfloat16
f32 = jnp.float32


def split_bf16(value, pieces):
    out = []
    for _ in range(pieces):
        part = lax.reduce_precision(value, 8, 7)
        out.append(part.astype(bf16))
        value = value - part
    return out


def from_peers(value, axis, size):
    moves = [[(i, (i + k) % size) for i in range(size)] for k in range(size)]
    return [value] + [lax.ppermute(value, axis, moves[k]) for k in range(1, size)]


def to_peers(pick, axis, size, index):
    moves = [[(i, (i + k) % size) for i in range(size)] for k in range(size)]
    return [pick(index)] + [
        lax.ppermute(pick((index + k) % size), axis, moves[k]) for k in range(1, size)
    ]


def in_order(values, index):
    size = len(values)
    ordered = []
    for j in range(size):
        value = values[0]
        for k in range(1, size):
            value = jnp.where((index - j) % size == k, values[k], value)
        ordered.append(value)
    return ordered


def plain(nv, nm, nr, resid_base, mlp_hidden, edit_in, edit_out, norm_gain, head, token_ids):
    rows, feat = resid_base.shape
    hidden = mlp_hidden.shape[1]
    model, voc = head.shape
    group = nv * nr * rows
    peers = nv * nm * nr
    quarter = hidden // (nm * nr)
    everyone = ("vocab", "mp", "rep")

    v_i = lax.axis_index("vocab")
    m_i = lax.axis_index("mp")
    r_i = lax.axis_index("rep")

    vectors = from_peers(jnp.stack([edit_out, norm_gain]), "mp", nm)
    vectors = jnp.concatenate(in_order(vectors, m_i), axis=1)
    out_all = vectors[0]
    gain_all = vectors[1]

    units = mlp_hidden.reshape(rows, nm, nr, quarter)
    units = jnp.concatenate(
        [
            part
            for part in to_peers(
                lambda r: lax.dynamic_index_in_dim(units, r, 2, keepdims=False), "rep", nr, r_i
            )
        ]
    )
    units = to_peers(
        lambda m: lax.dynamic_index_in_dim(units, m, 1, keepdims=False), "mp", nm, m_i
    )

    hidden_f = mlp_hidden.astype(f32)
    mix_part = jnp.sum(hidden_f * edit_in[None, :], axis=1)
    mix_cols = jnp.stack(split_bf16(mix_part, 3), axis=1)
    packed = jnp.concatenate([resid_base, jnp.pad(mix_cols, ((0, 0), (0, 125)))], axis=1)
    packed = jnp.broadcast_to(packed[None], (nv * nm, rows, feat + 128))
    got = lax.all_to_all(packed, ("vocab", "mp"), 0, 0)
    got = jnp.concatenate(in_order(from_peers(got, "rep", nr), r_i)).reshape(nr * nv, nm, rows, feat + 128)

    base = jnp.concatenate([got[:, m, :, :feat].reshape(group, feat) for m in range(nm)], axis=1)
    base_f = base.astype(f32)
    mix = jnp.sum(got[:, :, :, feat : feat + 3].astype(f32), axis=(1, 3)).reshape(group)
    resid = base_f + mix[:, None] * out_all[None, :]
    edit_scale = lax.rsqrt(jnp.mean(resid * resid, axis=1) + epsilon)
    base_scale = lax.rsqrt(jnp.mean(base_f * base_f, axis=1) + epsilon)
    along = jnp.sum(resid * out_all[None, :], axis=1)
    x_edit = (resid * edit_scale[:, None] * gain_all[None, :]).astype(bf16)
    x_base = (base_f * base_scale[:, None] * gain_all[None, :]).astype(bf16)
    direction = jnp.stack(split_bf16(out_all * gain_all, 3) + [jnp.zeros((model,), bf16)] * 5)
    pre = jnp.dot(
        jnp.concatenate([x_edit, x_base, direction]), head, preferred_element_type=f32
    )
    pre_edit = pre[:group]
    pre_base = pre[group : 2 * group]
    toward = jnp.sum(pre[2 * group :], axis=0)
    z_edit = softcap * jnp.tanh(pre_edit / softcap)
    z_base = softcap * jnp.tanh(pre_base / softcap)
    slope = 1.0 - (z_edit / softcap) ** 2
    exp_edit = jnp.exp(z_edit)
    exp_base = jnp.exp(z_base)
    ids = token_ids.reshape(nv, nr, rows).transpose(1, 0, 2).reshape(group)
    first_col = lax.axis_index(everyone) * voc
    onehot = (ids[:, None] == (first_col + jnp.arange(voc, dtype=jnp.int32))[None, :]).astype(f32)
    diff = z_base - z_edit
    pe = exp_edit * slope
    pb = exp_base * slope
    po = onehot * slope
    sums = jnp.stack(
        [
            jnp.sum(a, axis=1)
            for a in (
                exp_edit,
                exp_base,
                exp_base * diff,
                onehot * diff,
                pe * pre_edit,
                pb * pre_edit,
                po * pre_edit,
                pe * toward[None, :],
                pb * toward[None, :],
                po * toward[None, :],
            )
        ]
    )
    weight = mix * edit_scale
    wo = jnp.sum(weight[:, None] * po, axis=0)
    high_e, low_e = split_bf16(pe, 2)
    high_b, low_b = split_bf16(pb, 2)
    tail = jnp.stack(split_bf16(wo, 3) + [jnp.zeros((voc,), bf16)] * 5)
    outer = lax.dot_general(
        jnp.concatenate([high_e, high_b, low_e, low_b, tail]),
        head,
        (((1,), (1,)), ((), ())),
        preferred_element_type=f32,
    )
    rows_e = outer[:group] + outer[2 * group : 3 * group]
    rows_b = outer[group : 2 * group] + outer[3 * group : 4 * group]
    row_o = jnp.sum(outer[4 * group :], axis=0)
    flat = 10 * group
    padded = -(-flat // 1024) * 1024
    mine = jnp.pad(sums.reshape(flat), (0, padded - flat)).reshape(padded // 128, 128)
    theirs = lax.all_to_all(
        jnp.broadcast_to(mine[None], (peers, padded // 128, 128)), everyone, 0, 0
    )
    sums = jnp.sum(theirs, axis=0).reshape(padded)[:flat].reshape(10, group)
    se, sb, kl, gap, ae, ab, ao, te, tb, to = [sums[i] for i in range(10)]
    inv_e = 2.0 / se
    inv_b = 1.0 / sb
    align = ae * inv_e - ab * inv_b - ao
    proj = te * inv_e - tb * inv_b - to
    penalty = kl * inv_b + gap + 2.0 * (jnp.log(se) - jnp.log(sb))
    shrink = edit_scale * align / model
    coeff = edit_scale * proj - shrink * (edit_scale * along)
    weighted = jnp.sum((weight * inv_e)[:, None] * rows_e, axis=0) - jnp.sum((weight * inv_b)[:, None] * rows_b, axis=0) - row_o
    w_hi, w_lo = split_bf16(weighted, 2)
    mine = lax.dynamic_index_in_dim(coeff.reshape(nr, nv, rows), v_i, 1, keepdims=False)
    own = jnp.concatenate([lax.dynamic_index_in_dim(mine, (r_i - k) % nr, 0, keepdims=False) for k in range(nr)])
    part_in = [jnp.sum(u.astype(f32) * own[:, None], axis=0) for u in units]
    part_in = jnp.stack(in_order(part_in, m_i)).astype(bf16)
    slab = jnp.concatenate([w_hi.reshape(nm, feat), w_lo.reshape(nm, feat), part_in], axis=1)
    width = 2 * feat + quarter
    if width % 128 == 0:
        slab = slab.reshape(nm, width // 128, 128)
    slab = jnp.broadcast_to(slab[None, :, None], (nv, nm, nr) + slab.shape[1:])
    back = lax.all_to_all(slab.reshape((peers,) + slab.shape[3:]), everyone, 0, 0)
    back = back.reshape(nv, nm * nr, width).astype(f32)
    grad_in = jnp.sum(back[:, :, 2 * feat :], axis=0).reshape(hidden)
    weighted_own = jnp.sum(back[:, :, :feat] + back[:, :, feat : 2 * feat], axis=(0, 1))
    pull = mix * shrink * edit_scale
    base_own = lax.dynamic_slice_in_dim(base, m_i * feat, feat, 1).astype(f32)
    second = jnp.sum(pull[:, None] * base_own, axis=0) + jnp.sum(pull * mix) * edit_out
    grad_out = norm_gain * weighted_own - second
    penalty = lax.dynamic_slice(penalty.reshape(nr, nv, rows), (r_i, v_i, 0), (1, 1, rows))
    return (penalty.reshape(rows), grad_in, grad_out)


def send_kernel(copies, pieces, base_hbm, hidden_hbm, in_hbm, out_hbm, gain_hbm, packed_hbm, vec_ref, *refs):
    unit_refs = refs[:2]
    base_ref, hidden_ref, in_ref, packed_ref, mix_ref, sems = refs[2:]
    rows, hidden = hidden_ref.shape
    feat = base_ref.shape[1]
    quarter = hidden // (2 * pieces)
    get_hidden = pltpu.make_async_copy(hidden_hbm, hidden_ref, sems.at[0])
    get_in = pltpu.make_async_copy(in_hbm, in_ref, sems.at[1])
    get_base = pltpu.make_async_copy(base_hbm, base_ref, sems.at[2])
    later = [
        pltpu.make_async_copy(out_hbm, vec_ref.at[0], sems.at[3]),
        pltpu.make_async_copy(gain_hbm, vec_ref.at[1], sems.at[4]),
    ]
    r_i = lax.axis_index("rep")
    for i in range(pieces):
        for j in range(2):
            start = pl.multiple_of((2 * i + lax.rem(r_i + j, 2)) * quarter, 128)
            later.append(
                pltpu.make_async_copy(
                    hidden_hbm.at[:, pl.ds(start, quarter)],
                    unit_refs[j].at[i],
                    sems.at[7 + 2 * i + j],
                )
            )
    get_base.start()
    get_hidden.start()
    get_in.start()
    for move in later:
        move.start()
    get_base.wait()
    for i in range(copies):
        packed_ref[i] = base_ref[...]
    put_base = pltpu.make_async_copy(packed_ref, packed_hbm.at[:, :, pl.ds(0, feat)], sems.at[5])
    put_base.start()
    get_hidden.wait()
    get_in.wait()
    total = jnp.zeros((rows, 128), f32)
    for c in range(0, hidden, 128):
        total += hidden_ref[:, c : c + 128].astype(f32) * in_ref[:, c : c + 128]
    mix = jnp.sum(total, axis=1, keepdims=True)
    lane = lax.broadcasted_iota(jnp.int32, (rows, 128), 1)
    cols = jnp.zeros((rows, 128), f32)
    for i in range(3):
        piece = mix.astype(bf16).astype(f32)
        cols = jnp.where(lane == i, piece, cols)
        mix = mix - piece
    cols = cols.astype(bf16)
    for i in range(copies):
        mix_ref[i] = cols
    put_mix = pltpu.make_async_copy(mix_ref, packed_hbm.at[:, :, pl.ds(feat, 128)], sems.at[6])
    put_mix.start()
    for move in later:
        move.wait()
    put_base.wait()
    put_mix.wait()


def normed_rows(nv, nm, got_ref, vec_ref, cols_ref, x_ref):
    rows = got_ref.shape[1]
    feat = got_ref.shape[2] - 128
    model = nm * feat
    half = nv * rows
    pair = 2 * rows
    lane = lax.broadcasted_iota(jnp.int32, (pair, 128), 1)
    for v in range(0, nv, 2):
        at = v * rows

        def tile(m, c):
            first = got_ref[v * nm + m, :, c : c + 128].astype(f32)
            second = got_ref[(v + 1) * nm + m, :, c : c + 128].astype(f32)
            return jnp.concatenate([first, second], axis=0)

        mixed = tile(0, feat)
        for m in range(1, nm):
            mixed += tile(m, feat)
        mix = jnp.sum(mixed, axis=1, keepdims=True)
        mix_b = jnp.broadcast_to(mix, (pair, 128))
        sq_b = jnp.zeros((pair, 128), f32)
        sq_e = jnp.zeros((pair, 128), f32)
        dot_o = jnp.zeros((pair, 128), f32)
        for m in range(nm):
            for c in range(0, feat, 128):
                out = vec_ref[m, 0, c // 128 : c // 128 + 1, :]
                b = tile(m, c)
                e = b + mix_b * out
                sq_b += b * b
                sq_e += e * e
                dot_o += e * out
        scale_e = lax.rsqrt(jnp.sum(sq_e, axis=1, keepdims=True) / model + epsilon)
        scale_b = lax.rsqrt(jnp.sum(sq_b, axis=1, keepdims=True) / model + epsilon)
        along = jnp.sum(dot_o, axis=1, keepdims=True)
        cols_ref[at : at + pair, :] = jnp.where(
            lane == 0, mix, jnp.where(lane == 1, scale_e, jnp.where(lane == 2, along, 0.0))
        )
        scale_e = jnp.broadcast_to(scale_e, (pair, 128))
        scale_b = jnp.broadcast_to(scale_b, (pair, 128))
        for m in range(nm):
            for c in range(0, feat, 128):
                d = m * feat + c
                t = c // 128
                out = vec_ref[m, 0, t : t + 1, :]
                gain = vec_ref[m, 1, t : t + 1, :]
                b = tile(m, c)
                e = b + mix_b * out
                x_ref[at : at + pair, d : d + 128] = (e * scale_e * gain).astype(bf16)
                x_ref[half + at : half + at + pair, d : d + 128] = (b * scale_b * gain).astype(bf16)


def stage_kernel(after_ref, head_hbm, head_ref, sems):
    part = head_ref.shape[0] // sems.shape[0]
    moves = []
    for i in range(sems.shape[0]):
        span = pl.ds(i * part, part)
        moves.append(pltpu.make_async_copy(head_hbm.at[span], head_ref.at[span], sems.at[i]))
        moves[i].start()
    for move in moves:
        move.wait()


def early_kernel(nv, nm, own_ref, vec_ref, staged_ref, head_hbm, head_ref, pre_ref, cols_ref, x_ref, sems):
    model = head_hbm.shape[0]
    first = staged_ref.shape[0]
    part = (model - first) // sems.shape[0]
    moves = []
    for i in range(sems.shape[0]):
        move = pltpu.make_async_copy(
            head_hbm.at[pl.ds(first + i * part, part)],
            head_ref.at[pl.ds(i * part, part)],
            sems.at[i],
        )
        move.start()
        moves.append(move)
    feat = own_ref.shape[2] - 128
    half = cols_ref.shape[0]
    normed_rows(nv, nm, own_ref, vec_ref, cols_ref, x_ref)
    sub = lax.broadcasted_iota(jnp.int32, (16, 128), 0)
    for d in range(0, model, 128):
        m, t = d // feat, d % feat // 128
        rest = vec_ref[m, 0, t : t + 1, :] * vec_ref[m, 1, t : t + 1, :]
        block = jnp.zeros((16, 128), f32)
        for i in range(3):
            piece = rest.astype(bf16).astype(f32)
            block = jnp.where(sub == i, piece, block)
            rest = rest - piece
        x_ref[2 * half :, d : d + 128] = block.astype(bf16)
    pre = jnp.dot(x_ref[:, :first], staged_ref[...], preferred_element_type=f32)
    for i, move in enumerate(moves):
        move.wait()
        at = i * part
        pre += jnp.dot(
            x_ref[:, first + at : first + at + part],
            head_ref[at : at + part, :],
            preferred_element_type=f32,
        )
    pre_ref[...] = pre


def score_kernel(nv, nm, other_ref, vec_ref, ids_ref, staged_ref, head_ref, early_ref, early_cols_ref, slab_hbm, cols_ref, ops_hbm, x_ref, slab_ref, ops_ref, sems):
    voc = head_ref.shape[1]
    half = early_cols_ref.shape[0]
    group = 2 * half
    cols_ref[:half] = early_cols_ref[...]
    normed_rows(nv, nm, other_ref, vec_ref, cols_ref.at[half:], x_ref)
    first = staged_ref.shape[0]
    late = jnp.dot(x_ref[:, :first], staged_ref[...], preferred_element_type=f32)
    late += jnp.dot(x_ref[:, first:], head_ref[...], preferred_element_type=f32)
    pre_edit = jnp.concatenate([early_ref[:half], late[:half]], axis=0)
    pre_base = jnp.concatenate([early_ref[half:group], late[half:]], axis=0)
    toward = jnp.sum(early_ref[group:], axis=0, keepdims=True)
    th = jnp.tanh(pre_edit / softcap)
    z_edit = softcap * th
    z_base = softcap * jnp.tanh(pre_base / softcap)
    slope = 1.0 - th * th
    exp_edit = jnp.exp(z_edit)
    exp_base = jnp.exp(z_base)
    first_col = lax.axis_index(("vocab", "mp", "rep")) * voc
    column = lax.broadcasted_iota(jnp.int32, (group, voc), 1) + first_col
    hit = column == ids_ref[...]
    diff = z_base - z_edit
    pe = exp_edit * slope
    pb = exp_base * slope
    po = jnp.where(hit, slope, 0.0)

    high_e = pe.astype(bf16)
    high_b = pb.astype(bf16)
    ops_ref[:group] = high_e
    ops_ref[group : 2 * group] = high_b
    ops_ref[2 * group : 3 * group] = (pe - high_e.astype(f32)).astype(bf16)
    ops_ref[3 * group : 4 * group] = (pb - high_b.astype(f32)).astype(bf16)
    weight = cols_ref[:, 0:1] * cols_ref[:, 1:2]
    rest = jnp.sum(weight * po, axis=0, keepdims=True)
    sub = lax.broadcasted_iota(jnp.int32, (16, voc), 0)
    block = jnp.zeros((16, voc), f32)
    for i in range(3):
        piece = rest.astype(bf16).astype(f32)
        block = jnp.where(sub == i, piece, block)
        rest = rest - piece
    ops_ref[4 * group :] = block.astype(bf16)
    put_ops = pltpu.make_async_copy(ops_ref, ops_hbm, sems.at[1])
    put_ops.start()

    def total(a):
        return jnp.sum(a, axis=1, keepdims=True)

    sums = [
        total(exp_edit),
        total(exp_base),
        total(exp_base * diff),
        total(jnp.where(hit, diff, 0.0)),
        total(pe * pre_edit),
        total(pb * pre_edit),
        total(po * pre_edit),
        total(pe * toward),
        total(pb * toward),
        total(po * toward),
    ]
    lane = lax.broadcasted_iota(jnp.int32, (group, 128), 1)
    first = jnp.zeros((group, 128), f32)
    second = jnp.zeros((group, 128), f32)
    for i in range(8):
        first = jnp.where(lane == i, sums[i], first)
    for i in range(8, 10):
        second = jnp.where(lane == i - 8, sums[i], second)
    straight = jnp.concatenate([first, second], axis=0)
    swapped = jnp.concatenate([first[half:], first[:half], second[half:], second[:half]], axis=0)
    table = jnp.where(lax.axis_index("rep") == 0, straight, swapped)
    table = table.T[:8]
    for p in range(slab_ref.shape[0]):
        slab_ref[p] = table
    put_slab = pltpu.make_async_copy(slab_ref, slab_hbm, sems.at[0])
    put_slab.start()

    put_slab.wait()
    put_ops.wait()


def outer_kernel(ops_hbm, head_hbm, outer_ref, ops_ref, head_ref, sems):
    both = outer_ref.shape[0] - 16
    part = outer_ref.shape[1] // (sems.shape[0] - 1)
    get = pltpu.make_async_copy(ops_hbm, ops_ref, sems.at[0])
    get.start()
    moves = []
    for i in range(outer_ref.shape[1] // part):
        span = pl.ds(i * part, part)
        source = head_hbm.at[span]
        moves.append(pltpu.make_async_copy(source, head_ref.at[span], sems.at[1 + i]))
    for move in moves:
        move.start()
    get.wait()
    for i, move in enumerate(moves):
        move.wait()
        c = i * part
        block = lax.dot_general(
            ops_ref[...],
            head_ref[c : c + part, :],
            (((1,), (1,)), ((), ())),
            preferred_element_type=f32,
        )
        outer_ref[:both, c : c + part] = block[:both] + block[both : 2 * both]
        outer_ref[both:, c : c + part] = block[2 * both :]


def close_kernel(nv, nm, theirs_ref, cols_ref, outer_ref, own_ref, all_ref, *refs):
    units = refs[:nm]
    slab_hbm, penalty_hbm, coeff_ref, pen_ref, pull_ref, vec_ref, slab_ref, second_ref, sems = refs[nm:]
    rows = own_ref.shape[1]
    feat = own_ref.shape[2] - 128
    model = outer_ref.shape[1]
    group = 2 * nv * rows
    half = group // 2
    tiles = feat // 128
    v_i = lax.axis_index("vocab")
    m_i = lax.axis_index("mp")
    r_i = lax.axis_index("rep")

    table = theirs_ref[0]
    for p in range(1, theirs_ref.shape[0]):
        table += theirs_ref[p]
    table = jnp.concatenate([table, jnp.zeros((120, 128), f32)], axis=0).T
    first = table[:group]
    second = table[group:]
    swap_first = jnp.concatenate([first[half:], first[:half]], axis=0)
    swap_second = jnp.concatenate([second[half:], second[:half]], axis=0)
    first = jnp.where(r_i == 0, first, swap_first)
    second = jnp.where(r_i == 0, second, swap_second)
    se, sb, kl, gap, ae, ab, ao, te = [first[:, i : i + 1] for i in range(8)]
    tb, to = second[:, 0:1], second[:, 1:2]
    mix = cols_ref[:, 0:1]
    scale = cols_ref[:, 1:2]
    along = cols_ref[:, 2:3]
    inv_e = 2.0 / se
    inv_b = 1.0 / sb
    align = ae * inv_e - ab * inv_b - ao
    proj = te * inv_e - tb * inv_b - to
    penalty = kl * inv_b + gap + 2.0 * (jnp.log(se) - jnp.log(sb))
    shrink = scale * align / model
    coeff = scale * proj - shrink * (scale * along)
    weight = mix * scale
    pull = weight * shrink
    coeff_ref[...] = jnp.broadcast_to(coeff, (group, 128))
    pen_ref[...] = jnp.broadcast_to(penalty, (group, 128))
    put_pen = pltpu.make_async_copy(
        pen_ref.at[pl.ds(pl.multiple_of(v_i * rows, rows), rows)], penalty_hbm, sems.at[0]
    )
    put_pen.start()

    pull_ref[...] = jnp.broadcast_to(pull, (group, 128))
    pulls = pull_ref[pl.ds(pl.multiple_of(v_i * rows, rows), rows), :]
    pull_ref[...] = jnp.broadcast_to(pull * mix, (group, 128))
    pulled = jnp.sum(pull_ref[pl.ds(pl.multiple_of(v_i * rows, rows), rows), :], axis=0, keepdims=True)
    for t in range(tiles):
        part = own_ref[v_i * nm + m_i, :, t * 128 : (t + 1) * 128].astype(f32) * pulls
        second_ref[t : t + 1, :] = (
            jnp.sum(part, axis=0, keepdims=True) + pulled * all_ref[m_i, 0, t : t + 1, :]
        )

    own = [
        coeff_ref[pl.ds(pl.multiple_of((k * nv + v_i) * rows, rows), rows), :] for k in range(2)
    ]
    for k in range(nm):
        m = lax.rem(m_i - k + nm, nm)
        for t in range(units[0].shape[1] // 128):
            c = t * 128
            row = units[k][:rows, c : c + 128].astype(f32) * own[0]
            row += units[k][rows:, c : c + 128].astype(f32) * own[1]
            vec_ref[m, pl.ds(tiles + t, 1), :] = jnp.sum(row, axis=0, keepdims=True)
    by_e = jnp.broadcast_to(weight * inv_e, (group, 128))
    by_b = jnp.broadcast_to(weight * inv_b, (group, 128))
    puts = []
    for m in range(nm):
        for t in range(tiles):
            d = m * feat + t * 128
            plus = outer_ref[:group, d : d + 128] * by_e
            less = outer_ref[group : 2 * group, d : d + 128] * by_b
            row = jnp.sum(plus - less, axis=0, keepdims=True)
            row -= jnp.sum(outer_ref[2 * group :, d : d + 128], axis=0, keepdims=True)
            row = row * all_ref[m, 1, t : t + 1, :] - jnp.where(
                m_i == m, second_ref[t : t + 1, :], 0.0
            )
            vec_ref[m, t : t + 1, :] = row
        block = vec_ref[m].astype(bf16)
        for v in range(nv):
            for r in range(2):
                slab_ref[m, 2 * v + r] = block
        for v in range(nv):
            put = pltpu.make_async_copy(
                slab_ref.at[m, pl.ds(2 * v, 2)],
                slab_hbm.at[pl.ds((v * nm + m) * 2, 2)],
                sems.at[1 + v * nm + m],
            )
            put.start()
            puts.append(put)
    put_pen.wait()
    for put in puts:
        put.wait()


def sum_kernel(back_ref, in_ref, out_ref):
    peers = back_ref.shape[0]
    tiles = out_ref.shape[0]
    units = back_ref.shape[1] - tiles
    pieces = in_ref.shape[0] // units
    wide = jnp.zeros((tiles, 128), f32)
    for q in range(pieces):
        total = back_ref[q].astype(f32)
        for p in range(q + pieces, peers, pieces):
            total += back_ref[p].astype(f32)
        wide += total[:tiles]
        in_ref[q * units : (q + 1) * units, :] = total[tiles:]
    out_ref[...] = wide


def in_hbm(value):
    return pltpu.with_memory_space_constraint(value, pltpu.HBM)


def call(kernel, out_shape, scratch=(), megabytes=6, **more):
    return pl.pallas_call(
        kernel,
        out_shape=out_shape,
        scratch_shapes=scratch,
        compiler_params=pltpu.CompilerParams(vmem_limit_bytes=megabytes << 20),
        **more,
    )


def fused(nv, nm, nr, resid_base, mlp_hidden, edit_in, edit_out, norm_gain, head, token_ids):
    rows, feat = resid_base.shape
    hidden = mlp_hidden.shape[1]
    model, voc = head.shape
    group = nv * nr * rows
    peers = nv * nm * nr
    quarter = hidden // (nm * nr)
    everyone = ("vocab", "mp", "rep")
    m_i = lax.axis_index("mp")
    r_i = lax.axis_index("rep")
    shape = jax.ShapeDtypeStruct

    tiles = feat // 128
    hbm = pl.BlockSpec(memory_space=pltpu.HBM)
    vmem = pl.BlockSpec(memory_space=pltpu.VMEM)
    out_tiles = edit_out.reshape(tiles, 128)
    gain_tiles = norm_gain.reshape(tiles, 128)

    packed, vectors, keep, give = call(
        functools.partial(send_kernel, nv * nm, nm),
        (
            pltpu.HBM((nv * nm, rows, feat + 128), bf16),
            shape((2, tiles, 128), f32),
        )
        + (shape((nm, rows, quarter), bf16),) * 2,
        [
            pltpu.VMEM((rows, feat), bf16),
            pltpu.VMEM((rows, hidden), bf16),
            pltpu.VMEM((1, hidden), f32),
            pltpu.VMEM((nv * nm, rows, feat), bf16),
            pltpu.VMEM((nv * nm, rows, 128), bf16),
            pltpu.SemaphoreType.DMA((7 + 2 * nm,)),
        ],
        in_specs=[hbm] * 5,
        out_specs=(hbm,) + (vmem,) * 3,
    )(
        *(
            in_hbm(a)
            for a in (resid_base, mlp_hidden, edit_in.reshape(1, hidden), out_tiles, gain_tiles)
        )
    )
    got = lax.all_to_all(packed, ("vocab", "mp"), 0, 0)
    other = lax.ppermute(got, "rep", [(0, 1), (1, 0)])
    took = lax.ppermute(give, "rep", [(0, 1), (1, 0)])
    units = [
        jnp.concatenate(
            [lax.dynamic_index_in_dim(a, (m_i + k) % nm, 0, keepdims=False) for a in (keep, took)]
        )
        for k in range(nm)
    ]
    vectors = from_peers(vectors, "mp", nm)
    first = model * 5 // 9
    staged = call(
        stage_kernel,
        pltpu.VMEM((first, voc), bf16),
        [pltpu.SemaphoreType.DMA((5,))],
        in_specs=[vmem, hbm],
        out_specs=vmem,
    )(took, in_hbm(head))
    vectors, units, staged = lax.optimization_barrier((vectors, units, staged))
    vectors = jnp.stack(in_order(vectors, m_i))
    half = group // 2
    unstaged, early, early_cols = call(
        functools.partial(early_kernel, nv, nm),
        (
            pltpu.VMEM((model - first, voc), bf16),
            shape((group + 16, voc), f32),
            shape((half, 128), f32),
        ),
        [pltpu.VMEM((group + 16, model), bf16), pltpu.SemaphoreType.DMA((4,))],
        8,
        in_specs=[vmem, vmem, vmem, hbm],
        out_specs=(vmem, vmem, vmem),
    )(got, vectors, staged, in_hbm(head))
    ids = token_ids.reshape(nv, nr, rows)
    ids = jnp.concatenate(
        [lax.dynamic_index_in_dim(ids, (r_i + k) % nr, 1, keepdims=False) for k in range(nr)]
    ).reshape(group, 1)

    slab, cols, ops = call(
        functools.partial(score_kernel, nv, nm),
        (
            pltpu.HBM((peers, 8, 128), f32),
            shape((group, 128), f32),
            pltpu.HBM((4 * group + 16, voc), bf16),
        ),
        [
            pltpu.VMEM((group, model), bf16),
            pltpu.VMEM((peers, 8, 128), f32),
            pltpu.VMEM((4 * group + 16, voc), bf16),
            pltpu.SemaphoreType.DMA((2,)),
        ],
        in_specs=[vmem] * 7,
        out_specs=(hbm, vmem, hbm),
    )(other, vectors, ids, staged, unstaged, early, early_cols)
    theirs = lax.all_to_all(slab, everyone, 0, 0)
    parts = 3
    outer = call(
        outer_kernel,
        shape((2 * group + 16, model), f32),
        [
            pltpu.VMEM((4 * group + 16, voc), bf16),
            pltpu.VMEM((model, voc), bf16),
            pltpu.SemaphoreType.DMA((1 + parts,)),
        ],
        12,
        in_specs=[hbm, hbm],
    )(in_hbm(ops), in_hbm(head))

    moves = [[(m, (m + k) % nm) for m in range(nm)] for k in range(nm)]
    units = [units[0]] + [lax.ppermute(units[k], "mp", moves[k]) for k in range(1, nm)]

    width = (feat + quarter) // 128
    slab, penalty = call(
        functools.partial(close_kernel, nv, nm),
        (pltpu.HBM((peers, width, 128), bf16), pltpu.HBM((rows, 128), f32)),
        [
            pltpu.VMEM((group, 128), f32),
            pltpu.VMEM((group, 128), f32),
            pltpu.VMEM((group, 128), f32),
            pltpu.VMEM((nm, width, 128), f32),
            pltpu.VMEM((nm, 2 * nv, width, 128), bf16),
            pltpu.VMEM((tiles, 128), f32),
            pltpu.SemaphoreType.DMA((1 + nm * nv,)),
        ],
        in_specs=[vmem] * (5 + nm),
        out_specs=(hbm, hbm),
    )(theirs, cols, outer, got, vectors, *units)
    back = lax.all_to_all(slab, everyone, 0, 0)
    grad_in, grad_out = call(
        sum_kernel, (shape((hidden // 128, 128), f32), shape((tiles, 128), f32))
    )(back)
    return (penalty[:, 0], grad_in.reshape(hidden), grad_out.reshape(feat))


def local(nv, nm, nr, resid_base, mlp_hidden, *rest):
    rows, feat = resid_base.shape
    quarter = mlp_hidden.shape[1] // (nm * nr)
    whole_tiles = rows == 8 and feat % 128 == 0 and quarter % 128 == 0
    small = nr == 2 and nv % 2 == 0 and nv * nr * rows == 64
    step = fused if whole_tiles and small else plain
    return step(nv, nm, nr, resid_base, mlp_hidden, *rest)


def solution(mesh):
    in_specs = (
        P(("parts", "vocab", "rep"), "mp"),
        P(("parts", "vocab", "rep"), "mp"),
        P(("parts", "mp")),
        P(("parts", "mp")),
        P("mp"),
        P(None, ("vocab", "mp", "rep")),
        P("parts"),
    )
    out_specs = (P(("parts", "vocab", "rep")), P(("parts", "mp")), P(("parts", "mp")))
    step = functools.partial(local, mesh.shape["vocab"], mesh.shape["mp"], mesh.shape["rep"])
    return jax.shard_map(step, mesh=mesh, in_specs=in_specs, out_specs=out_specs, check_vma=False)
```

```python
import functools

import jax
import jax.numpy as jnp
from jax import lax
from jax.experimental import pallas as pl
from jax.experimental.pallas import tpu as pltpu
from jax.sharding import PartitionSpec as P

softcap = 30.0
epsilon = 1e-06
bf16 = jnp.bfloat16
f32 = jnp.float32


def split_bf16(value, pieces):
    out = []
    for _ in range(pieces):
        part = lax.reduce_precision(value, 8, 7)
        out.append(part.astype(bf16))
        value = value - part
    return out


def from_peers(value, axis, size):
    moves = [[(i, (i + k) % size) for i in range(size)] for k in range(size)]
    return [value] + [lax.ppermute(value, axis, moves[k]) for k in range(1, size)]


def to_peers(pick, axis, size, index):
    moves = [[(i, (i + k) % size) for i in range(size)] for k in range(size)]
    return [pick(index)] + [
        lax.ppermute(pick((index + k) % size), axis, moves[k]) for k in range(1, size)
    ]


def in_order(values, index):
    size = len(values)
    ordered = []
    for j in range(size):
        value = values[0]
        for k in range(1, size):
            value = jnp.where((index - j) % size == k, values[k], value)
        ordered.append(value)
    return ordered


def plain(nv, nm, nr, resid_base, mlp_hidden, edit_in, edit_out, norm_gain, head, token_ids):
    rows, feat = resid_base.shape
    hidden = mlp_hidden.shape[1]
    model, voc = head.shape
    group = nv * nr * rows
    peers = nv * nm * nr
    quarter = hidden // (nm * nr)
    everyone = ("vocab", "mp", "rep")

    v_i = lax.axis_index("vocab")
    m_i = lax.axis_index("mp")
    r_i = lax.axis_index("rep")

    vectors = from_peers(jnp.stack([edit_out, norm_gain]), "mp", nm)
    vectors = jnp.concatenate(in_order(vectors, m_i), axis=1)
    out_all = vectors[0]
    gain_all = vectors[1]

    units = mlp_hidden.reshape(rows, nm, nr, quarter)
    units = jnp.concatenate(
        [
            part
            for part in to_peers(
                lambda r: lax.dynamic_index_in_dim(units, r, 2, keepdims=False), "rep", nr, r_i
            )
        ]
    )
    units = to_peers(
        lambda m: lax.dynamic_index_in_dim(units, m, 1, keepdims=False), "mp", nm, m_i
    )

    hidden_f = mlp_hidden.astype(f32)
    mix_part = jnp.sum(hidden_f * edit_in[None, :], axis=1)
    mix_cols = jnp.stack(split_bf16(mix_part, 3), axis=1)
    packed = jnp.concatenate([resid_base, jnp.pad(mix_cols, ((0, 0), (0, 125)))], axis=1)
    packed = jnp.broadcast_to(packed[None], (nv * nm, rows, feat + 128))
    got = lax.all_to_all(packed, ("vocab", "mp"), 0, 0)
    got = jnp.concatenate(in_order(from_peers(got, "rep", nr), r_i)).reshape(nr * nv, nm, rows, feat + 128)

    base = jnp.concatenate([got[:, m, :, :feat].reshape(group, feat) for m in range(nm)], axis=1)
    base_f = base.astype(f32)
    mix = jnp.sum(got[:, :, :, feat : feat + 3].astype(f32), axis=(1, 3)).reshape(group)
    resid = base_f + mix[:, None] * out_all[None, :]
    edit_scale = lax.rsqrt(jnp.mean(resid * resid, axis=1) + epsilon)
    base_scale = lax.rsqrt(jnp.mean(base_f * base_f, axis=1) + epsilon)
    along = jnp.sum(resid * out_all[None, :], axis=1)
    x_edit = (resid * edit_scale[:, None] * gain_all[None, :]).astype(bf16)
    x_base = (base_f * base_scale[:, None] * gain_all[None, :]).astype(bf16)
    direction = jnp.stack(split_bf16(out_all * gain_all, 3) + [jnp.zeros((model,), bf16)] * 5)
    pre = jnp.dot(
        jnp.concatenate([x_edit, x_base, direction]), head, preferred_element_type=f32
    )
    pre_edit = pre[:group]
    pre_base = pre[group : 2 * group]
    toward = jnp.sum(pre[2 * group :], axis=0)
    z_edit = softcap * jnp.tanh(pre_edit / softcap)
    z_base = softcap * jnp.tanh(pre_base / softcap)
    slope = 1.0 - (z_edit / softcap) ** 2
    exp_edit = jnp.exp(z_edit)
    exp_base = jnp.exp(z_base)
    ids = token_ids.reshape(nv, nr, rows).transpose(1, 0, 2).reshape(group)
    first_col = lax.axis_index(everyone) * voc
    onehot = (ids[:, None] == (first_col + jnp.arange(voc, dtype=jnp.int32))[None, :]).astype(f32)
    diff = z_base - z_edit
    pe = exp_edit * slope
    pb = exp_base * slope
    po = onehot * slope
    sums = jnp.stack(
        [
            jnp.sum(a, axis=1)
            for a in (
                exp_edit,
                exp_base,
                exp_base * diff,
                onehot * diff,
                pe * pre_edit,
                pb * pre_edit,
                po * pre_edit,
                pe * toward[None, :],
                pb * toward[None, :],
                po * toward[None, :],
            )
        ]
    )
    weight = mix * edit_scale
    wo = jnp.sum(weight[:, None] * po, axis=0)
    high_e, low_e = split_bf16(pe, 2)
    high_b, low_b = split_bf16(pb, 2)
    tail = jnp.stack(split_bf16(wo, 3) + [jnp.zeros((voc,), bf16)] * 5)
    outer = lax.dot_general(
        jnp.concatenate([high_e, high_b, low_e, low_b, tail]),
        head,
        (((1,), (1,)), ((), ())),
        preferred_element_type=f32,
    )
    rows_e = outer[:group] + outer[2 * group : 3 * group]
    rows_b = outer[group : 2 * group] + outer[3 * group : 4 * group]
    row_o = jnp.sum(outer[4 * group :], axis=0)
    flat = 10 * group
    padded = -(-flat // 1024) * 1024
    mine = jnp.pad(sums.reshape(flat), (0, padded - flat)).reshape(padded // 128, 128)
    theirs = lax.all_to_all(
        jnp.broadcast_to(mine[None], (peers, padded // 128, 128)), everyone, 0, 0
    )
    sums = jnp.sum(theirs, axis=0).reshape(padded)[:flat].reshape(10, group)
    se, sb, kl, gap, ae, ab, ao, te, tb, to = [sums[i] for i in range(10)]
    inv_e = 2.0 / se
    inv_b = 1.0 / sb
    align = ae * inv_e - ab * inv_b - ao
    proj = te * inv_e - tb * inv_b - to
    penalty = kl * inv_b + gap + 2.0 * (jnp.log(se) - jnp.log(sb))
    shrink = edit_scale * align / model
    coeff = edit_scale * proj - shrink * (edit_scale * along)
    weighted = jnp.sum((weight * inv_e)[:, None] * rows_e, axis=0) - jnp.sum((weight * inv_b)[:, None] * rows_b, axis=0) - row_o
    w_hi, w_lo = split_bf16(weighted, 2)
    mine = lax.dynamic_index_in_dim(coeff.reshape(nr, nv, rows), v_i, 1, keepdims=False)
    own = jnp.concatenate([lax.dynamic_index_in_dim(mine, (r_i - k) % nr, 0, keepdims=False) for k in range(nr)])
    part_in = [jnp.sum(u.astype(f32) * own[:, None], axis=0) for u in units]
    part_in = jnp.stack(in_order(part_in, m_i)).astype(bf16)
    slab = jnp.concatenate([w_hi.reshape(nm, feat), w_lo.reshape(nm, feat), part_in], axis=1)
    width = 2 * feat + quarter
    if width % 128 == 0:
        slab = slab.reshape(nm, width // 128, 128)
    slab = jnp.broadcast_to(slab[None, :, None], (nv, nm, nr) + slab.shape[1:])
    back = lax.all_to_all(slab.reshape((peers,) + slab.shape[3:]), everyone, 0, 0)
    back = back.reshape(nv, nm * nr, width).astype(f32)
    grad_in = jnp.sum(back[:, :, 2 * feat :], axis=0).reshape(hidden)
    weighted_own = jnp.sum(back[:, :, :feat] + back[:, :, feat : 2 * feat], axis=(0, 1))
    pull = mix * shrink * edit_scale
    base_own = lax.dynamic_slice_in_dim(base, m_i * feat, feat, 1).astype(f32)
    second = jnp.sum(pull[:, None] * base_own, axis=0) + jnp.sum(pull * mix) * edit_out
    grad_out = norm_gain * weighted_own - second
    penalty = lax.dynamic_slice(penalty.reshape(nr, nv, rows), (r_i, v_i, 0), (1, 1, rows))
    return (penalty.reshape(rows), grad_in, grad_out)


def send_kernel(copies, pieces, base_hbm, hidden_hbm, in_hbm, out_hbm, gain_hbm, packed_hbm, vec_ref, *refs):
    unit_refs = refs[:2]
    base_ref, hidden_ref, in_ref, packed_ref, mix_ref, sems = refs[2:]
    rows, hidden = hidden_ref.shape
    feat = base_ref.shape[1]
    quarter = hidden // (2 * pieces)
    get_hidden = pltpu.make_async_copy(hidden_hbm, hidden_ref, sems.at[0])
    get_in = pltpu.make_async_copy(in_hbm, in_ref, sems.at[1])
    get_base = pltpu.make_async_copy(base_hbm, base_ref, sems.at[2])
    later = [
        pltpu.make_async_copy(out_hbm, vec_ref.at[0], sems.at[3]),
        pltpu.make_async_copy(gain_hbm, vec_ref.at[1], sems.at[4]),
    ]
    r_i = lax.axis_index("rep")
    for i in range(pieces):
        for j in range(2):
            start = pl.multiple_of((2 * i + lax.rem(r_i + j, 2)) * quarter, 128)
            later.append(
                pltpu.make_async_copy(
                    hidden_hbm.at[:, pl.ds(start, quarter)],
                    unit_refs[j].at[i],
                    sems.at[7 + 2 * i + j],
                )
            )
    get_base.start()
    get_hidden.start()
    get_in.start()
    for move in later:
        move.start()
    get_base.wait()
    for i in range(copies):
        packed_ref[i] = base_ref[...]
    put_base = pltpu.make_async_copy(packed_ref, packed_hbm.at[:, :, pl.ds(0, feat)], sems.at[5])
    put_base.start()
    get_hidden.wait()
    get_in.wait()
    totals = [jnp.zeros((rows, 128), f32)] * 8
    for i, c in enumerate(range(0, hidden, 128)):
        product = hidden_ref[:, c : c + 128].astype(f32) * in_ref[:, c : c + 128]
        totals[i % 8] = totals[i % 8] + product
    while len(totals) > 1:
        totals = [a + b for a, b in zip(totals[::2], totals[1::2])]
    mix = jnp.sum(totals[0], axis=1, keepdims=True)
    lane = lax.broadcasted_iota(jnp.int32, (rows, 128), 1)
    cols = jnp.zeros((rows, 128), f32)
    for i in range(3):
        piece = mix.astype(bf16).astype(f32)
        cols = jnp.where(lane == i, piece, cols)
        mix = mix - piece
    cols = cols.astype(bf16)
    for i in range(copies):
        mix_ref[i] = cols
    put_mix = pltpu.make_async_copy(mix_ref, packed_hbm.at[:, :, pl.ds(feat, 128)], sems.at[6])
    put_mix.start()
    for move in later:
        move.wait()
    put_base.wait()
    put_mix.wait()


def normed_rows(nv, nm, got_ref, vec_ref, cols_ref, x_ref):
    rows = got_ref.shape[1]
    feat = got_ref.shape[2] - 128
    model = nm * feat
    half = nv * rows
    pair = 2 * rows
    lane = lax.broadcasted_iota(jnp.int32, (pair, 128), 1)
    for v in range(0, nv, 2):
        at = v * rows

        def tile(m, c):
            first = got_ref[v * nm + m, :, c : c + 128].astype(f32)
            second = got_ref[(v + 1) * nm + m, :, c : c + 128].astype(f32)
            return jnp.concatenate([first, second], axis=0)

        mixed = tile(0, feat)
        for m in range(1, nm):
            mixed += tile(m, feat)
        mix = jnp.sum(mixed, axis=1, keepdims=True)
        mix_b = jnp.broadcast_to(mix, (pair, 128))
        sq_b = jnp.zeros((pair, 128), f32)
        sq_e = jnp.zeros((pair, 128), f32)
        dot_o = jnp.zeros((pair, 128), f32)
        for m in range(nm):
            for c in range(0, feat, 128):
                out = vec_ref[m, 0, c // 128 : c // 128 + 1, :]
                b = tile(m, c)
                e = b + mix_b * out
                sq_b += b * b
                sq_e += e * e
                dot_o += e * out
        scale_e = lax.rsqrt(jnp.sum(sq_e, axis=1, keepdims=True) / model + epsilon)
        scale_b = lax.rsqrt(jnp.sum(sq_b, axis=1, keepdims=True) / model + epsilon)
        along = jnp.sum(dot_o, axis=1, keepdims=True)
        cols_ref[at : at + pair, :] = jnp.where(
            lane == 0, mix, jnp.where(lane == 1, scale_e, jnp.where(lane == 2, along, 0.0))
        )
        scale_e = jnp.broadcast_to(scale_e, (pair, 128))
        scale_b = jnp.broadcast_to(scale_b, (pair, 128))
        for m in range(nm):
            for c in range(0, feat, 128):
                d = m * feat + c
                t = c // 128
                out = vec_ref[m, 0, t : t + 1, :]
                gain = vec_ref[m, 1, t : t + 1, :]
                b = tile(m, c)
                e = b + mix_b * out
                x_ref[at : at + pair, d : d + 128] = (e * scale_e * gain).astype(bf16)
                x_ref[half + at : half + at + pair, d : d + 128] = (b * scale_b * gain).astype(bf16)


def stage_kernel(after_ref, head_hbm, head_ref, sems):
    part = head_ref.shape[0] // sems.shape[0]
    moves = []
    for i in range(sems.shape[0]):
        span = pl.ds(i * part, part)
        moves.append(pltpu.make_async_copy(head_hbm.at[span], head_ref.at[span], sems.at[i]))
        moves[i].start()
    for move in moves:
        move.wait()


def early_kernel(nv, nm, own_ref, vec_ref, staged_ref, head_hbm, head_ref, pre_ref, cols_ref, x_ref, sems):
    model = head_hbm.shape[0]
    first = staged_ref.shape[0]
    part = (model - first) // sems.shape[0]
    moves = []
    for i in range(sems.shape[0]):
        move = pltpu.make_async_copy(
            head_hbm.at[pl.ds(first + i * part, part)],
            head_ref.at[pl.ds(i * part, part)],
            sems.at[i],
        )
        move.start()
        moves.append(move)
    feat = own_ref.shape[2] - 128
    half = cols_ref.shape[0]
    normed_rows(nv, nm, own_ref, vec_ref, cols_ref, x_ref)
    sub = lax.broadcasted_iota(jnp.int32, (16, 128), 0)
    for d in range(0, model, 128):
        m, t = d // feat, d % feat // 128
        rest = vec_ref[m, 0, t : t + 1, :] * vec_ref[m, 1, t : t + 1, :]
        block = jnp.zeros((16, 128), f32)
        for i in range(3):
            piece = rest.astype(bf16).astype(f32)
            block = jnp.where(sub == i, piece, block)
            rest = rest - piece
        x_ref[2 * half :, d : d + 128] = block.astype(bf16)
    pre = jnp.dot(x_ref[:, :first], staged_ref[...], preferred_element_type=f32)
    for i, move in enumerate(moves):
        move.wait()
        at = i * part
        pre += jnp.dot(
            x_ref[:, first + at : first + at + part],
            head_ref[at : at + part, :],
            preferred_element_type=f32,
        )
    pre_ref[...] = pre


def score_kernel(nv, nm, other_ref, vec_ref, ids_ref, staged_ref, head_ref, early_ref, early_cols_ref, slab_hbm, cols_ref, ops_hbm, x_ref, slab_ref, ops_ref, sems):
    voc = head_ref.shape[1]
    half = early_cols_ref.shape[0]
    group = 2 * half
    cols_ref[:half] = early_cols_ref[...]
    normed_rows(nv, nm, other_ref, vec_ref, cols_ref.at[half:], x_ref)
    first = staged_ref.shape[0]
    late = jnp.dot(x_ref[:, :first], staged_ref[...], preferred_element_type=f32)
    late += jnp.dot(x_ref[:, first:], head_ref[...], preferred_element_type=f32)
    pre_edit = jnp.concatenate([early_ref[:half], late[:half]], axis=0)
    pre_base = jnp.concatenate([early_ref[half:group], late[half:]], axis=0)
    toward = jnp.sum(early_ref[group:], axis=0, keepdims=True)
    th = jnp.tanh(pre_edit / softcap)
    z_edit = softcap * th
    z_base = softcap * jnp.tanh(pre_base / softcap)
    slope = 1.0 - th * th
    exp_edit = jnp.exp(z_edit)
    exp_base = jnp.exp(z_base)
    first_col = lax.axis_index(("vocab", "mp", "rep")) * voc
    column = lax.broadcasted_iota(jnp.int32, (group, voc), 1) + first_col
    hit = column == ids_ref[...]
    diff = z_base - z_edit
    pe = exp_edit * slope
    pb = exp_base * slope
    po = jnp.where(hit, slope, 0.0)

    high_e = pe.astype(bf16)
    high_b = pb.astype(bf16)
    ops_ref[:group] = high_e
    ops_ref[group : 2 * group] = high_b
    ops_ref[2 * group : 3 * group] = (pe - high_e.astype(f32)).astype(bf16)
    ops_ref[3 * group : 4 * group] = (pb - high_b.astype(f32)).astype(bf16)
    weight = cols_ref[:, 0:1] * cols_ref[:, 1:2]
    rest = jnp.sum(weight * po, axis=0, keepdims=True)
    sub = lax.broadcasted_iota(jnp.int32, (16, voc), 0)
    block = jnp.zeros((16, voc), f32)
    for i in range(3):
        piece = rest.astype(bf16).astype(f32)
        block = jnp.where(sub == i, piece, block)
        rest = rest - piece
    ops_ref[4 * group :] = block.astype(bf16)
    put_ops = pltpu.make_async_copy(ops_ref, ops_hbm, sems.at[1])
    put_ops.start()

    def total(a):
        return jnp.sum(a, axis=1, keepdims=True)

    sums = [
        total(exp_edit),
        total(exp_base),
        total(exp_base * diff),
        total(jnp.where(hit, diff, 0.0)),
        total(pe * pre_edit),
        total(pb * pre_edit),
        total(po * pre_edit),
        total(pe * toward),
        total(pb * toward),
        total(po * toward),
    ]
    lane = lax.broadcasted_iota(jnp.int32, (group, 128), 1)
    first = jnp.zeros((group, 128), f32)
    second = jnp.zeros((group, 128), f32)
    for i in range(8):
        first = jnp.where(lane == i, sums[i], first)
    for i in range(8, 10):
        second = jnp.where(lane == i - 8, sums[i], second)
    straight = jnp.concatenate([first, second], axis=0)
    swapped = jnp.concatenate([first[half:], first[:half], second[half:], second[:half]], axis=0)
    table = jnp.where(lax.axis_index("rep") == 0, straight, swapped)
    table = table.T[:8]
    for p in range(slab_ref.shape[0]):
        slab_ref[p] = table
    put_slab = pltpu.make_async_copy(slab_ref, slab_hbm, sems.at[0])
    put_slab.start()

    put_slab.wait()
    put_ops.wait()


def outer_kernel(ops_hbm, head_hbm, outer_ref, ops_ref, head_ref, sems):
    both = outer_ref.shape[0] - 16
    part = outer_ref.shape[1] // (sems.shape[0] - 1)
    get = pltpu.make_async_copy(ops_hbm, ops_ref, sems.at[0])
    get.start()
    moves = []
    for i in range(outer_ref.shape[1] // part):
        span = pl.ds(i * part, part)
        source = head_hbm.at[span]
        moves.append(pltpu.make_async_copy(source, head_ref.at[span], sems.at[1 + i]))
    for move in moves:
        move.start()
    get.wait()
    for i, move in enumerate(moves):
        move.wait()
        c = i * part
        block = lax.dot_general(
            ops_ref[...],
            head_ref[c : c + part, :],
            (((1,), (1,)), ((), ())),
            preferred_element_type=f32,
        )
        outer_ref[:both, c : c + part] = block[:both] + block[both : 2 * both]
        outer_ref[both:, c : c + part] = block[2 * both :]


def close_kernel(nv, nm, theirs_ref, cols_ref, outer_ref, own_ref, all_ref, *refs):
    units = refs[:nm]
    slab_hbm, penalty_hbm, coeff_ref, pen_ref, pull_ref, vec_ref, slab_ref, second_ref, line_ref, sems = refs[nm:]
    rows = own_ref.shape[1]
    feat = own_ref.shape[2] - 128
    model = outer_ref.shape[1]
    group = 2 * nv * rows
    half = group // 2
    tiles = feat // 128
    v_i = lax.axis_index("vocab")
    m_i = lax.axis_index("mp")
    r_i = lax.axis_index("rep")

    table = theirs_ref[0]
    for p in range(1, theirs_ref.shape[0]):
        table += theirs_ref[p]
    table = jnp.concatenate([table, jnp.zeros((120, 128), f32)], axis=0).T
    first = table[:group]
    second = table[group:]
    swap_first = jnp.concatenate([first[half:], first[:half]], axis=0)
    swap_second = jnp.concatenate([second[half:], second[:half]], axis=0)
    first = jnp.where(r_i == 0, first, swap_first)
    second = jnp.where(r_i == 0, second, swap_second)
    se, sb, kl, gap, ae, ab, ao, te = [first[:, i : i + 1] for i in range(8)]
    tb, to = second[:, 0:1], second[:, 1:2]
    mix = cols_ref[:, 0:1]
    scale = cols_ref[:, 1:2]
    along = cols_ref[:, 2:3]
    inv_e = 2.0 / se
    inv_b = 1.0 / sb
    align = ae * inv_e - ab * inv_b - ao
    proj = te * inv_e - tb * inv_b - to
    penalty = kl * inv_b + gap + 2.0 * (jnp.log(se) - jnp.log(sb))
    shrink = scale * align / model
    coeff = scale * proj - shrink * (scale * along)
    weight = mix * scale
    pull = weight * shrink
    coeff_ref[...] = jnp.broadcast_to(coeff, (group, 128))
    pen_ref[...] = jnp.broadcast_to(penalty, (group, 128))
    mine = pen_ref[pl.ds(pl.multiple_of(v_i * rows, rows), rows), :]
    diagonal = lax.broadcasted_iota(jnp.int32, (rows, 128), 0) == lax.broadcasted_iota(
        jnp.int32, (rows, 128), 1
    )
    line_ref[...] = jnp.sum(jnp.where(diagonal, mine, 0.0), axis=0, keepdims=True)[:, :rows]
    put_pen = pltpu.make_async_copy(line_ref, penalty_hbm, sems.at[0])
    put_pen.start()

    pull_ref[...] = jnp.broadcast_to(pull, (group, 128))
    pulls = pull_ref[pl.ds(pl.multiple_of(v_i * rows, rows), rows), :]
    pull_ref[...] = jnp.broadcast_to(pull * mix, (group, 128))
    pulled = jnp.sum(pull_ref[pl.ds(pl.multiple_of(v_i * rows, rows), rows), :], axis=0, keepdims=True)
    for t in range(tiles):
        part = own_ref[v_i * nm + m_i, :, t * 128 : (t + 1) * 128].astype(f32) * pulls
        second_ref[t : t + 1, :] = (
            jnp.sum(part, axis=0, keepdims=True) + pulled * all_ref[m_i, 0, t : t + 1, :]
        )

    own = [
        coeff_ref[pl.ds(pl.multiple_of((k * nv + v_i) * rows, rows), rows), :] for k in range(2)
    ]
    for k in range(nm):
        m = lax.rem(m_i - k + nm, nm)
        for t in range(units[0].shape[1] // 128):
            c = t * 128
            row = units[k][:rows, c : c + 128].astype(f32) * own[0]
            row += units[k][rows:, c : c + 128].astype(f32) * own[1]
            vec_ref[m, pl.ds(tiles + t, 1), :] = jnp.sum(row, axis=0, keepdims=True)
    by_e = jnp.broadcast_to(weight * inv_e, (group, 128))
    by_b = jnp.broadcast_to(weight * inv_b, (group, 128))
    puts = []
    for m in range(nm):
        for t in range(tiles):
            d = m * feat + t * 128
            plus = outer_ref[:group, d : d + 128] * by_e
            less = outer_ref[group : 2 * group, d : d + 128] * by_b
            row = jnp.sum(plus - less, axis=0, keepdims=True)
            row -= jnp.sum(outer_ref[2 * group :, d : d + 128], axis=0, keepdims=True)
            row = row * all_ref[m, 1, t : t + 1, :] - jnp.where(
                m_i == m, second_ref[t : t + 1, :], 0.0
            )
            vec_ref[m, t : t + 1, :] = row
        slab_ref[m] = vec_ref[m].astype(bf16)
        for v in range(nv):
            put = pltpu.make_async_copy(
                slab_ref.at[m], slab_hbm.at[v * nm + m], sems.at[1 + v * nm + m]
            )
            put.start()
            puts.append(put)
    put_pen.wait()
    for put in puts:
        put.wait()


def sum_kernel(nm, back_ref, sums_ref):
    senders = back_ref.shape[0]
    units = (sums_ref.shape[0] - back_ref.shape[1]) // (nm - 1)
    tiles = back_ref.shape[1] - units
    wide = jnp.zeros((tiles, 128), f32)
    for m in range(nm):
        total = back_ref[m].astype(f32)
        for p in range(m + nm, senders, nm):
            total += back_ref[p].astype(f32)
        wide += total[:tiles]
        sums_ref[m * units : (m + 1) * units, :] = total[tiles:]
    sums_ref[nm * units :, :] = wide


def join_kernel(nm, own_ref, other_ref, in_ref, out_ref):
    units = in_ref.shape[0] // (2 * nm)
    even = lax.axis_index("rep") == 0
    for m in range(nm):
        own = own_ref[m * units : (m + 1) * units, :]
        other = other_ref[m * units : (m + 1) * units, :]
        at = 2 * m * units
        in_ref[at : at + units, :] = jnp.where(even, own, other)
        in_ref[at + units : at + 2 * units, :] = jnp.where(even, other, own)
    out_ref[...] = own_ref[nm * units :, :] + other_ref[nm * units :, :]


def in_hbm(value):
    return pltpu.with_memory_space_constraint(value, pltpu.HBM)


def call(kernel, out_shape, scratch=(), megabytes=6, **more):
    return pl.pallas_call(
        kernel,
        out_shape=out_shape,
        scratch_shapes=scratch,
        compiler_params=pltpu.CompilerParams(vmem_limit_bytes=megabytes << 20),
        **more,
    )


def fused(nv, nm, nr, resid_base, mlp_hidden, edit_in, edit_out, norm_gain, head, token_ids):
    rows, feat = resid_base.shape
    hidden = mlp_hidden.shape[1]
    model, voc = head.shape
    group = nv * nr * rows
    peers = nv * nm * nr
    quarter = hidden // (nm * nr)
    everyone = ("vocab", "mp", "rep")
    m_i = lax.axis_index("mp")
    r_i = lax.axis_index("rep")
    shape = jax.ShapeDtypeStruct

    tiles = feat // 128
    hbm = pl.BlockSpec(memory_space=pltpu.HBM)
    vmem = pl.BlockSpec(memory_space=pltpu.VMEM)
    out_tiles = edit_out.reshape(tiles, 128)
    gain_tiles = norm_gain.reshape(tiles, 128)

    packed, vectors, keep, give = call(
        functools.partial(send_kernel, nv * nm, nm),
        (
            pltpu.HBM((nv * nm, rows, feat + 128), bf16),
            shape((2, tiles, 128), f32),
        )
        + (shape((nm, rows, quarter), bf16),) * 2,
        [
            pltpu.VMEM((rows, feat), bf16),
            pltpu.VMEM((rows, hidden), bf16),
            pltpu.VMEM((1, hidden), f32),
            pltpu.VMEM((nv * nm, rows, feat), bf16),
            pltpu.VMEM((nv * nm, rows, 128), bf16),
            pltpu.SemaphoreType.DMA((7 + 2 * nm,)),
        ],
        in_specs=[hbm] * 5,
        out_specs=(hbm,) + (vmem,) * 3,
    )(
        *(
            in_hbm(a)
            for a in (resid_base, mlp_hidden, edit_in.reshape(1, hidden), out_tiles, gain_tiles)
        )
    )
    got = lax.all_to_all(packed, ("vocab", "mp"), 0, 0)
    other = lax.ppermute(got, "rep", [(0, 1), (1, 0)])
    took = lax.ppermute(give, "rep", [(0, 1), (1, 0)])
    units = [
        jnp.concatenate(
            [lax.dynamic_index_in_dim(a, (m_i + k) % nm, 0, keepdims=False) for a in (keep, took)]
        )
        for k in range(nm)
    ]
    vectors = from_peers(vectors, "mp", nm)
    first = model * 5 // 9
    staged = call(
        stage_kernel,
        pltpu.VMEM((first, voc), bf16),
        [pltpu.SemaphoreType.DMA((5,))],
        in_specs=[vmem, hbm],
        out_specs=vmem,
    )(took, in_hbm(head))
    vectors, units, staged = lax.optimization_barrier((vectors, units, staged))
    vectors = jnp.stack(in_order(vectors, m_i))
    half = group // 2
    unstaged, early, early_cols = call(
        functools.partial(early_kernel, nv, nm),
        (
            pltpu.VMEM((model - first, voc), bf16),
            shape((group + 16, voc), f32),
            shape((half, 128), f32),
        ),
        [pltpu.VMEM((group + 16, model), bf16), pltpu.SemaphoreType.DMA((4,))],
        8,
        in_specs=[vmem, vmem, vmem, hbm],
        out_specs=(vmem, vmem, vmem),
    )(got, vectors, staged, in_hbm(head))
    ids = token_ids.reshape(nv, nr, rows)
    ids = jnp.concatenate(
        [lax.dynamic_index_in_dim(ids, (r_i + k) % nr, 1, keepdims=False) for k in range(nr)]
    ).reshape(group, 1)

    slab, cols, ops = call(
        functools.partial(score_kernel, nv, nm),
        (
            pltpu.HBM((peers, 8, 128), f32),
            shape((group, 128), f32),
            pltpu.HBM((4 * group + 16, voc), bf16),
        ),
        [
            pltpu.VMEM((group, model), bf16),
            pltpu.VMEM((peers, 8, 128), f32),
            pltpu.VMEM((4 * group + 16, voc), bf16),
            pltpu.SemaphoreType.DMA((2,)),
        ],
        in_specs=[vmem] * 7,
        out_specs=(hbm, vmem, hbm),
    )(other, vectors, ids, staged, unstaged, early, early_cols)
    theirs = lax.all_to_all(slab, everyone, 0, 0)
    parts = 3
    outer = call(
        outer_kernel,
        shape((2 * group + 16, model), f32),
        [
            pltpu.VMEM((4 * group + 16, voc), bf16),
            pltpu.VMEM((model, voc), bf16),
            pltpu.SemaphoreType.DMA((1 + parts,)),
        ],
        12,
        in_specs=[hbm, hbm],
    )(in_hbm(ops), in_hbm(head))

    moves = [[(m, (m + k) % nm) for m in range(nm)] for k in range(nm)]
    units = [units[0]] + [lax.ppermute(units[k], "mp", moves[k]) for k in range(1, nm)]

    width = (feat + quarter) // 128
    slab, penalty = call(
        functools.partial(close_kernel, nv, nm),
        (pltpu.HBM((nv * nm, width, 128), bf16), pltpu.HBM((1, rows), f32)),
        [
            pltpu.VMEM((group, 128), f32),
            pltpu.VMEM((group, 128), f32),
            pltpu.VMEM((group, 128), f32),
            pltpu.VMEM((nm, width, 128), f32),
            pltpu.VMEM((nm, width, 128), bf16),
            pltpu.VMEM((tiles, 128), f32),
            pltpu.VMEM((1, rows), f32),
            pltpu.SemaphoreType.DMA((1 + nm * nv,)),
        ],
        in_specs=[vmem] * (5 + nm),
        out_specs=(hbm, hbm),
    )(theirs, cols, outer, got, vectors, *units)
    back = lax.all_to_all(slab, ("vocab", "mp"), 0, 0)
    sums = call(
        functools.partial(sum_kernel, nm), shape((nm * quarter // 128 + tiles, 128), f32)
    )(back)
    others = lax.ppermute(sums, "rep", [(0, 1), (1, 0)])
    grad_in, grad_out = call(
        functools.partial(join_kernel, nm),
        (shape((hidden // 128, 128), f32), shape((tiles, 128), f32)),
    )(sums, others)
    return (penalty.reshape(rows), grad_in.reshape(hidden), grad_out.reshape(feat))


def local(nv, nm, nr, resid_base, mlp_hidden, *rest):
    rows, feat = resid_base.shape
    quarter = mlp_hidden.shape[1] // (nm * nr)
    whole_tiles = rows == 8 and feat % 128 == 0 and quarter % 128 == 0
    small = nr == 2 and nm > 1 and nv % 2 == 0 and nv * nr * rows == 64
    step = fused if whole_tiles and small else plain
    return step(nv, nm, nr, resid_base, mlp_hidden, *rest)


def solution(mesh):
    in_specs = (
        P(("parts", "vocab", "rep"), "mp"),
        P(("parts", "vocab", "rep"), "mp"),
        P(("parts", "mp")),
        P(("parts", "mp")),
        P("mp"),
        P(None, ("vocab", "mp", "rep")),
        P("parts"),
    )
    out_specs = (P(("parts", "vocab", "rep")), P(("parts", "mp")), P(("parts", "mp")))
    step = functools.partial(local, mesh.shape["vocab"], mesh.shape["mp"], mesh.shape["rep"])
    return jax.shard_map(step, mesh=mesh, in_specs=in_specs, out_specs=out_specs, check_vma=False)
```

```python
import functools

import jax
import jax.numpy as jnp
from jax import lax
from jax.experimental import pallas as pl
from jax.experimental.pallas import tpu as pltpu
from jax.sharding import PartitionSpec as P

softcap = 30.0
epsilon = 1e-06
bf16 = jnp.bfloat16
f32 = jnp.float32


def split_bf16(value, pieces):
    out = []
    for _ in range(pieces):
        part = lax.reduce_precision(value, 8, 7)
        out.append(part.astype(bf16))
        value = value - part
    return out


def from_peers(value, axis, size):
    moves = [[(i, (i + k) % size) for i in range(size)] for k in range(size)]
    return [value] + [lax.ppermute(value, axis, moves[k]) for k in range(1, size)]


def to_peers(pick, axis, size, index):
    moves = [[(i, (i + k) % size) for i in range(size)] for k in range(size)]
    return [pick(index)] + [
        lax.ppermute(pick((index + k) % size), axis, moves[k]) for k in range(1, size)
    ]


def in_order(values, index):
    size = len(values)
    ordered = []
    for j in range(size):
        value = values[0]
        for k in range(1, size):
            value = jnp.where((index - j) % size == k, values[k], value)
        ordered.append(value)
    return ordered


def plain(nv, nm, nr, resid_base, mlp_hidden, edit_in, edit_out, norm_gain, head, token_ids):
    rows, feat = resid_base.shape
    hidden = mlp_hidden.shape[1]
    model, voc = head.shape
    group = nv * nr * rows
    peers = nv * nm * nr
    quarter = hidden // (nm * nr)
    everyone = ("vocab", "mp", "rep")

    v_i = lax.axis_index("vocab")
    m_i = lax.axis_index("mp")
    r_i = lax.axis_index("rep")

    vectors = from_peers(jnp.stack([edit_out, norm_gain]), "mp", nm)
    vectors = jnp.concatenate(in_order(vectors, m_i), axis=1)
    out_all = vectors[0]
    gain_all = vectors[1]

    units = mlp_hidden.reshape(rows, nm, nr, quarter)
    units = jnp.concatenate(
        [
            part
            for part in to_peers(
                lambda r: lax.dynamic_index_in_dim(units, r, 2, keepdims=False), "rep", nr, r_i
            )
        ]
    )
    units = to_peers(
        lambda m: lax.dynamic_index_in_dim(units, m, 1, keepdims=False), "mp", nm, m_i
    )

    hidden_f = mlp_hidden.astype(f32)
    mix_part = jnp.sum(hidden_f * edit_in[None, :], axis=1)
    mix_cols = jnp.stack(split_bf16(mix_part, 3), axis=1)
    packed = jnp.concatenate([resid_base, jnp.pad(mix_cols, ((0, 0), (0, 125)))], axis=1)
    packed = jnp.broadcast_to(packed[None], (nv * nm, rows, feat + 128))
    got = lax.all_to_all(packed, ("vocab", "mp"), 0, 0)
    got = jnp.concatenate(in_order(from_peers(got, "rep", nr), r_i)).reshape(nr * nv, nm, rows, feat + 128)

    base = jnp.concatenate([got[:, m, :, :feat].reshape(group, feat) for m in range(nm)], axis=1)
    base_f = base.astype(f32)
    mix = jnp.sum(got[:, :, :, feat : feat + 3].astype(f32), axis=(1, 3)).reshape(group)
    resid = base_f + mix[:, None] * out_all[None, :]
    edit_scale = lax.rsqrt(jnp.mean(resid * resid, axis=1) + epsilon)
    base_scale = lax.rsqrt(jnp.mean(base_f * base_f, axis=1) + epsilon)
    along = jnp.sum(resid * out_all[None, :], axis=1)
    x_edit = (resid * edit_scale[:, None] * gain_all[None, :]).astype(bf16)
    x_base = (base_f * base_scale[:, None] * gain_all[None, :]).astype(bf16)
    direction = jnp.stack(split_bf16(out_all * gain_all, 3) + [jnp.zeros((model,), bf16)] * 5)
    pre = jnp.dot(
        jnp.concatenate([x_edit, x_base, direction]), head, preferred_element_type=f32
    )
    pre_edit = pre[:group]
    pre_base = pre[group : 2 * group]
    toward = jnp.sum(pre[2 * group :], axis=0)
    z_edit = softcap * jnp.tanh(pre_edit / softcap)
    z_base = softcap * jnp.tanh(pre_base / softcap)
    slope = 1.0 - (z_edit / softcap) ** 2
    exp_edit = jnp.exp(z_edit)
    exp_base = jnp.exp(z_base)
    ids = token_ids.reshape(nv, nr, rows).transpose(1, 0, 2).reshape(group)
    first_col = lax.axis_index(everyone) * voc
    onehot = (ids[:, None] == (first_col + jnp.arange(voc, dtype=jnp.int32))[None, :]).astype(f32)
    diff = z_base - z_edit
    pe = exp_edit * slope
    pb = exp_base * slope
    po = onehot * slope
    sums = jnp.stack(
        [
            jnp.sum(a, axis=1)
            for a in (
                exp_edit,
                exp_base,
                exp_base * diff,
                onehot * diff,
                pe * pre_edit,
                pb * pre_edit,
                po * pre_edit,
                pe * toward[None, :],
                pb * toward[None, :],
                po * toward[None, :],
            )
        ]
    )
    weight = mix * edit_scale
    wo = jnp.sum(weight[:, None] * po, axis=0)
    high_e, low_e = split_bf16(pe, 2)
    high_b, low_b = split_bf16(pb, 2)
    tail = jnp.stack(split_bf16(wo, 3) + [jnp.zeros((voc,), bf16)] * 5)
    outer = lax.dot_general(
        jnp.concatenate([high_e, high_b, low_e, low_b, tail]),
        head,
        (((1,), (1,)), ((), ())),
        preferred_element_type=f32,
    )
    rows_e = outer[:group] + outer[2 * group : 3 * group]
    rows_b = outer[group : 2 * group] + outer[3 * group : 4 * group]
    row_o = jnp.sum(outer[4 * group :], axis=0)
    flat = 10 * group
    padded = -(-flat // 1024) * 1024
    mine = jnp.pad(sums.reshape(flat), (0, padded - flat)).reshape(padded // 128, 128)
    theirs = lax.all_to_all(
        jnp.broadcast_to(mine[None], (peers, padded // 128, 128)), everyone, 0, 0
    )
    sums = jnp.sum(theirs, axis=0).reshape(padded)[:flat].reshape(10, group)
    se, sb, kl, gap, ae, ab, ao, te, tb, to = [sums[i] for i in range(10)]
    inv_e = 2.0 / se
    inv_b = 1.0 / sb
    align = ae * inv_e - ab * inv_b - ao
    proj = te * inv_e - tb * inv_b - to
    penalty = kl * inv_b + gap + 2.0 * (jnp.log(se) - jnp.log(sb))
    shrink = edit_scale * align / model
    coeff = edit_scale * proj - shrink * (edit_scale * along)
    weighted = jnp.sum((weight * inv_e)[:, None] * rows_e, axis=0) - jnp.sum((weight * inv_b)[:, None] * rows_b, axis=0) - row_o
    w_hi, w_lo = split_bf16(weighted, 2)
    mine = lax.dynamic_index_in_dim(coeff.reshape(nr, nv, rows), v_i, 1, keepdims=False)
    own = jnp.concatenate([lax.dynamic_index_in_dim(mine, (r_i - k) % nr, 0, keepdims=False) for k in range(nr)])
    part_in = [jnp.sum(u.astype(f32) * own[:, None], axis=0) for u in units]
    part_in = jnp.stack(in_order(part_in, m_i)).astype(bf16)
    slab = jnp.concatenate([w_hi.reshape(nm, feat), w_lo.reshape(nm, feat), part_in], axis=1)
    width = 2 * feat + quarter
    if width % 128 == 0:
        slab = slab.reshape(nm, width // 128, 128)
    slab = jnp.broadcast_to(slab[None, :, None], (nv, nm, nr) + slab.shape[1:])
    back = lax.all_to_all(slab.reshape((peers,) + slab.shape[3:]), everyone, 0, 0)
    back = back.reshape(nv, nm * nr, width).astype(f32)
    grad_in = jnp.sum(back[:, :, 2 * feat :], axis=0).reshape(hidden)
    weighted_own = jnp.sum(back[:, :, :feat] + back[:, :, feat : 2 * feat], axis=(0, 1))
    pull = mix * shrink * edit_scale
    base_own = lax.dynamic_slice_in_dim(base, m_i * feat, feat, 1).astype(f32)
    second = jnp.sum(pull[:, None] * base_own, axis=0) + jnp.sum(pull * mix) * edit_out
    grad_out = norm_gain * weighted_own - second
    penalty = lax.dynamic_slice(penalty.reshape(nr, nv, rows), (r_i, v_i, 0), (1, 1, rows))
    return (penalty.reshape(rows), grad_in, grad_out)


def send_kernel(copies, pieces, base_hbm, hidden_hbm, in_hbm, out_hbm, gain_hbm, packed_hbm, vec_ref, *refs):
    unit_refs = refs[:2]
    base_ref, hidden_ref, in_ref, packed_ref, mix_ref, sems = refs[2:]
    rows, hidden = hidden_ref.shape
    feat = base_ref.shape[1]
    quarter = hidden // (2 * pieces)
    get_hidden = pltpu.make_async_copy(hidden_hbm, hidden_ref, sems.at[0])
    get_in = pltpu.make_async_copy(in_hbm, in_ref, sems.at[1])
    get_base = pltpu.make_async_copy(base_hbm, base_ref, sems.at[2])
    later = [
        pltpu.make_async_copy(out_hbm, vec_ref.at[0], sems.at[3]),
        pltpu.make_async_copy(gain_hbm, vec_ref.at[1], sems.at[4]),
    ]
    r_i = lax.axis_index("rep")
    for i in range(pieces):
        for j in range(2):
            start = pl.multiple_of((2 * i + lax.rem(r_i + j, 2)) * quarter, 128)
            later.append(
                pltpu.make_async_copy(
                    hidden_hbm.at[:, pl.ds(start, quarter)],
                    unit_refs[j].at[i],
                    sems.at[7 + 2 * i + j],
                )
            )
    get_base.start()
    get_hidden.start()
    get_in.start()
    for move in later:
        move.start()
    get_base.wait()
    for i in range(copies):
        packed_ref[i] = base_ref[...]
    put_base = pltpu.make_async_copy(packed_ref, packed_hbm.at[:, :, pl.ds(0, feat)], sems.at[5])
    put_base.start()
    get_hidden.wait()
    get_in.wait()
    totals = [jnp.zeros((rows, 128), f32)] * 8
    for i, c in enumerate(range(0, hidden, 128)):
        product = hidden_ref[:, c : c + 128].astype(f32) * in_ref[:, c : c + 128]
        totals[i % 8] = totals[i % 8] + product
    while len(totals) > 1:
        totals = [a + b for a, b in zip(totals[::2], totals[1::2])]
    mix = jnp.sum(totals[0], axis=1, keepdims=True)
    lane = lax.broadcasted_iota(jnp.int32, (rows, 128), 1)
    cols = jnp.zeros((rows, 128), f32)
    for i in range(3):
        piece = mix.astype(bf16).astype(f32)
        cols = jnp.where(lane == i, piece, cols)
        mix = mix - piece
    cols = cols.astype(bf16)
    for i in range(copies):
        mix_ref[i] = cols
    put_mix = pltpu.make_async_copy(mix_ref, packed_hbm.at[:, :, pl.ds(feat, 128)], sems.at[6])
    put_mix.start()
    for move in later:
        move.wait()
    put_base.wait()
    put_mix.wait()


def normed_rows(nv, nm, got_ref, vec_ref, cols_ref, x_ref):
    rows = got_ref.shape[1]
    feat = got_ref.shape[2] - 128
    model = nm * feat
    half = nv * rows
    pair = 2 * rows
    lane = lax.broadcasted_iota(jnp.int32, (pair, 128), 1)
    for v in range(0, nv, 2):
        at = v * rows

        def tile(m, c):
            first = got_ref[v * nm + m, :, c : c + 128].astype(f32)
            second = got_ref[(v + 1) * nm + m, :, c : c + 128].astype(f32)
            return jnp.concatenate([first, second], axis=0)

        mixed = tile(0, feat)
        for m in range(1, nm):
            mixed += tile(m, feat)
        mix = jnp.sum(mixed, axis=1, keepdims=True)
        mix_b = jnp.broadcast_to(mix, (pair, 128))
        sq_b = jnp.zeros((pair, 128), f32)
        sq_e = jnp.zeros((pair, 128), f32)
        dot_o = jnp.zeros((pair, 128), f32)
        for m in range(nm):
            for c in range(0, feat, 128):
                out = vec_ref[m, 0, c // 128 : c // 128 + 1, :]
                b = tile(m, c)
                e = b + mix_b * out
                sq_b += b * b
                sq_e += e * e
                dot_o += e * out
        scale_e = lax.rsqrt(jnp.sum(sq_e, axis=1, keepdims=True) / model + epsilon)
        scale_b = lax.rsqrt(jnp.sum(sq_b, axis=1, keepdims=True) / model + epsilon)
        along = jnp.sum(dot_o, axis=1, keepdims=True)
        cols_ref[at : at + pair, :] = jnp.where(
            lane == 0, mix, jnp.where(lane == 1, scale_e, jnp.where(lane == 2, along, 0.0))
        )
        scale_e = jnp.broadcast_to(scale_e, (pair, 128))
        scale_b = jnp.broadcast_to(scale_b, (pair, 128))
        for m in range(nm):
            for c in range(0, feat, 128):
                d = m * feat + c
                t = c // 128
                out = vec_ref[m, 0, t : t + 1, :]
                gain = vec_ref[m, 1, t : t + 1, :]
                b = tile(m, c)
                e = b + mix_b * out
                x_ref[at : at + pair, d : d + 128] = (e * scale_e * gain).astype(bf16)
                x_ref[half + at : half + at + pair, d : d + 128] = (b * scale_b * gain).astype(bf16)


def stage_kernel(after_ref, head_hbm, head_ref, sems):
    part = head_ref.shape[0] // sems.shape[0]
    moves = []
    for i in range(sems.shape[0]):
        span = pl.ds(i * part, part)
        moves.append(pltpu.make_async_copy(head_hbm.at[span], head_ref.at[span], sems.at[i]))
        moves[i].start()
    for move in moves:
        move.wait()


def early_kernel(nv, nm, own_ref, vec_ref, staged_ref, head_hbm, head_ref, pre_ref, cols_ref, x_ref, sems):
    model = head_hbm.shape[0]
    first = staged_ref.shape[0]
    part = (model - first) // sems.shape[0]
    moves = []
    for i in range(sems.shape[0]):
        move = pltpu.make_async_copy(
            head_hbm.at[pl.ds(first + i * part, part)],
            head_ref.at[pl.ds(i * part, part)],
            sems.at[i],
        )
        move.start()
        moves.append(move)
    feat = own_ref.shape[2] - 128
    half = cols_ref.shape[0]
    normed_rows(nv, nm, own_ref, vec_ref, cols_ref, x_ref)
    sub = lax.broadcasted_iota(jnp.int32, (16, 128), 0)
    for d in range(0, model, 128):
        m, t = d // feat, d % feat // 128
        rest = vec_ref[m, 0, t : t + 1, :] * vec_ref[m, 1, t : t + 1, :]
        block = jnp.zeros((16, 128), f32)
        for i in range(3):
            piece = rest.astype(bf16).astype(f32)
            block = jnp.where(sub == i, piece, block)
            rest = rest - piece
        x_ref[2 * half :, d : d + 128] = block.astype(bf16)
    pre = jnp.dot(x_ref[:, :first], staged_ref[...], preferred_element_type=f32)
    for i, move in enumerate(moves):
        move.wait()
        at = i * part
        pre += jnp.dot(
            x_ref[:, first + at : first + at + part],
            head_ref[at : at + part, :],
            preferred_element_type=f32,
        )
    pre_ref[...] = pre


def score_kernel(nv, nm, other_ref, vec_ref, ids_ref, staged_ref, head_ref, early_ref, early_cols_ref, slab_hbm, cols_ref, ops_hbm, x_ref, slab_ref, ops_ref, sems):
    voc = head_ref.shape[1]
    half = early_cols_ref.shape[0]
    group = 2 * half
    cols_ref[:half] = early_cols_ref[...]
    normed_rows(nv, nm, other_ref, vec_ref, cols_ref.at[half:], x_ref)
    first = staged_ref.shape[0]
    late = jnp.dot(x_ref[:, :first], staged_ref[...], preferred_element_type=f32)
    late += jnp.dot(x_ref[:, first:], head_ref[...], preferred_element_type=f32)
    pre_edit = jnp.concatenate([early_ref[:half], late[:half]], axis=0)
    pre_base = jnp.concatenate([early_ref[half:group], late[half:]], axis=0)
    toward = jnp.sum(early_ref[group:], axis=0, keepdims=True)
    th = jnp.tanh(pre_edit / softcap)
    z_edit = softcap * th
    z_base = softcap * jnp.tanh(pre_base / softcap)
    slope = 1.0 - th * th
    exp_edit = jnp.exp(z_edit)
    exp_base = jnp.exp(z_base)
    first_col = lax.axis_index(("vocab", "mp", "rep")) * voc
    column = lax.broadcasted_iota(jnp.int32, (group, voc), 1) + first_col
    hit = column == ids_ref[...]
    diff = z_base - z_edit
    pe = exp_edit * slope
    pb = exp_base * slope
    po = jnp.where(hit, slope, 0.0)

    high_e = pe.astype(bf16)
    high_b = pb.astype(bf16)
    ops_ref[:group] = high_e
    ops_ref[group : 2 * group] = high_b
    ops_ref[2 * group : 3 * group] = (pe - high_e.astype(f32)).astype(bf16)
    ops_ref[3 * group : 4 * group] = (pb - high_b.astype(f32)).astype(bf16)
    weight = cols_ref[:, 0:1] * cols_ref[:, 1:2]
    rest = jnp.sum(weight * po, axis=0, keepdims=True)
    sub = lax.broadcasted_iota(jnp.int32, (16, voc), 0)
    block = jnp.zeros((16, voc), f32)
    for i in range(3):
        piece = rest.astype(bf16).astype(f32)
        block = jnp.where(sub == i, piece, block)
        rest = rest - piece
    ops_ref[4 * group :] = block.astype(bf16)
    put_ops = pltpu.make_async_copy(ops_ref, ops_hbm, sems.at[1])
    put_ops.start()

    def lanes(a):
        part = a[:, :128]
        for c in range(128, voc, 128):
            part += a[:, c : c + 128]
        return part

    parts = [
        lanes(a)
        for a in (
            exp_edit,
            exp_base,
            exp_base * diff,
            jnp.where(hit, diff, 0.0),
            pe * pre_edit,
            pb * pre_edit,
            po * pre_edit,
            pe * toward,
            pb * toward,
            po * toward,
        )
    ]
    even = lax.axis_index("rep") == 0
    sub = lax.broadcasted_iota(jnp.int32, (8, 128), 0)
    table = jnp.zeros((8, 128), f32)
    for i in range(5):
        a, b = parts[i], parts[i + 5]
        straight = jnp.concatenate([a, b], axis=0)
        swapped = jnp.concatenate([a[half:], a[:half], b[half:], b[:half]], axis=0)
        row = jnp.sum(jnp.where(even, straight, swapped).T, axis=0, keepdims=True)
        table = jnp.where(sub == i, row, table)
    for p in range(slab_ref.shape[0]):
        slab_ref[p] = table
    put_slab = pltpu.make_async_copy(slab_ref, slab_hbm, sems.at[0])
    put_slab.start()

    put_slab.wait()
    put_ops.wait()


def outer_kernel(ops_hbm, head_hbm, outer_ref, ops_ref, head_ref, sems):
    both = outer_ref.shape[0] - 16
    part = outer_ref.shape[1] // (sems.shape[0] - 1)
    get = pltpu.make_async_copy(ops_hbm, ops_ref, sems.at[0])
    get.start()
    moves = []
    for i in range(outer_ref.shape[1] // part):
        span = pl.ds(i * part, part)
        source = head_hbm.at[span]
        moves.append(pltpu.make_async_copy(source, head_ref.at[span], sems.at[1 + i]))
    for move in moves:
        move.start()
    get.wait()
    for i, move in enumerate(moves):
        move.wait()
        c = i * part
        block = lax.dot_general(
            ops_ref[...],
            head_ref[c : c + part, :],
            (((1,), (1,)), ((), ())),
            preferred_element_type=f32,
        )
        outer_ref[:both, c : c + part] = block[:both] + block[both : 2 * both]
        outer_ref[both:, c : c + part] = block[2 * both :]


def close_kernel(nv, nm, theirs_ref, cols_ref, outer_ref, own_ref, all_ref, *refs):
    units = refs[:nm]
    slab_hbm, penalty_hbm, coeff_ref, pen_ref, pull_ref, vec_ref, slab_ref, second_ref, line_ref, sems = refs[nm:]
    rows = own_ref.shape[1]
    feat = own_ref.shape[2] - 128
    model = outer_ref.shape[1]
    group = 2 * nv * rows
    half = group // 2
    tiles = feat // 128
    v_i = lax.axis_index("vocab")
    m_i = lax.axis_index("mp")
    r_i = lax.axis_index("rep")

    table = theirs_ref[0]
    for p in range(1, theirs_ref.shape[0]):
        table += theirs_ref[p]
    table = jnp.concatenate([table, jnp.zeros((120, 128), f32)], axis=0).T
    first = table[:group]
    second = table[group:]
    swap_first = jnp.concatenate([first[half:], first[:half]], axis=0)
    swap_second = jnp.concatenate([second[half:], second[:half]], axis=0)
    first = jnp.where(r_i == 0, first, swap_first)
    second = jnp.where(r_i == 0, second, swap_second)
    se, sb, kl, gap, ae = [first[:, i : i + 1] for i in range(5)]
    ab, ao, te, tb, to = [second[:, i : i + 1] for i in range(5)]
    mix = cols_ref[:, 0:1]
    scale = cols_ref[:, 1:2]
    along = cols_ref[:, 2:3]
    inv_e = 2.0 / se
    inv_b = 1.0 / sb
    align = ae * inv_e - ab * inv_b - ao
    proj = te * inv_e - tb * inv_b - to
    penalty = kl * inv_b + gap + 2.0 * (jnp.log(se) - jnp.log(sb))
    shrink = scale * align / model
    coeff = scale * proj - shrink * (scale * along)
    weight = mix * scale
    pull = weight * shrink
    coeff_ref[...] = jnp.broadcast_to(coeff, (group, 128))
    pen_ref[...] = jnp.broadcast_to(penalty, (group, 128))
    mine = pen_ref[pl.ds(pl.multiple_of(v_i * rows, rows), rows), :]
    diagonal = lax.broadcasted_iota(jnp.int32, (rows, 128), 0) == lax.broadcasted_iota(
        jnp.int32, (rows, 128), 1
    )
    line_ref[...] = jnp.sum(jnp.where(diagonal, mine, 0.0), axis=0, keepdims=True)[:, :rows]
    put_pen = pltpu.make_async_copy(line_ref, penalty_hbm, sems.at[0])
    put_pen.start()

    pull_ref[...] = jnp.broadcast_to(pull, (group, 128))
    pulls = pull_ref[pl.ds(pl.multiple_of(v_i * rows, rows), rows), :]
    pull_ref[...] = jnp.broadcast_to(pull * mix, (group, 128))
    pulled = jnp.sum(pull_ref[pl.ds(pl.multiple_of(v_i * rows, rows), rows), :], axis=0, keepdims=True)
    for t in range(tiles):
        part = own_ref[v_i * nm + m_i, :, t * 128 : (t + 1) * 128].astype(f32) * pulls
        second_ref[t : t + 1, :] = (
            jnp.sum(part, axis=0, keepdims=True) + pulled * all_ref[m_i, 0, t : t + 1, :]
        )

    own = [
        coeff_ref[pl.ds(pl.multiple_of((k * nv + v_i) * rows, rows), rows), :] for k in range(2)
    ]
    for k in range(nm):
        m = lax.rem(m_i - k + nm, nm)
        for t in range(units[0].shape[1] // 128):
            c = t * 128
            row = units[k][:rows, c : c + 128].astype(f32) * own[0]
            row += units[k][rows:, c : c + 128].astype(f32) * own[1]
            vec_ref[m, pl.ds(tiles + t, 1), :] = jnp.sum(row, axis=0, keepdims=True)
    by_e = jnp.broadcast_to(weight * inv_e, (group, 128))
    by_b = jnp.broadcast_to(weight * inv_b, (group, 128))
    puts = []
    for m in range(nm):
        for t in range(tiles):
            d = m * feat + t * 128
            plus = outer_ref[:group, d : d + 128] * by_e
            less = outer_ref[group : 2 * group, d : d + 128] * by_b
            row = jnp.sum(plus - less, axis=0, keepdims=True)
            row -= jnp.sum(outer_ref[2 * group :, d : d + 128], axis=0, keepdims=True)
            row = row * all_ref[m, 1, t : t + 1, :] - jnp.where(
                m_i == m, second_ref[t : t + 1, :], 0.0
            )
            vec_ref[m, t : t + 1, :] = row
        slab_ref[m] = vec_ref[m].astype(bf16)
        for v in range(nv):
            put = pltpu.make_async_copy(
                slab_ref.at[m], slab_hbm.at[v * nm + m], sems.at[1 + v * nm + m]
            )
            put.start()
            puts.append(put)
    put_pen.wait()
    for put in puts:
        put.wait()


def sum_kernel(nm, back_ref, sums_ref):
    senders = back_ref.shape[0]
    units = (sums_ref.shape[0] - back_ref.shape[1]) // (nm - 1)
    tiles = back_ref.shape[1] - units
    wide = jnp.zeros((tiles, 128), f32)
    for m in range(nm):
        total = back_ref[m].astype(f32)
        for p in range(m + nm, senders, nm):
            total += back_ref[p].astype(f32)
        wide += total[:tiles]
        sums_ref[m * units : (m + 1) * units, :] = total[tiles:]
    sums_ref[nm * units :, :] = wide


def join_kernel(nm, own_ref, other_ref, in_ref, out_ref):
    units = in_ref.shape[0] // (2 * nm)
    even = lax.axis_index("rep") == 0
    for m in range(nm):
        own = own_ref[m * units : (m + 1) * units, :]
        other = other_ref[m * units : (m + 1) * units, :]
        at = 2 * m * units
        in_ref[at : at + units, :] = jnp.where(even, own, other)
        in_ref[at + units : at + 2 * units, :] = jnp.where(even, other, own)
    out_ref[...] = own_ref[nm * units :, :] + other_ref[nm * units :, :]


def in_hbm(value):
    return pltpu.with_memory_space_constraint(value, pltpu.HBM)


def call(kernel, out_shape, scratch=(), megabytes=6, **more):
    return pl.pallas_call(
        kernel,
        out_shape=out_shape,
        scratch_shapes=scratch,
        compiler_params=pltpu.CompilerParams(vmem_limit_bytes=megabytes << 20),
        **more,
    )


def fused(nv, nm, nr, resid_base, mlp_hidden, edit_in, edit_out, norm_gain, head, token_ids):
    rows, feat = resid_base.shape
    hidden = mlp_hidden.shape[1]
    model, voc = head.shape
    group = nv * nr * rows
    peers = nv * nm * nr
    quarter = hidden // (nm * nr)
    everyone = ("vocab", "mp", "rep")
    m_i = lax.axis_index("mp")
    r_i = lax.axis_index("rep")
    shape = jax.ShapeDtypeStruct

    tiles = feat // 128
    hbm = pl.BlockSpec(memory_space=pltpu.HBM)
    vmem = pl.BlockSpec(memory_space=pltpu.VMEM)
    out_tiles = edit_out.reshape(tiles, 128)
    gain_tiles = norm_gain.reshape(tiles, 128)

    packed, vectors, keep, give = call(
        functools.partial(send_kernel, nv * nm, nm),
        (
            pltpu.HBM((nv * nm, rows, feat + 128), bf16),
            shape((2, tiles, 128), f32),
        )
        + (shape((nm, rows, quarter), bf16),) * 2,
        [
            pltpu.VMEM((rows, feat), bf16),
            pltpu.VMEM((rows, hidden), bf16),
            pltpu.VMEM((1, hidden), f32),
            pltpu.VMEM((nv * nm, rows, feat), bf16),
            pltpu.VMEM((nv * nm, rows, 128), bf16),
            pltpu.SemaphoreType.DMA((7 + 2 * nm,)),
        ],
        in_specs=[hbm] * 5,
        out_specs=(hbm,) + (vmem,) * 3,
    )(
        *(
            in_hbm(a)
            for a in (resid_base, mlp_hidden, edit_in.reshape(1, hidden), out_tiles, gain_tiles)
        )
    )
    got = lax.all_to_all(packed, ("vocab", "mp"), 0, 0)
    other = lax.ppermute(got, "rep", [(0, 1), (1, 0)])
    took = lax.ppermute(give, "rep", [(0, 1), (1, 0)])
    units = [
        jnp.concatenate(
            [lax.dynamic_index_in_dim(a, (m_i + k) % nm, 0, keepdims=False) for a in (keep, took)]
        )
        for k in range(nm)
    ]
    vectors = from_peers(vectors, "mp", nm)
    first = model * 5 // 9
    staged = call(
        stage_kernel,
        pltpu.VMEM((first, voc), bf16),
        [pltpu.SemaphoreType.DMA((5,))],
        in_specs=[vmem, hbm],
        out_specs=vmem,
    )(took, in_hbm(head))
    vectors, units, staged = lax.optimization_barrier((vectors, units, staged))
    vectors = jnp.stack(in_order(vectors, m_i))
    half = group // 2
    unstaged, early, early_cols = call(
        functools.partial(early_kernel, nv, nm),
        (
            pltpu.VMEM((model - first, voc), bf16),
            shape((group + 16, voc), f32),
            shape((half, 128), f32),
        ),
        [pltpu.VMEM((group + 16, model), bf16), pltpu.SemaphoreType.DMA((4,))],
        8,
        in_specs=[vmem, vmem, vmem, hbm],
        out_specs=(vmem, vmem, vmem),
    )(got, vectors, staged, in_hbm(head))
    ids = token_ids.reshape(nv, nr, rows)
    ids = jnp.concatenate(
        [lax.dynamic_index_in_dim(ids, (r_i + k) % nr, 1, keepdims=False) for k in range(nr)]
    ).reshape(group, 1)

    slab, cols, ops = call(
        functools.partial(score_kernel, nv, nm),
        (
            pltpu.HBM((peers, 8, 128), f32),
            shape((group, 128), f32),
            pltpu.HBM((4 * group + 16, voc), bf16),
        ),
        [
            pltpu.VMEM((group, model), bf16),
            pltpu.VMEM((peers, 8, 128), f32),
            pltpu.VMEM((4 * group + 16, voc), bf16),
            pltpu.SemaphoreType.DMA((2,)),
        ],
        in_specs=[vmem] * 7,
        out_specs=(hbm, vmem, hbm),
    )(other, vectors, ids, staged, unstaged, early, early_cols)
    theirs = lax.all_to_all(slab, everyone, 0, 0)
    parts = 3
    outer = call(
        outer_kernel,
        shape((2 * group + 16, model), f32),
        [
            pltpu.VMEM((4 * group + 16, voc), bf16),
            pltpu.VMEM((model, voc), bf16),
            pltpu.SemaphoreType.DMA((1 + parts,)),
        ],
        12,
        in_specs=[hbm, hbm],
    )(in_hbm(ops), in_hbm(head))

    moves = [[(m, (m + k) % nm) for m in range(nm)] for k in range(nm)]
    units = [units[0]] + [lax.ppermute(units[k], "mp", moves[k]) for k in range(1, nm)]

    width = (feat + quarter) // 128
    slab, penalty = call(
        functools.partial(close_kernel, nv, nm),
        (pltpu.HBM((nv * nm, width, 128), bf16), pltpu.HBM((1, rows), f32)),
        [
            pltpu.VMEM((group, 128), f32),
            pltpu.VMEM((group, 128), f32),
            pltpu.VMEM((group, 128), f32),
            pltpu.VMEM((nm, width, 128), f32),
            pltpu.VMEM((nm, width, 128), bf16),
            pltpu.VMEM((tiles, 128), f32),
            pltpu.VMEM((1, rows), f32),
            pltpu.SemaphoreType.DMA((1 + nm * nv,)),
        ],
        in_specs=[vmem] * (5 + nm),
        out_specs=(hbm, hbm),
    )(theirs, cols, outer, got, vectors, *units)
    back = lax.all_to_all(slab, ("vocab", "mp"), 0, 0)
    sums = call(
        functools.partial(sum_kernel, nm), shape((nm * quarter // 128 + tiles, 128), f32)
    )(back)
    others = lax.ppermute(sums, "rep", [(0, 1), (1, 0)])
    grad_in, grad_out = call(
        functools.partial(join_kernel, nm),
        (shape((hidden // 128, 128), f32), shape((tiles, 128), f32)),
    )(sums, others)
    return (penalty.reshape(rows), grad_in.reshape(hidden), grad_out.reshape(feat))


def local(nv, nm, nr, resid_base, mlp_hidden, *rest):
    rows, feat = resid_base.shape
    quarter = mlp_hidden.shape[1] // (nm * nr)
    whole_tiles = rows == 8 and feat % 128 == 0 and quarter % 128 == 0
    small = nr == 2 and nm > 1 and nv % 2 == 0 and nv * nr * rows == 64
    step = fused if whole_tiles and small else plain
    return step(nv, nm, nr, resid_base, mlp_hidden, *rest)


def solution(mesh):
    in_specs = (
        P(("parts", "vocab", "rep"), "mp"),
        P(("parts", "vocab", "rep"), "mp"),
        P(("parts", "mp")),
        P(("parts", "mp")),
        P("mp"),
        P(None, ("vocab", "mp", "rep")),
        P("parts"),
    )
    out_specs = (P(("parts", "vocab", "rep")), P(("parts", "mp")), P(("parts", "mp")))
    step = functools.partial(local, mesh.shape["vocab"], mesh.shape["mp"], mesh.shape["rep"])
    return jax.shard_map(step, mesh=mesh, in_specs=in_specs, out_specs=out_specs, check_vma=False)
```

```python
import functools

import jax
import jax.numpy as jnp
from jax import lax
from jax.experimental import pallas as pl
from jax.experimental.pallas import tpu as pltpu
from jax.sharding import PartitionSpec as P

softcap = 30.0
epsilon = 1e-06
bf16 = jnp.bfloat16
f32 = jnp.float32


def split_bf16(value, pieces):
    out = []
    for _ in range(pieces):
        part = lax.reduce_precision(value, 8, 7)
        out.append(part.astype(bf16))
        value = value - part
    return out


def from_peers(value, axis, size):
    moves = [[(i, (i + k) % size) for i in range(size)] for k in range(size)]
    return [value] + [lax.ppermute(value, axis, moves[k]) for k in range(1, size)]


def to_peers(pick, axis, size, index):
    moves = [[(i, (i + k) % size) for i in range(size)] for k in range(size)]
    return [pick(index)] + [
        lax.ppermute(pick((index + k) % size), axis, moves[k]) for k in range(1, size)
    ]


def in_order(values, index):
    size = len(values)
    ordered = []
    for j in range(size):
        value = values[0]
        for k in range(1, size):
            value = jnp.where((index - j) % size == k, values[k], value)
        ordered.append(value)
    return ordered


def plain(nv, nm, nr, resid_base, mlp_hidden, edit_in, edit_out, norm_gain, head, token_ids):
    rows, feat = resid_base.shape
    hidden = mlp_hidden.shape[1]
    model, voc = head.shape
    group = nv * nr * rows
    peers = nv * nm * nr
    quarter = hidden // (nm * nr)
    everyone = ("vocab", "mp", "rep")

    v_i = lax.axis_index("vocab")
    m_i = lax.axis_index("mp")
    r_i = lax.axis_index("rep")

    vectors = from_peers(jnp.stack([edit_out, norm_gain]), "mp", nm)
    vectors = jnp.concatenate(in_order(vectors, m_i), axis=1)
    out_all = vectors[0]
    gain_all = vectors[1]

    units = mlp_hidden.reshape(rows, nm, nr, quarter)
    units = jnp.concatenate(
        [
            part
            for part in to_peers(
                lambda r: lax.dynamic_index_in_dim(units, r, 2, keepdims=False), "rep", nr, r_i
            )
        ]
    )
    units = to_peers(
        lambda m: lax.dynamic_index_in_dim(units, m, 1, keepdims=False), "mp", nm, m_i
    )

    hidden_f = mlp_hidden.astype(f32)
    mix_part = jnp.sum(hidden_f * edit_in[None, :], axis=1)
    mix_cols = jnp.stack(split_bf16(mix_part, 3), axis=1)
    packed = jnp.concatenate([resid_base, jnp.pad(mix_cols, ((0, 0), (0, 125)))], axis=1)
    packed = jnp.broadcast_to(packed[None], (nv * nm, rows, feat + 128))
    got = lax.all_to_all(packed, ("vocab", "mp"), 0, 0)
    got = jnp.concatenate(in_order(from_peers(got, "rep", nr), r_i)).reshape(nr * nv, nm, rows, feat + 128)

    base = jnp.concatenate([got[:, m, :, :feat].reshape(group, feat) for m in range(nm)], axis=1)
    base_f = base.astype(f32)
    mix = jnp.sum(got[:, :, :, feat : feat + 3].astype(f32), axis=(1, 3)).reshape(group)
    resid = base_f + mix[:, None] * out_all[None, :]
    edit_scale = lax.rsqrt(jnp.mean(resid * resid, axis=1) + epsilon)
    base_scale = lax.rsqrt(jnp.mean(base_f * base_f, axis=1) + epsilon)
    along = jnp.sum(resid * out_all[None, :], axis=1)
    x_edit = (resid * edit_scale[:, None] * gain_all[None, :]).astype(bf16)
    x_base = (base_f * base_scale[:, None] * gain_all[None, :]).astype(bf16)
    direction = jnp.stack(split_bf16(out_all * gain_all, 3) + [jnp.zeros((model,), bf16)] * 5)
    pre = jnp.dot(
        jnp.concatenate([x_edit, x_base, direction]), head, preferred_element_type=f32
    )
    pre_edit = pre[:group]
    pre_base = pre[group : 2 * group]
    toward = jnp.sum(pre[2 * group :], axis=0)
    z_edit = softcap * jnp.tanh(pre_edit / softcap)
    z_base = softcap * jnp.tanh(pre_base / softcap)
    slope = 1.0 - (z_edit / softcap) ** 2
    exp_edit = jnp.exp(z_edit)
    exp_base = jnp.exp(z_base)
    ids = token_ids.reshape(nv, nr, rows).transpose(1, 0, 2).reshape(group)
    first_col = lax.axis_index(everyone) * voc
    onehot = (ids[:, None] == (first_col + jnp.arange(voc, dtype=jnp.int32))[None, :]).astype(f32)
    diff = z_base - z_edit
    pe = exp_edit * slope
    pb = exp_base * slope
    po = onehot * slope
    sums = jnp.stack(
        [
            jnp.sum(a, axis=1)
            for a in (
                exp_edit,
                exp_base,
                exp_base * diff,
                onehot * diff,
                pe * pre_edit,
                pb * pre_edit,
                po * pre_edit,
                pe * toward[None, :],
                pb * toward[None, :],
                po * toward[None, :],
            )
        ]
    )
    weight = mix * edit_scale
    wo = jnp.sum(weight[:, None] * po, axis=0)
    high_e, low_e = split_bf16(pe, 2)
    high_b, low_b = split_bf16(pb, 2)
    tail = jnp.stack(split_bf16(wo, 3) + [jnp.zeros((voc,), bf16)] * 5)
    outer = lax.dot_general(
        jnp.concatenate([high_e, high_b, low_e, low_b, tail]),
        head,
        (((1,), (1,)), ((), ())),
        preferred_element_type=f32,
    )
    rows_e = outer[:group] + outer[2 * group : 3 * group]
    rows_b = outer[group : 2 * group] + outer[3 * group : 4 * group]
    row_o = jnp.sum(outer[4 * group :], axis=0)
    flat = 10 * group
    padded = -(-flat // 1024) * 1024
    mine = jnp.pad(sums.reshape(flat), (0, padded - flat)).reshape(padded // 128, 128)
    theirs = lax.all_to_all(
        jnp.broadcast_to(mine[None], (peers, padded // 128, 128)), everyone, 0, 0
    )
    sums = jnp.sum(theirs, axis=0).reshape(padded)[:flat].reshape(10, group)
    se, sb, kl, gap, ae, ab, ao, te, tb, to = [sums[i] for i in range(10)]
    inv_e = 2.0 / se
    inv_b = 1.0 / sb
    align = ae * inv_e - ab * inv_b - ao
    proj = te * inv_e - tb * inv_b - to
    penalty = kl * inv_b + gap + 2.0 * (jnp.log(se) - jnp.log(sb))
    shrink = edit_scale * align / model
    coeff = edit_scale * proj - shrink * (edit_scale * along)
    weighted = jnp.sum((weight * inv_e)[:, None] * rows_e, axis=0) - jnp.sum((weight * inv_b)[:, None] * rows_b, axis=0) - row_o
    w_hi, w_lo = split_bf16(weighted, 2)
    mine = lax.dynamic_index_in_dim(coeff.reshape(nr, nv, rows), v_i, 1, keepdims=False)
    own = jnp.concatenate([lax.dynamic_index_in_dim(mine, (r_i - k) % nr, 0, keepdims=False) for k in range(nr)])
    part_in = [jnp.sum(u.astype(f32) * own[:, None], axis=0) for u in units]
    part_in = jnp.stack(in_order(part_in, m_i)).astype(bf16)
    slab = jnp.concatenate([w_hi.reshape(nm, feat), w_lo.reshape(nm, feat), part_in], axis=1)
    width = 2 * feat + quarter
    if width % 128 == 0:
        slab = slab.reshape(nm, width // 128, 128)
    slab = jnp.broadcast_to(slab[None, :, None], (nv, nm, nr) + slab.shape[1:])
    back = lax.all_to_all(slab.reshape((peers,) + slab.shape[3:]), everyone, 0, 0)
    back = back.reshape(nv, nm * nr, width).astype(f32)
    grad_in = jnp.sum(back[:, :, 2 * feat :], axis=0).reshape(hidden)
    weighted_own = jnp.sum(back[:, :, :feat] + back[:, :, feat : 2 * feat], axis=(0, 1))
    pull = mix * shrink * edit_scale
    base_own = lax.dynamic_slice_in_dim(base, m_i * feat, feat, 1).astype(f32)
    second = jnp.sum(pull[:, None] * base_own, axis=0) + jnp.sum(pull * mix) * edit_out
    grad_out = norm_gain * weighted_own - second
    penalty = lax.dynamic_slice(penalty.reshape(nr, nv, rows), (r_i, v_i, 0), (1, 1, rows))
    return (penalty.reshape(rows), grad_in, grad_out)


def send_kernel(copies, pieces, base_hbm, hidden_hbm, in_hbm, out_hbm, gain_hbm, packed_hbm, vec_ref, *refs):
    unit_refs = refs[:2]
    base_ref, hidden_ref, in_ref, packed_ref, mix_ref, sems = refs[2:]
    rows, hidden = hidden_ref.shape
    feat = base_ref.shape[1]
    quarter = hidden // (2 * pieces)
    get_hidden = pltpu.make_async_copy(hidden_hbm, hidden_ref, sems.at[0])
    get_in = pltpu.make_async_copy(in_hbm, in_ref, sems.at[1])
    get_base = pltpu.make_async_copy(base_hbm, base_ref, sems.at[2])
    later = [
        pltpu.make_async_copy(out_hbm, vec_ref.at[0], sems.at[3]),
        pltpu.make_async_copy(gain_hbm, vec_ref.at[1], sems.at[4]),
    ]
    r_i = lax.axis_index("rep")
    for i in range(pieces):
        for j in range(2):
            start = pl.multiple_of((2 * i + lax.rem(r_i + j, 2)) * quarter, 128)
            later.append(
                pltpu.make_async_copy(
                    hidden_hbm.at[:, pl.ds(start, quarter)],
                    unit_refs[j].at[i],
                    sems.at[7 + 2 * i + j],
                )
            )
    get_base.start()
    get_hidden.start()
    get_in.start()
    for move in later:
        move.start()
    get_base.wait()
    for i in range(copies):
        packed_ref[i] = base_ref[...]
    put_base = pltpu.make_async_copy(packed_ref, packed_hbm.at[:, :, pl.ds(0, feat)], sems.at[5])
    put_base.start()
    get_hidden.wait()
    get_in.wait()
    totals = [jnp.zeros((rows, 128), f32)] * 8
    for i, c in enumerate(range(0, hidden, 128)):
        product = hidden_ref[:, c : c + 128].astype(f32) * in_ref[:, c : c + 128]
        totals[i % 8] = totals[i % 8] + product
    while len(totals) > 1:
        totals = [a + b for a, b in zip(totals[::2], totals[1::2])]
    mix = jnp.sum(totals[0], axis=1, keepdims=True)
    lane = lax.broadcasted_iota(jnp.int32, (rows, 128), 1)
    cols = jnp.zeros((rows, 128), f32)
    for i in range(3):
        piece = mix.astype(bf16).astype(f32)
        cols = jnp.where(lane == i, piece, cols)
        mix = mix - piece
    cols = cols.astype(bf16)
    for i in range(copies):
        mix_ref[i] = cols
    put_mix = pltpu.make_async_copy(mix_ref, packed_hbm.at[:, :, pl.ds(feat, 128)], sems.at[6])
    put_mix.start()
    for move in later:
        move.wait()
    put_base.wait()
    put_mix.wait()


def normed_rows(nv, nm, got_ref, vec_ref, cols_ref, x_ref):
    rows = got_ref.shape[1]
    feat = got_ref.shape[2] - 128
    model = nm * feat
    half = nv * rows
    pair = 2 * rows
    lane = lax.broadcasted_iota(jnp.int32, (pair, 128), 1)
    for v in range(0, nv, 2):
        at = v * rows

        def tile(m, c):
            first = got_ref[v * nm + m, :, c : c + 128].astype(f32)
            second = got_ref[(v + 1) * nm + m, :, c : c + 128].astype(f32)
            return jnp.concatenate([first, second], axis=0)

        mixed = tile(0, feat)
        for m in range(1, nm):
            mixed += tile(m, feat)
        mix = jnp.sum(mixed, axis=1, keepdims=True)
        mix_b = jnp.broadcast_to(mix, (pair, 128))
        sq_b = jnp.zeros((pair, 128), f32)
        sq_e = jnp.zeros((pair, 128), f32)
        dot_o = jnp.zeros((pair, 128), f32)
        for m in range(nm):
            for c in range(0, feat, 128):
                out = vec_ref[m, 0, c // 128 : c // 128 + 1, :]
                b = tile(m, c)
                e = b + mix_b * out
                sq_b += b * b
                sq_e += e * e
                dot_o += e * out
        scale_e = lax.rsqrt(jnp.sum(sq_e, axis=1, keepdims=True) / model + epsilon)
        scale_b = lax.rsqrt(jnp.sum(sq_b, axis=1, keepdims=True) / model + epsilon)
        along = jnp.sum(dot_o, axis=1, keepdims=True)
        cols_ref[at : at + pair, :] = jnp.where(
            lane == 0, mix, jnp.where(lane == 1, scale_e, jnp.where(lane == 2, along, 0.0))
        )
        scale_e = jnp.broadcast_to(scale_e, (pair, 128))
        scale_b = jnp.broadcast_to(scale_b, (pair, 128))
        for m in range(nm):
            for c in range(0, feat, 128):
                d = m * feat + c
                t = c // 128
                out = vec_ref[m, 0, t : t + 1, :]
                gain = vec_ref[m, 1, t : t + 1, :]
                b = tile(m, c)
                e = b + mix_b * out
                x_ref[at : at + pair, d : d + 128] = (e * scale_e * gain).astype(bf16)
                x_ref[half + at : half + at + pair, d : d + 128] = (b * scale_b * gain).astype(bf16)


def stage_kernel(after_ref, head_hbm, head_ref, sems):
    part = head_ref.shape[0] // sems.shape[0]
    moves = []
    for i in range(sems.shape[0]):
        span = pl.ds(i * part, part)
        moves.append(pltpu.make_async_copy(head_hbm.at[span], head_ref.at[span], sems.at[i]))
        moves[i].start()
    for move in moves:
        move.wait()


def early_kernel(nv, nm, own_ref, vec_ref, staged_ref, head_hbm, head_ref, pre_ref, cols_ref, x_ref, sems):
    model = head_hbm.shape[0]
    first = staged_ref.shape[0]
    part = (model - first) // sems.shape[0]
    moves = []
    for i in range(sems.shape[0]):
        move = pltpu.make_async_copy(
            head_hbm.at[pl.ds(first + i * part, part)],
            head_ref.at[pl.ds(i * part, part)],
            sems.at[i],
        )
        move.start()
        moves.append(move)
    feat = own_ref.shape[2] - 128
    half = cols_ref.shape[0]
    normed_rows(nv, nm, own_ref, vec_ref, cols_ref, x_ref)
    sub = lax.broadcasted_iota(jnp.int32, (16, 128), 0)
    for d in range(0, model, 128):
        m, t = d // feat, d % feat // 128
        rest = vec_ref[m, 0, t : t + 1, :] * vec_ref[m, 1, t : t + 1, :]
        block = jnp.zeros((16, 128), f32)
        for i in range(3):
            piece = rest.astype(bf16).astype(f32)
            block = jnp.where(sub == i, piece, block)
            rest = rest - piece
        x_ref[2 * half :, d : d + 128] = block.astype(bf16)
    pre = jnp.dot(x_ref[:, :first], staged_ref[...], preferred_element_type=f32)
    for i, move in enumerate(moves):
        move.wait()
        at = i * part
        pre += jnp.dot(
            x_ref[:, first + at : first + at + part],
            head_ref[at : at + part, :],
            preferred_element_type=f32,
        )
    pre_ref[...] = pre


def score_kernel(nv, nm, other_ref, vec_ref, ids_ref, staged_ref, head_ref, early_ref, early_cols_ref, slab_hbm, cols_ref, ops_hbm, x_ref, slab_ref, ops_ref, sems):
    voc = head_ref.shape[1]
    half = early_cols_ref.shape[0]
    group = 2 * half
    cols_ref[:half] = early_cols_ref[...]
    normed_rows(nv, nm, other_ref, vec_ref, cols_ref.at[half:], x_ref)
    first = staged_ref.shape[0]
    late = jnp.dot(x_ref[:, :first], staged_ref[...], preferred_element_type=f32)
    late += jnp.dot(x_ref[:, first:], head_ref[...], preferred_element_type=f32)
    pre_edit = jnp.concatenate([early_ref[:half], late[:half]], axis=0)
    pre_base = jnp.concatenate([early_ref[half:group], late[half:]], axis=0)
    toward = jnp.sum(early_ref[group:], axis=0, keepdims=True)
    th = jnp.tanh(pre_edit / softcap)
    z_edit = softcap * th
    z_base = softcap * jnp.tanh(pre_base / softcap)
    slope = 1.0 - th * th
    exp_edit = jnp.exp(z_edit)
    exp_base = jnp.exp(z_base)
    first_col = lax.axis_index(("vocab", "mp", "rep")) * voc
    column = lax.broadcasted_iota(jnp.int32, (group, voc), 1) + first_col
    hit = column == ids_ref[...]
    diff = z_base - z_edit
    pe = exp_edit * slope
    pb = exp_base * slope
    po = jnp.where(hit, slope, 0.0)

    high_e = pe.astype(bf16)
    high_b = pb.astype(bf16)
    ops_ref[:group] = high_e
    ops_ref[group : 2 * group] = high_b
    ops_ref[2 * group : 3 * group] = (pe - high_e.astype(f32)).astype(bf16)
    ops_ref[3 * group : 4 * group] = (pb - high_b.astype(f32)).astype(bf16)
    weight = cols_ref[:, 0:1] * cols_ref[:, 1:2]
    rest = jnp.sum(weight * po, axis=0, keepdims=True)
    sub = lax.broadcasted_iota(jnp.int32, (16, voc), 0)
    block = jnp.zeros((16, voc), f32)
    for i in range(3):
        piece = rest.astype(bf16).astype(f32)
        block = jnp.where(sub == i, piece, block)
        rest = rest - piece
    ops_ref[4 * group :] = block.astype(bf16)
    put_ops = pltpu.make_async_copy(ops_ref, ops_hbm, sems.at[1])
    put_ops.start()

    def total(a):
        return jnp.sum(a, axis=1, keepdims=True)

    sums = [
        total(exp_edit),
        total(exp_base),
        total(exp_base * diff),
        total(jnp.where(hit, diff, 0.0)),
        total(pe * pre_edit),
        total(pb * pre_edit),
        total(po * pre_edit),
        total(pe * toward),
        total(pb * toward),
        total(po * toward),
    ]
    lane = lax.broadcasted_iota(jnp.int32, (group, 128), 1)
    first = jnp.zeros((group, 128), f32)
    second = jnp.zeros((group, 128), f32)
    for i in range(8):
        first = jnp.where(lane == i, sums[i], first)
    for i in range(8, 10):
        second = jnp.where(lane == i - 8, sums[i], second)
    straight = jnp.concatenate([first, second], axis=0)
    swapped = jnp.concatenate([first[half:], first[:half], second[half:], second[:half]], axis=0)
    table = jnp.where(lax.axis_index("rep") == 0, straight, swapped)
    table = table.T[:8]
    slab_ref[...] = table
    puts = []
    for p in range(slab_hbm.shape[0]):
        puts.append(pltpu.make_async_copy(slab_ref, slab_hbm.at[p], sems.at[2 + p]))
        puts[p].start()
    for put in puts:
        put.wait()
    put_ops.wait()


def outer_kernel(ops_hbm, head_hbm, outer_ref, ops_ref, head_ref, sems):
    both = outer_ref.shape[0] - 16
    part = outer_ref.shape[1] // (sems.shape[0] - 1)
    get = pltpu.make_async_copy(ops_hbm, ops_ref, sems.at[0])
    get.start()
    moves = []
    for i in range(outer_ref.shape[1] // part):
        span = pl.ds(i * part, part)
        source = head_hbm.at[span]
        moves.append(pltpu.make_async_copy(source, head_ref.at[span], sems.at[1 + i]))
    for move in moves:
        move.start()
    get.wait()
    for i, move in enumerate(moves):
        move.wait()
        c = i * part
        block = lax.dot_general(
            ops_ref[...],
            head_ref[c : c + part, :],
            (((1,), (1,)), ((), ())),
            preferred_element_type=f32,
        )
        outer_ref[:both, c : c + part] = block[:both] + block[both : 2 * both]
        outer_ref[both:, c : c + part] = block[2 * both :]


def close_kernel(nv, nm, theirs_ref, cols_ref, outer_ref, own_ref, all_ref, *refs):
    units = refs[:nm]
    slab_hbm, penalty_hbm, coeff_ref, pen_ref, pull_ref, vec_ref, slab_ref, second_ref, line_ref, sems = refs[nm:]
    rows = own_ref.shape[1]
    feat = own_ref.shape[2] - 128
    model = outer_ref.shape[1]
    group = 2 * nv * rows
    half = group // 2
    tiles = feat // 128
    v_i = lax.axis_index("vocab")
    m_i = lax.axis_index("mp")
    r_i = lax.axis_index("rep")

    table = theirs_ref[0]
    for p in range(1, theirs_ref.shape[0]):
        table += theirs_ref[p]
    table = jnp.concatenate([table, jnp.zeros((120, 128), f32)], axis=0).T
    first = table[:group]
    second = table[group:]
    swap_first = jnp.concatenate([first[half:], first[:half]], axis=0)
    swap_second = jnp.concatenate([second[half:], second[:half]], axis=0)
    first = jnp.where(r_i == 0, first, swap_first)
    second = jnp.where(r_i == 0, second, swap_second)
    se, sb, kl, gap, ae, ab, ao, te = [first[:, i : i + 1] for i in range(8)]
    tb, to = second[:, 0:1], second[:, 1:2]
    mix = cols_ref[:, 0:1]
    scale = cols_ref[:, 1:2]
    along = cols_ref[:, 2:3]
    inv_e = 2.0 / se
    inv_b = 1.0 / sb
    align = ae * inv_e - ab * inv_b - ao
    proj = te * inv_e - tb * inv_b - to
    penalty = kl * inv_b + gap + 2.0 * (jnp.log(se) - jnp.log(sb))
    shrink = scale * align / model
    coeff = scale * proj - shrink * (scale * along)
    weight = mix * scale
    pull = weight * shrink
    coeff_ref[...] = jnp.broadcast_to(coeff, (group, 128))
    pen_ref[...] = jnp.broadcast_to(penalty, (group, 128))
    mine = pen_ref[pl.ds(pl.multiple_of(v_i * rows, rows), rows), :]
    diagonal = lax.broadcasted_iota(jnp.int32, (rows, 128), 0) == lax.broadcasted_iota(
        jnp.int32, (rows, 128), 1
    )
    line_ref[...] = jnp.sum(jnp.where(diagonal, mine, 0.0), axis=0, keepdims=True)[:, :rows]
    put_pen = pltpu.make_async_copy(line_ref, penalty_hbm, sems.at[0])
    put_pen.start()

    pull_ref[...] = jnp.broadcast_to(pull, (group, 128))
    pulls = pull_ref[pl.ds(pl.multiple_of(v_i * rows, rows), rows), :]
    pull_ref[...] = jnp.broadcast_to(pull * mix, (group, 128))
    pulled = jnp.sum(pull_ref[pl.ds(pl.multiple_of(v_i * rows, rows), rows), :], axis=0, keepdims=True)
    for t in range(tiles):
        part = own_ref[v_i * nm + m_i, :, t * 128 : (t + 1) * 128].astype(f32) * pulls
        second_ref[t : t + 1, :] = (
            jnp.sum(part, axis=0, keepdims=True) + pulled * all_ref[m_i, 0, t : t + 1, :]
        )

    own = [
        coeff_ref[pl.ds(pl.multiple_of((k * nv + v_i) * rows, rows), rows), :] for k in range(2)
    ]
    for k in range(nm):
        m = lax.rem(m_i - k + nm, nm)
        for t in range(units[0].shape[1] // 128):
            c = t * 128
            row = units[k][:rows, c : c + 128].astype(f32) * own[0]
            row += units[k][rows:, c : c + 128].astype(f32) * own[1]
            vec_ref[m, pl.ds(tiles + t, 1), :] = jnp.sum(row, axis=0, keepdims=True)
    by_e = jnp.broadcast_to(weight * inv_e, (group, 128))
    by_b = jnp.broadcast_to(weight * inv_b, (group, 128))
    puts = []
    for m in range(nm):
        for t in range(tiles):
            d = m * feat + t * 128
            plus = outer_ref[:group, d : d + 128] * by_e
            less = outer_ref[group : 2 * group, d : d + 128] * by_b
            row = jnp.sum(plus - less, axis=0, keepdims=True)
            row -= jnp.sum(outer_ref[2 * group :, d : d + 128], axis=0, keepdims=True)
            row = row * all_ref[m, 1, t : t + 1, :] - jnp.where(
                m_i == m, second_ref[t : t + 1, :], 0.0
            )
            vec_ref[m, t : t + 1, :] = row
        slab_ref[m] = vec_ref[m].astype(bf16)
        for v in range(nv):
            put = pltpu.make_async_copy(
                slab_ref.at[m], slab_hbm.at[v * nm + m], sems.at[1 + v * nm + m]
            )
            put.start()
            puts.append(put)
    put_pen.wait()
    for put in puts:
        put.wait()


def sum_kernel(nm, back_ref, sums_ref):
    senders = back_ref.shape[0]
    units = (sums_ref.shape[0] - back_ref.shape[1]) // (nm - 1)
    tiles = back_ref.shape[1] - units
    wide = jnp.zeros((tiles, 128), f32)
    for m in range(nm):
        total = back_ref[m].astype(f32)
        for p in range(m + nm, senders, nm):
            total += back_ref[p].astype(f32)
        wide += total[:tiles]
        sums_ref[m * units : (m + 1) * units, :] = total[tiles:]
    sums_ref[nm * units :, :] = wide


def join_kernel(nm, own_ref, other_ref, in_ref, out_ref):
    units = in_ref.shape[0] // (2 * nm)
    even = lax.axis_index("rep") == 0
    for m in range(nm):
        own = own_ref[m * units : (m + 1) * units, :]
        other = other_ref[m * units : (m + 1) * units, :]
        at = 2 * m * units
        in_ref[at : at + units, :] = jnp.where(even, own, other)
        in_ref[at + units : at + 2 * units, :] = jnp.where(even, other, own)
    out_ref[...] = own_ref[nm * units :, :] + other_ref[nm * units :, :]


def in_hbm(value):
    return pltpu.with_memory_space_constraint(value, pltpu.HBM)


def call(kernel, out_shape, scratch=(), megabytes=6, **more):
    return pl.pallas_call(
        kernel,
        out_shape=out_shape,
        scratch_shapes=scratch,
        compiler_params=pltpu.CompilerParams(vmem_limit_bytes=megabytes << 20),
        **more,
    )


def fused(nv, nm, nr, resid_base, mlp_hidden, edit_in, edit_out, norm_gain, head, token_ids):
    rows, feat = resid_base.shape
    hidden = mlp_hidden.shape[1]
    model, voc = head.shape
    group = nv * nr * rows
    peers = nv * nm * nr
    quarter = hidden // (nm * nr)
    everyone = ("vocab", "mp", "rep")
    m_i = lax.axis_index("mp")
    r_i = lax.axis_index("rep")
    shape = jax.ShapeDtypeStruct

    tiles = feat // 128
    hbm = pl.BlockSpec(memory_space=pltpu.HBM)
    vmem = pl.BlockSpec(memory_space=pltpu.VMEM)
    out_tiles = edit_out.reshape(tiles, 128)
    gain_tiles = norm_gain.reshape(tiles, 128)

    packed, vectors, keep, give = call(
        functools.partial(send_kernel, nv * nm, nm),
        (
            pltpu.HBM((nv * nm, rows, feat + 128), bf16),
            shape((2, tiles, 128), f32),
        )
        + (shape((nm, rows, quarter), bf16),) * 2,
        [
            pltpu.VMEM((rows, feat), bf16),
            pltpu.VMEM((rows, hidden), bf16),
            pltpu.VMEM((1, hidden), f32),
            pltpu.VMEM((nv * nm, rows, feat), bf16),
            pltpu.VMEM((nv * nm, rows, 128), bf16),
            pltpu.SemaphoreType.DMA((7 + 2 * nm,)),
        ],
        in_specs=[hbm] * 5,
        out_specs=(hbm,) + (vmem,) * 3,
    )(
        *(
            in_hbm(a)
            for a in (resid_base, mlp_hidden, edit_in.reshape(1, hidden), out_tiles, gain_tiles)
        )
    )
    got = lax.all_to_all(packed, ("vocab", "mp"), 0, 0)
    other = lax.ppermute(got, "rep", [(0, 1), (1, 0)])
    took = lax.ppermute(give, "rep", [(0, 1), (1, 0)])
    units = [
        jnp.concatenate(
            [lax.dynamic_index_in_dim(a, (m_i + k) % nm, 0, keepdims=False) for a in (keep, took)]
        )
        for k in range(nm)
    ]
    vectors = from_peers(vectors, "mp", nm)
    first = model * 5 // 9
    staged = call(
        stage_kernel,
        pltpu.VMEM((first, voc), bf16),
        [pltpu.SemaphoreType.DMA((5,))],
        in_specs=[vmem, hbm],
        out_specs=vmem,
    )(took, in_hbm(head))
    vectors, units, staged = lax.optimization_barrier((vectors, units, staged))
    vectors = jnp.stack(in_order(vectors, m_i))
    half = group // 2
    unstaged, early, early_cols = call(
        functools.partial(early_kernel, nv, nm),
        (
            pltpu.VMEM((model - first, voc), bf16),
            shape((group + 16, voc), f32),
            shape((half, 128), f32),
        ),
        [pltpu.VMEM((group + 16, model), bf16), pltpu.SemaphoreType.DMA((4,))],
        8,
        in_specs=[vmem, vmem, vmem, hbm],
        out_specs=(vmem, vmem, vmem),
    )(got, vectors, staged, in_hbm(head))
    ids = token_ids.reshape(nv, nr, rows)
    ids = jnp.concatenate(
        [lax.dynamic_index_in_dim(ids, (r_i + k) % nr, 1, keepdims=False) for k in range(nr)]
    ).reshape(group, 1)

    slab, cols, ops = call(
        functools.partial(score_kernel, nv, nm),
        (
            pltpu.HBM((peers, 8, 128), f32),
            shape((group, 128), f32),
            pltpu.HBM((4 * group + 16, voc), bf16),
        ),
        [
            pltpu.VMEM((group, model), bf16),
            pltpu.VMEM((8, 128), f32),
            pltpu.VMEM((4 * group + 16, voc), bf16),
            pltpu.SemaphoreType.DMA((2 + peers,)),
        ],
        in_specs=[vmem] * 7,
        out_specs=(hbm, vmem, hbm),
    )(other, vectors, ids, staged, unstaged, early, early_cols)
    theirs = lax.all_to_all(slab, everyone, 0, 0)
    parts = 3
    outer = call(
        outer_kernel,
        shape((2 * group + 16, model), f32),
        [
            pltpu.VMEM((4 * group + 16, voc), bf16),
            pltpu.VMEM((model, voc), bf16),
            pltpu.SemaphoreType.DMA((1 + parts,)),
        ],
        12,
        in_specs=[hbm, hbm],
    )(in_hbm(ops), in_hbm(head))

    moves = [[(m, (m + k) % nm) for m in range(nm)] for k in range(nm)]
    units = [units[0]] + [lax.ppermute(units[k], "mp", moves[k]) for k in range(1, nm)]

    width = (feat + quarter) // 128
    slab, penalty = call(
        functools.partial(close_kernel, nv, nm),
        (pltpu.HBM((nv * nm, width, 128), bf16), pltpu.HBM((1, rows), f32)),
        [
            pltpu.VMEM((group, 128), f32),
            pltpu.VMEM((group, 128), f32),
            pltpu.VMEM((group, 128), f32),
            pltpu.VMEM((nm, width, 128), f32),
            pltpu.VMEM((nm, width, 128), bf16),
            pltpu.VMEM((tiles, 128), f32),
            pltpu.VMEM((1, rows), f32),
            pltpu.SemaphoreType.DMA((1 + nm * nv,)),
        ],
        in_specs=[vmem] * (5 + nm),
        out_specs=(hbm, hbm),
    )(theirs, cols, outer, got, vectors, *units)
    back = lax.all_to_all(slab, ("vocab", "mp"), 0, 0)
    sums = call(
        functools.partial(sum_kernel, nm), shape((nm * quarter // 128 + tiles, 128), f32)
    )(back)
    others = lax.ppermute(sums, "rep", [(0, 1), (1, 0)])
    grad_in, grad_out = call(
        functools.partial(join_kernel, nm),
        (shape((hidden // 128, 128), f32), shape((tiles, 128), f32)),
    )(sums, others)
    return (penalty.reshape(rows), grad_in.reshape(hidden), grad_out.reshape(feat))


def local(nv, nm, nr, resid_base, mlp_hidden, *rest):
    rows, feat = resid_base.shape
    quarter = mlp_hidden.shape[1] // (nm * nr)
    whole_tiles = rows == 8 and feat % 128 == 0 and quarter % 128 == 0
    small = nr == 2 and nm > 1 and nv % 2 == 0 and nv * nr * rows == 64
    step = fused if whole_tiles and small else plain
    return step(nv, nm, nr, resid_base, mlp_hidden, *rest)


def solution(mesh):
    in_specs = (
        P(("parts", "vocab", "rep"), "mp"),
        P(("parts", "vocab", "rep"), "mp"),
        P(("parts", "mp")),
        P(("parts", "mp")),
        P("mp"),
        P(None, ("vocab", "mp", "rep")),
        P("parts"),
    )
    out_specs = (P(("parts", "vocab", "rep")), P(("parts", "mp")), P(("parts", "mp")))
    step = functools.partial(local, mesh.shape["vocab"], mesh.shape["mp"], mesh.shape["rep"])
    return jax.shard_map(step, mesh=mesh, in_specs=in_specs, out_specs=out_specs, check_vma=False)
```
